32 devices in a mesh: seq: 2 (over x), row: 16 (over z, y, core).
Axes of the slice: x: 2, y: 2, z: 4, core: 2. Of those that a mesh axis runs over, the one named last changes fastest.
Arguments:
- qm: float32 [2, 16, 7, 256, 256], P('seq', 'row'), parts along dimension 0, may hold values from 0.005 to 0.05
- qm1: float32 [2, 16, 7, 256, 256], P('seq', 'row'), parts along dimension 0, may hold values from 0.005 to 0.05
- qb: float32 [2, 16, 7, 256, 256], P('seq', 'row'), parts along dimension 0, may hold values from 0.05 to 2
- codes: int32 [2, 16, 256], P('seq', 'row'), parts along dimension 0, may hold values from 0 to 3
- energy_index: int32 [2, 16, 256, 256], P('seq', 'row'), parts along dimension 0, may hold values from 0 to 63
- turner: float32 [64], replicated, may hold values from -1 to 1.5
Outputs:
- qb_new: float32 [2, 16, 256, 256], P('seq', 'row'), parts along dimension 0
- qm1_new: float32 [2, 16, 256, 256], P('seq', 'row'), parts along dimension 0
- qm_new: float32 [2, 16, 256, 256], P('seq', 'row'), parts along dimension 0
The draws below stay inside these ranges and needn't reach their ends.
There are 2 independent parts, one for each index of `seq`. The reference program is written for one: setup_inputs(seed, part) draws one part's arguments, and reference() takes and returns one part's arrays. A program takes and returns all parts, laid end to end along the dimension named above; an argument that names none is the same for every part. Nothing has to cross between parts.
All inputs are finite; a program needn't handle non-finite values.
Results may differ from the reference program's by a relative error of at most 0.0003.
Values sent between devices are 32-bit elements; how exact they have to be, the bound alone decides.
A program may use at most 64 MiB of HBM per device.

```python
import math
import jax
import jax.numpy as jnp
import numpy as np
from jax import lax

B = 256
DIST = 8
CYCLES = 1
TABLE = 64
DM = 7
BLOCK_ROWS = 16


def plant(entries, own_key, smallest, top_value):
    index_at = [jax.random.randint(jax.random.fold_in(own_key, axis), (), 0, length) for axis, length in enumerate(entries.shape)]
    main_axis = entries.shape.index(max(entries.shape))
    beside = index_at[:main_axis] + [(index_at[main_axis] + 1) % entries.shape[main_axis]] + index_at[main_axis + 1:]
    return entries.at[tuple(index_at)].set(smallest).at[tuple(beside)].set(top_value)


def levels(key, extent, cuts, smallest, largest):
    factor_of, own = 1.0, jax.random.fold_in(key, 6)
    for axis_at, blocks in cuts:
        steps = jnp.exp(jax.random.uniform(jax.random.fold_in(own, axis_at), (blocks,), jnp.float32, smallest / len(cuts), largest / len(cuts)))
        factor_of = factor_of * jnp.repeat(steps, extent[axis_at] // blocks).reshape([-1 if axis == axis_at else 1 for axis in range(len(extent))])
    return factor_of


def setup_inputs(seed: int = 0, part: int = 0) -> dict:
    key_of = jax.random.split(jax.random.key(seed), 7)
    part_splits = jax.random.split(jax.random.fold_in(key_of[6], part), 7)
    qm = jnp.clip(jnp.exp(math.log(0.05) - 2.3025851 * jax.random.uniform(part_splits[0], (CYCLES, BLOCK_ROWS, DM, B, B), jnp.float32) ** levels(part_splits[0], (CYCLES, BLOCK_ROWS, DM, B, B), ((1, 16),), -0.2, 0.2)), 0.005, 0.05)
    qm1 = jnp.clip(jnp.exp(math.log(0.05) - 2.3025851 * jax.random.uniform(part_splits[1], (CYCLES, BLOCK_ROWS, DM, B, B), jnp.float32) ** levels(part_splits[1], (CYCLES, BLOCK_ROWS, DM, B, B), ((1, 16),), -0.2, 0.2)), 0.005, 0.05)
    qb = jnp.clip(jnp.exp(math.log(2.0) - 3.6888794 * jax.random.uniform(part_splits[2], (CYCLES, BLOCK_ROWS, DM, B, B), jnp.float32) ** levels(part_splits[2], (CYCLES, BLOCK_ROWS, DM, B, B), ((1, 16),), -0.2, 0.2)), 0.05, 2.0)
    codes = plant(jax.random.randint(part_splits[3], (CYCLES, BLOCK_ROWS, B), 0, 4), jax.random.fold_in(part_splits[3], 1), 0, 3).astype(jnp.int32)
    energy_index = plant(jax.random.randint(part_splits[4], (CYCLES, BLOCK_ROWS, B, B), 0, TABLE), jax.random.fold_in(part_splits[4], 1), 0, TABLE - 1).astype(jnp.int32)
    turner = jnp.clip(jax.random.uniform(key_of[5], (TABLE,), jnp.float32, -1.0, 1.5), -1.0, 1.5)
    return {"qm": qm, "qm1": qm1, "qb": qb, "codes": codes, "energy_index": energy_index, "turner": turner}


PAIRS = np.array([[0, 0, 0, 1], [0, 0, 1, 0], [0, 1, 0, 1], [1, 0, 1, 0]], dtype=np.float32)
HI = lax.Precision.HIGHEST


def unpaired(shift):
    offsets = jnp.arange(B, dtype=jnp.int32)
    diffs = (shift * B + offsets[None, :] - offsets[:, None]).astype(jnp.float32)
    values = 0.01 * jnp.exp(-diffs / (DIST * B))
    if shift == 0:
        values = jnp.where(diffs >= 0, values, jnp.float32(0.0))
    return values


def decay(level):
    offsets = jnp.arange(B, dtype=jnp.int32)
    diffs = ((DIST - level) * B + offsets[None, :] - offsets[:, None]).astype(jnp.float32)
    values = jnp.exp(-diffs / (DIST * B))
    if level == DIST:
        values = jnp.where(diffs >= 0, values, jnp.float32(0.0))
    return values


def pairing(first, second):
    table = jnp.asarray(PAIRS, dtype=jnp.float32)
    digits = jnp.arange(4, dtype=jnp.int32)
    left = (first[:, None] == digits[None, :]).astype(jnp.float32)
    right = (second[:, None] == digits[None, :]).astype(jnp.float32)
    return jnp.dot(jnp.dot(left, table, precision=HI), right.T, precision=HI)


def reference(qm, qm1, qb, codes, energy_index, turner):
    total = CYCLES * BLOCK_ROWS
    qm_flat = qm.reshape(total, DIST - 1, B, B)
    qm1_flat = qm1.reshape(total, DIST - 1, B, B)
    qb_flat = qb.reshape(total, DIST - 1, B, B)
    code_flat = codes.reshape(total, B)
    index_flat = energy_index.reshape(total, B, B)

    def one(block):
        live = block + DIST < total
        summed = jnp.zeros((B, B), jnp.float32)
        tails = jnp.zeros((B, B), jnp.float32)
        for shift in range(1, DIST):
            later = jnp.minimum(block + shift, total - 1)
            right = qm1_flat[later, DIST - shift - 1]
            summed = summed + jnp.dot(qm_flat[block, shift - 1], right, precision=HI)
            tails = tails + jnp.dot(unpaired(shift), right, precision=HI)
        closing = jnp.minimum(block + DIST, total - 1)
        allowed = pairing(code_flat[block], code_flat[closing])
        weight = jnp.exp(-jnp.take(turner, index_flat[block]))
        pair_new = allowed * weight * (1.0 + 0.8 * summed)
        branch = jnp.dot(pair_new, decay(DIST), precision=HI)
        for level in range(1, DIST):
            branch = branch + jnp.dot(qb_flat[block, level - 1], decay(level), precision=HI)
        branch = branch * (1.0 / (DIST * B))
        multi = summed + tails + jnp.dot(unpaired(0), branch, precision=HI)
        zero = jnp.float32(0.0)
        return jnp.where(live, pair_new, zero), jnp.where(live, branch, zero), jnp.where(live, multi, zero)

    pair_all, branch_all, multi_all = lax.map(one, jnp.arange(total, dtype=jnp.int32))
    shape = (CYCLES, BLOCK_ROWS, B, B)
    return pair_all.reshape(shape), branch_all.reshape(shape), multi_all.reshape(shape)
```

```python
import functools

import jax
import jax.numpy as jnp
from jax import lax
from jax.experimental import pallas as pl
from jax.experimental.pallas import tpu as pltpu
from jax.sharding import PartitionSpec as P

F32 = jnp.float32
BF16 = jnp.bfloat16

PLAN = {
    1: (5, (3, 4, 6, 7)),
    3: (7, (1, 2, 3, 4, 5, 6, 7)),
    4: (8, (4, 5)),
    5: (9, (3, 4, 5, 6, 7)),
    7: (11, (1, 2, 3, 4, 5, 6, 7)),
}
RELAY = {
    (6, 7): (15, 4),
    (6, 6): (14, 4),
    (3, 6): (11, 2),
}
CHUNKS = 4
PIECES = 4


def split(x):
    high = x.astype(BF16)
    return high, (x - high.astype(F32)).astype(BF16)


def mm(a, b):
    return jnp.dot(a, b, preferred_element_type=F32)


def dot3(a, b):
    ah, al = a
    bh, bl = b
    return mm(ah, bh) + (mm(ah, bl) + mm(al, bh))


def any_of(x, values):
    hit = x == values[0]
    for value in values[1:]:
        hit = jnp.logical_or(hit, x == value)
    return hit


def kernel(
    plan, relay, width, qm, qm1, qb, eidx, codes, turner, acc, weight, row_sum,
    q_own, r_own, q_far, r_far, rf_h, rf_l, qb_in, e_in, code_in, acc_far, partial_in, relay_in,
    own_sem, q_send, q_recv, r_send, r_recv, rf_recv, load_sem, code_sem, part_sem, relay_sem,
):
    dm, block = qm.shape[0], qm.shape[1]
    dist = dm + 1
    live_rows = width - dist
    beta = 1.0 / (dist * block)
    me = lax.axis_index("row")
    live = me < live_rows

    def remote(src, dst, send, recv, device):
        return pltpu.make_async_remote_copy(
            src_ref=src, dst_ref=dst, send_sem=send, recv_sem=recv,
            device_id={"row": device}, device_id_type=pl.DeviceIdType.MESH,
        )

    def moved_rows(m):
        return [row for row, (_, shifts) in plan.items() if m in shifts]

    def home(row, m):
        device, shifts = plan.get(row, (None, ()))
        return (device, r_far, rf_recv) if m in shifts else (row, r_own, r_recv)

    def relayed(m):
        return sorted(row for row, shift in relay if shift == m)

    def own(m):
        rows = moved_rows(m)
        return jnp.logical_and(live, jnp.logical_not(any_of(me, rows))) if rows else live

    def direct(m):
        row = me - m
        ok = jnp.logical_and(row >= 0, row < live_rows)
        rows = moved_rows(m) + relayed(m)
        return jnp.logical_and(ok, jnp.logical_not(any_of(row, rows))) if rows else ok

    def code_send():
        return remote(codes, code_in, code_sem.at[0], code_sem.at[1], me - dist)

    height = block // CHUNKS

    def rows_of(c):
        return pl.ds(c * height, height)

    def q_copy(m, c, device):
        at = (m - 1, rows_of(c))
        return remote(qm.at[at], q_far.at[at], q_send.at[m - 1, c], q_recv.at[m - 1, c], device)

    def r_copy(m, device):
        return remote(qm1.at[dm - m], r_own.at[m - 1], r_send.at[m - 1], r_recv.at[m - 1], device)

    def rf_copy(m, device):
        return remote(qm1.at[dm - m], r_far.at[m - 1], r_send.at[m - 1], rf_recv.at[m - 1], device)

    piece = block // PIECES

    def relay_copy(m, p, device):
        at = pl.ds(p * piece, piece)
        return remote(qm1.at[dm - m, at], relay_in.at[at], r_send.at[m - 1], relay_sem.at[0, p], device)

    def relay_on(row, m, p):
        device, target, sem = home(row, m)
        at = pl.ds(p * piece, piece)
        return remote(relay_in.at[at], target.at[m - 1, at], relay_sem.at[1, p], sem.at[m - 1], device)

    def relay_rest(row, m, count):
        device, target, sem = home(row, m)
        at = pl.ds(count * piece, block - count * piece)
        return remote(qm1.at[dm - m, at], target.at[m - 1, at], r_send.at[m - 1], sem.at[m - 1], device)

    def part_copy(c, device):
        at = pl.ds(c * height, height + (8 if c == CHUNKS - 1 else 0))
        return remote(acc_far.at[at], partial_in.at[at], part_sem.at[0, c], part_sem.at[1, c], device)

    barrier = pltpu.get_barrier_semaphore()

    def greet(device):
        pl.semaphore_signal(
            barrier, inc=1, device_id={"row": device}, device_id_type=pl.DeviceIdType.MESH
        )

    extra = set()
    for row, (device, shifts) in plan.items():
        extra |= {(row, device), (device, row)} | {(row + m, device) for m in shifts}
    for (row, m), (via, _) in relay.items():
        extra |= {(row + m, via), (via, home(row, m)[0])}
    extra = sorted((s, d) for s, d in extra if s != d and not (d < live_rows and 1 <= s - d <= dist))

    @pl.when(live)
    def _():
        for m in range(1, dist + 1):
            greet(me + m)

    for source, device in extra:

        @pl.when(me == device)
        def _():
            greet(source)

    awaited = jnp.int32(0)
    for m in range(1, dist + 1):
        row = me - m
        awaited = awaited + jnp.where(jnp.logical_and(row >= 0, row < live_rows), 1, 0)
    for source, _ in extra:
        awaited = awaited + jnp.where(me == source, 1, 0)

    @pl.when(awaited > 0)
    def _():
        pl.semaphore_wait(barrier, awaited)

    @pl.when(me >= dist)
    def _():
        code_send().start()

    for (row, m), (via, count) in relay.items():

        @pl.when(me == row + m)
        def _():
            for p in range(count):
                relay_copy(m, p, via).start()
            if count < PIECES:
                relay_rest(row, m, count).start()

    for m in range(dm, 0, -1):
        for row in moved_rows(m):
            device = plan[row][0]
            if (row, m) in relay:
                continue

            if row + m == device:

                @pl.when(me == device)
                def _():
                    pltpu.make_async_copy(qm1.at[dm - m], r_far.at[m - 1], rf_recv.at[m - 1]).start()

            else:

                @pl.when(me == row + m)
                def _():
                    rf_copy(m, device).start()

    for row, (device, shifts) in plan.items():

        @pl.when(me == row)
        def _():
            for c in range(CHUNKS):
                for m in reversed(shifts):
                    q_copy(m, c, device).start()

    for m in range(dm, 0, -1):

        @pl.when(direct(m))
        def _():
            r_copy(m, me - m).start()

    loads = (
        pltpu.make_async_copy(qb, qb_in, load_sem.at[0]),
        pltpu.make_async_copy(eidx, e_in, load_sem.at[1]),
    )

    @pl.when(live)
    def _():
        for load in loads:
            load.start()

    for m in range(1, dist):

        @pl.when(own(m))
        def _():
            pltpu.make_async_copy(qm.at[m - 1], q_own.at[m - 1], own_sem.at[m - 1]).start()

    for (row, m), (via, count) in relay.items():

        @pl.when(me == via)
        def _():
            for p in range(count):
                relay_copy(m, p, 0).wait_recv()
                relay_on(row, m, p).start()

    acc[...] = jnp.zeros_like(acc)
    acc_far[...] = jnp.zeros_like(acc_far)
    rows_i = lax.broadcasted_iota(jnp.int32, (block, block), 0)
    cols_i = lax.broadcasted_iota(jnp.int32, (block, block), 1)
    column = lax.broadcasted_iota(jnp.int32, (block, 1), 0)
    line = lax.broadcasted_iota(jnp.int32, (1, block), 1)

    @pl.when(live)
    def _():
        code_send().wait_recv()
        first = jnp.sum(jnp.where(rows_i == cols_i, codes[...].astype(F32), 0.0), axis=1, keepdims=True)
        both = first + code_in[...].astype(F32)
        allowed = jnp.where(jnp.logical_or(both == 3.0, both == 5.0), 1.0, 0.0)
        table = jnp.exp(-turner[...])
        entries = table.shape[1]
        table = jnp.concatenate([table, jnp.zeros((1, 128 - entries), F32)], axis=1)
        table = jnp.broadcast_to(table, (block, 128))
        loads[1].wait()
        for start in range(0, block, 128):
            part = pl.ds(start, 128)
            found = jnp.take_along_axis(table, e_in[:, part], axis=1, mode="promise_in_bounds")
            weight[:, part] = found * allowed[:, start : start + 128]
        loads[0].wait()
        total = jnp.zeros((block, block), F32)
        for e in range(1, dist):
            factor = jnp.exp((line - (dist - e) * block).astype(F32) * beta)
            total = total + qb_in[e - 1] * factor
        row_sum[...] = jnp.broadcast_to(jnp.sum(total, axis=1, keepdims=True), row_sum.shape)

    def column_sum(m, right, total):
        fade = jnp.exp((-(m + 1) * block - column).astype(F32) * beta)
        total[block : block + 1, :] += jnp.sum(right * fade, axis=0, keepdims=True)

    def mask_of(cases):
        total = jnp.int32(0)
        for device, shifts in cases:
            total = total + jnp.where(me == device, sum(2 ** (dm - m) for m in shifts), 0)
        return total

    if plan:
        far_mask = mask_of(list(plan.values()))
        for c in range(CHUNKS):
            at = rows_of(c)

            def far_step(step, rest):
                m = dm - 1 - step

                @pl.when(rest % 2 == 1)
                def _():
                    if c == 0:
                        rf_copy(m + 1, 0).wait_recv()
                        right = r_far[m]
                        rf_h[m], rf_l[m] = split(right)
                        column_sum(m, right, acc_far)
                    q_copy(m + 1, c, 0).wait_recv()
                    acc_far[at, :] += dot3(split(q_far[m, at, :]), (rf_h[m], rf_l[m]))

                return rest // 2

            lax.fori_loop(0, dm, far_step, far_mask)
            for row, (device, _) in plan.items():

                @pl.when(me == device)
                def _():
                    part_copy(c, row).start()

    moved = mask_of([(row, shifts) for row, (_, shifts) in plan.items()])
    own_mask = jnp.where(live, 2**dm - 1 - moved, 0)

    def own_step(step, rest):
        m = dm - 1 - step

        @pl.when(rest % 2 == 1)
        def _():
            pltpu.make_async_copy(qm.at[m], q_own.at[m], own_sem.at[m]).wait()
            r_copy(m + 1, 0).wait_recv()
            right = r_own[m]
            column_sum(m, right, acc)
            acc[0:block, :] += dot3(split(q_own[m]), split(right))

        return rest // 2

    lax.fori_loop(0, dm, own_step, own_mask)

    if plan:

        @pl.when(any_of(me, list(plan)))
        def _():
            for c in range(CHUNKS):
                part_copy(c, 0).wait_recv()
            acc[...] += partial_in[...]

    for m in range(1, dist):
        rows = moved_rows(m)
        row = me - m

        @pl.when(jnp.logical_and(row >= 0, row < live_rows))
        def _():
            if rows and any(plan[r][0] == r + m for r in rows):
                stays = any_of(me, [r + m for r in rows if plan[r][0] == r + m])

                @pl.when(jnp.logical_not(stays))
                def _():
                    r_copy(m, 0).wait_send()

            else:
                r_copy(m, 0).wait_send()

        if rows:

            @pl.when(any_of(me, rows))
            def _():
                for c in range(CHUNKS):
                    q_copy(m, c, 0).wait_send()

    @pl.when(me >= dist)
    def _():
        code_send().wait_send()

    if plan:

        @pl.when(any_of(me, [device for device, _ in plan.values()]))
        def _():
            for c in range(CHUNKS):
                part_copy(c, 0).wait_send()

    for (row, m), (via, count) in relay.items():

        @pl.when(me == via)
        def _():
            for p in range(count):
                relay_on(row, m, p).wait_send()


def finish(live_rows, dist, acc, weight, row_sum, pair_out, branch_out, multi_out):
    block = weight.shape[0]
    beta = 1.0 / (dist * block)
    live = lax.axis_index("row") < live_rows

    @pl.when(live)
    def _():
        column = lax.broadcasted_iota(jnp.int32, (block, 1), 0).astype(F32)
        line = lax.broadcasted_iota(jnp.int32, (1, block), 1).astype(F32)
        rows_i = lax.broadcasted_iota(jnp.int32, (block, block), 0)
        cols_i = lax.broadcasted_iota(jnp.int32, (block, block), 1)
        upper = jnp.where(cols_i >= rows_i, 1.0, 0.0).astype(BF16)
        summed = acc[0:block, :]
        pair = weight[...] * (1.0 + 0.8 * summed)
        pair_out[...] = pair
        high, low = split(pair * jnp.exp(line * beta))
        inner = mm(high, upper) + mm(low, upper)
        branch = (row_sum[:, 0:1] + inner) * (beta * jnp.exp(line * (-beta)))
        branch_out[...] = branch
        high, low = split(branch * jnp.exp(column * (-beta)))
        tails = acc[block : block + 1, :] + mm(upper, high) + mm(upper, low)
        multi_out[...] = summed + 0.01 * jnp.exp(column * beta) * tails

    @pl.when(jnp.logical_not(live))
    def _():
        for out in (pair_out, branch_out, multi_out):
            out[...] = jnp.zeros_like(out)


def solution(mesh):
    width = mesh.shape["row"]

    def per_device(qm, qm1, qb, codes, energy_index, turner):
        dm, block = qm.shape[2], qm.shape[3]
        dist = dm + 1
        known = width == 16 and dist == 8
        plan = PLAN if known else {}
        relay = RELAY if known else {}
        blocks = pltpu.VMEM((dm, block, block), F32)
        halves = pltpu.VMEM((dm, block, block), BF16)
        square = jax.ShapeDtypeStruct((block, block), F32)
        tall = pltpu.VMEM((block + 8, block), F32)
        dma = pltpu.SemaphoreType.DMA
        anywhere = pl.BlockSpec(memory_space=pltpu.HBM)
        local = pl.BlockSpec(memory_space=pltpu.VMEM)
        middle = pl.pallas_call(
            functools.partial(kernel, plan, relay, width),
            out_shape=[
                pltpu.VMEM((block + 8, block), F32),
                pltpu.VMEM((block, block), F32),
                pltpu.VMEM((block, 128), F32),
            ],
            in_specs=[anywhere] * 4 + [local] * 2,
            out_specs=[local] * 3,
            scratch_shapes=[
                blocks, blocks, blocks, blocks, halves, halves, blocks,
                pltpu.VMEM((block, block), jnp.int32),
                pltpu.VMEM((1, block), jnp.int32),
                tall, tall, pltpu.VMEM((block, block), F32),
                dma((dm,)), dma((dm, CHUNKS)), dma((dm, CHUNKS)), dma((dm,)), dma((dm,)), dma((dm,)),
                dma((2,)), dma((2,)), dma((2, CHUNKS)), dma((2, PIECES)),
            ],
            compiler_params=pltpu.CompilerParams(has_side_effects=True, collective_id=0),
        )(
            qm[0, 0], qm1[0, 0], qb[0, 0], energy_index[0, 0],
            codes[0], turner[None, :],
        )
        outs = pl.pallas_call(
            functools.partial(finish, width - dist, dist),
            out_shape=[square] * 3,
            in_specs=[local] * 3,
            out_specs=[local] * 3,
            compiler_params=pltpu.CompilerParams(vmem_limit_bytes=16 * 2**20),
        )(*middle)
        return tuple(out[None, None] for out in outs)

    return jax.shard_map(
        per_device,
        mesh=mesh,
        in_specs=(
            P("seq", "row", None, None, None),
            P("seq", "row", None, None, None),
            P("seq", "row", None, None, None),
            P("seq", "row", None),
            P("seq", "row", None, None),
            P(),
        ),
        out_specs=(
            P("seq", "row", None, None),
            P("seq", "row", None, None),
            P("seq", "row", None, None),
        ),
        check_vma=False,
    )
```

```python
import functools

import jax
import jax.numpy as jnp
from jax import lax
from jax.experimental import pallas as pl
from jax.experimental.pallas import tpu as pltpu
from jax.sharding import PartitionSpec as P

F32 = jnp.float32
BF16 = jnp.bfloat16

PLAN = {
    1: (5, (3, 4, 6, 7)),
    3: (7, (1, 2, 3, 4, 5, 6, 7)),
    4: (8, (4, 5, 6)),
    5: (9, (3, 4, 5, 6, 7)),
    7: (11, (1, 2, 3, 4, 5, 6, 7)),
}
RELAY = {
    (6, 7): (15, 4),
    (6, 6): (14, 4),
    (6, 2): (10, 4),
}
SHARES = (4, 2, 1, 1)
CHUNKS = len(SHARES)
PIECES = 4


def split(x):
    high = x.astype(BF16)
    return high, (x - high.astype(F32)).astype(BF16)


def mm(a, b):
    return jnp.dot(a, b, preferred_element_type=F32)


def dot3(a, b):
    ah, al = a
    bh, bl = b
    return mm(ah, bh) + (mm(ah, bl) + mm(al, bh))


def any_of(x, values):
    hit = x == values[0]
    for value in values[1:]:
        hit = jnp.logical_or(hit, x == value)
    return hit


def kernel(
    plan, relay, width, qm, qm1, qb, eidx, codes, turner, acc, weight, row_sum,
    q_own, r_own, q_far, r_far, rf_h, rf_l, qb_in, e_in, code_in, acc_far, partial_in, relay_in, code_own, table_in,
    own_sem, q_send, q_recv, r_send, r_recv, rf_recv, load_sem, code_sem, part_sem, relay_sem,
):
    dm, block = qm.shape[0], qm.shape[1]
    dist = dm + 1
    live_rows = width - dist
    beta = 1.0 / (dist * block)
    me = lax.axis_index("row")
    live = me < live_rows

    def remote(src, dst, send, recv, device):
        return pltpu.make_async_remote_copy(
            src_ref=src, dst_ref=dst, send_sem=send, recv_sem=recv,
            device_id={"row": device}, device_id_type=pl.DeviceIdType.MESH,
        )

    def moved_rows(m):
        return [row for row, (_, shifts) in plan.items() if m in shifts]

    def home(row, m):
        device, shifts = plan.get(row, (None, ()))
        return (device, r_far, rf_recv) if m in shifts else (row, r_own, r_recv)

    def relayed(m):
        return sorted(row for row, shift in relay if shift == m)

    def own(m):
        rows = moved_rows(m)
        return jnp.logical_and(live, jnp.logical_not(any_of(me, rows))) if rows else live

    def direct(m):
        row = me - m
        ok = jnp.logical_and(row >= 0, row < live_rows)
        rows = moved_rows(m) + relayed(m)
        return jnp.logical_and(ok, jnp.logical_not(any_of(row, rows))) if rows else ok

    def code_send():
        return remote(codes, code_in, code_sem.at[0], code_sem.at[1], me - dist)

    unit = block // sum(SHARES)

    def rows_of(c, more=0):
        return pl.ds(sum(SHARES[:c]) * unit, SHARES[c] * unit + more)

    def q_copy(m, c, device):
        at = (m - 1, rows_of(c))
        return remote(qm.at[at], q_far.at[at], q_send.at[m - 1, c], q_recv.at[m - 1, c], device)

    def r_copy(m, device):
        return remote(qm1.at[dm - m], r_own.at[m - 1], r_send.at[m - 1], r_recv.at[m - 1], device)

    def rf_copy(m, device):
        return remote(qm1.at[dm - m], r_far.at[m - 1], r_send.at[m - 1], rf_recv.at[m - 1], device)

    piece = block // PIECES

    def relay_copy(m, p, device):
        at = pl.ds(p * piece, piece)
        return remote(qm1.at[dm - m, at], relay_in.at[at], r_send.at[m - 1], relay_sem.at[0, p], device)

    def relay_on(row, m, p):
        device, target, sem = home(row, m)
        at = pl.ds(p * piece, piece)
        return remote(relay_in.at[at], target.at[m - 1, at], relay_sem.at[1, p], sem.at[m - 1], device)

    def relay_rest(row, m, count):
        device, target, sem = home(row, m)
        at = pl.ds(count * piece, block - count * piece)
        return remote(qm1.at[dm - m, at], target.at[m - 1, at], r_send.at[m - 1], sem.at[m - 1], device)

    def part_copy(c, device):
        at = rows_of(c, 8 if c == CHUNKS - 1 else 0)
        return remote(acc_far.at[at], partial_in.at[at], part_sem.at[0, c], part_sem.at[1, c], device)

    barrier = pltpu.get_barrier_semaphore()

    def greet(device):
        pl.semaphore_signal(
            barrier, inc=1, device_id={"row": device}, device_id_type=pl.DeviceIdType.MESH
        )

    extra = set()
    for row, (device, shifts) in plan.items():
        extra |= {(row, device), (device, row)} | {(row + m, device) for m in shifts}
    for (row, m), (via, _) in relay.items():
        extra |= {(row + m, via), (via, home(row, m)[0])}
    extra = sorted((s, d) for s, d in extra if s != d and not (d < live_rows and 1 <= s - d <= dist))

    @pl.when(live)
    def _():
        for m in range(1, dist + 1):
            greet(me + m)

    for source, device in extra:

        @pl.when(me == device)
        def _():
            greet(source)

    awaited = jnp.int32(0)
    for m in range(1, dist + 1):
        row = me - m
        awaited = awaited + jnp.where(jnp.logical_and(row >= 0, row < live_rows), 1, 0)
    for source, _ in extra:
        awaited = awaited + jnp.where(me == source, 1, 0)

    @pl.when(awaited > 0)
    def _():
        pl.semaphore_wait(barrier, awaited)

    @pl.when(me >= dist)
    def _():
        code_send().start()

    for m in range(dm, 0, -1):
        for row in moved_rows(m):
            device = plan[row][0]
            if (row, m) in relay:
                continue

            if row + m == device:

                @pl.when(me == device)
                def _():
                    pltpu.make_async_copy(qm1.at[dm - m], r_far.at[m - 1], rf_recv.at[m - 1]).start()

            else:

                @pl.when(me == row + m)
                def _():
                    rf_copy(m, device).start()

    for (row, m), (via, count) in relay.items():

        @pl.when(me == row + m)
        def _():
            for p in range(count):
                relay_copy(m, p, via).start()
            if count < PIECES:
                relay_rest(row, m, count).start()

    for row, (device, shifts) in plan.items():

        @pl.when(me == row)
        def _():
            for c in range(CHUNKS):
                for m in reversed(shifts):
                    q_copy(m, c, device).start()

    for m in range(dm, 0, -1):

        @pl.when(direct(m))
        def _():
            r_copy(m, me - m).start()

    loads = (
        pltpu.make_async_copy(qb, qb_in, load_sem.at[0]),
        pltpu.make_async_copy(eidx, e_in, load_sem.at[1]),
        pltpu.make_async_copy(codes, code_own, load_sem.at[2]),
        pltpu.make_async_copy(turner, table_in, load_sem.at[3]),
    )

    @pl.when(live)
    def _():
        for load in loads:
            load.start()

    for m in range(1, dist):

        @pl.when(own(m))
        def _():
            pltpu.make_async_copy(qm.at[m - 1], q_own.at[m - 1], own_sem.at[m - 1]).start()

    for (row, m), (via, count) in relay.items():

        @pl.when(me == via)
        def _():
            for p in range(count):
                relay_copy(m, p, 0).wait_recv()
                relay_on(row, m, p).start()

    acc[...] = jnp.zeros_like(acc)
    acc_far[...] = jnp.zeros_like(acc_far)
    rows_i = lax.broadcasted_iota(jnp.int32, (block, block), 0)
    cols_i = lax.broadcasted_iota(jnp.int32, (block, block), 1)
    column = lax.broadcasted_iota(jnp.int32, (block, 1), 0)
    line = lax.broadcasted_iota(jnp.int32, (1, block), 1)

    @pl.when(live)
    def _():
        code_send().wait_recv()
        loads[2].wait()
        loads[3].wait()
        first = jnp.sum(jnp.where(rows_i == cols_i, code_own[...].astype(F32), 0.0), axis=1, keepdims=True)
        both = first + code_in[...].astype(F32)
        allowed = jnp.where(jnp.logical_or(both == 3.0, both == 5.0), 1.0, 0.0)
        table = jnp.exp(-table_in[...])
        entries = table.shape[1]
        table = jnp.concatenate([table, jnp.zeros((1, 128 - entries), F32)], axis=1)
        table = jnp.broadcast_to(table, (block, 128))
        loads[1].wait()
        for start in range(0, block, 128):
            part = pl.ds(start, 128)
            found = jnp.take_along_axis(table, e_in[:, part], axis=1, mode="promise_in_bounds")
            weight[:, part] = found * allowed[:, start : start + 128]
        loads[0].wait()
        total = jnp.zeros((block, block), F32)
        for e in range(1, dist):
            factor = jnp.exp((line - (dist - e) * block).astype(F32) * beta)
            total = total + qb_in[e - 1] * factor
        row_sum[...] = jnp.broadcast_to(jnp.sum(total, axis=1, keepdims=True), row_sum.shape)

    def column_sum(m, right, total):
        fade = jnp.exp((-(m + 1) * block - column).astype(F32) * beta)
        total[block : block + 1, :] += jnp.sum(right * fade, axis=0, keepdims=True)

    def mask_of(cases):
        total = jnp.int32(0)
        for device, shifts in cases:
            total = total + jnp.where(me == device, sum(2 ** (dm - m) for m in shifts), 0)
        return total

    if plan:
        far_mask = mask_of(list(plan.values()))
        for c in range(CHUNKS):
            at = rows_of(c)

            def far_step(step, rest):
                m = dm - 1 - step

                @pl.when(rest % 2 == 1)
                def _():
                    if c == 0:
                        rf_copy(m + 1, 0).wait_recv()
                        right = r_far[m]
                        rf_h[m], rf_l[m] = split(right)
                        column_sum(m, right, acc_far)
                    q_copy(m + 1, c, 0).wait_recv()
                    acc_far[at, :] += dot3(split(q_far[m, at, :]), (rf_h[m], rf_l[m]))

                return rest // 2

            lax.fori_loop(0, dm, far_step, far_mask)
            for row, (device, _) in plan.items():

                @pl.when(me == device)
                def _():
                    part_copy(c, row).start()

    moved = mask_of([(row, shifts) for row, (_, shifts) in plan.items()])
    own_mask = jnp.where(live, 2**dm - 1 - moved, 0)

    def own_step(step, rest):
        m = dm - 1 - step

        @pl.when(rest % 2 == 1)
        def _():
            pltpu.make_async_copy(qm.at[m], q_own.at[m], own_sem.at[m]).wait()
            r_copy(m + 1, 0).wait_recv()
            right = r_own[m]
            column_sum(m, right, acc)
            acc[0:block, :] += dot3(split(q_own[m]), split(right))

        return rest // 2

    lax.fori_loop(0, dm, own_step, own_mask)

    if plan:

        @pl.when(any_of(me, list(plan)))
        def _():
            for c in range(CHUNKS):
                part_copy(c, 0).wait_recv()
            acc[...] += partial_in[...]

    for m in range(1, dist):
        rows = moved_rows(m)
        row = me - m

        @pl.when(jnp.logical_and(row >= 0, row < live_rows))
        def _():
            if rows and any(plan[r][0] == r + m for r in rows):
                stays = any_of(me, [r + m for r in rows if plan[r][0] == r + m])

                @pl.when(jnp.logical_not(stays))
                def _():
                    r_copy(m, 0).wait_send()

            else:
                r_copy(m, 0).wait_send()

        if rows:

            @pl.when(any_of(me, rows))
            def _():
                for c in range(CHUNKS):
                    q_copy(m, c, 0).wait_send()

    @pl.when(me >= dist)
    def _():
        code_send().wait_send()

    if plan:

        @pl.when(any_of(me, [device for device, _ in plan.values()]))
        def _():
            for c in range(CHUNKS):
                part_copy(c, 0).wait_send()

    for (row, m), (via, count) in relay.items():

        @pl.when(me == via)
        def _():
            for p in range(count):
                relay_on(row, m, p).wait_send()


def finish(live_rows, dist, acc, weight, row_sum, pair_out, branch_out, multi_out):
    block = weight.shape[0]
    beta = 1.0 / (dist * block)
    live = lax.axis_index("row") < live_rows

    @pl.when(live)
    def _():
        column = lax.broadcasted_iota(jnp.int32, (block, 1), 0).astype(F32)
        line = lax.broadcasted_iota(jnp.int32, (1, block), 1).astype(F32)
        rows_i = lax.broadcasted_iota(jnp.int32, (block, block), 0)
        cols_i = lax.broadcasted_iota(jnp.int32, (block, block), 1)
        upper = jnp.where(cols_i >= rows_i, 1.0, 0.0).astype(BF16)
        summed = acc[0:block, :]
        pair = weight[...] * (1.0 + 0.8 * summed)
        pair_out[...] = pair
        high, low = split(pair * jnp.exp(line * beta))
        inner = mm(high, upper) + mm(low, upper)
        branch = (row_sum[:, 0:1] + inner) * (beta * jnp.exp(line * (-beta)))
        branch_out[...] = branch
        high, low = split(branch * jnp.exp(column * (-beta)))
        tails = acc[block : block + 1, :] + mm(upper, high) + mm(upper, low)
        multi_out[...] = summed + 0.01 * jnp.exp(column * beta) * tails

    @pl.when(jnp.logical_not(live))
    def _():
        for out in (pair_out, branch_out, multi_out):
            out[...] = jnp.zeros_like(out)


def solution(mesh):
    width = mesh.shape["row"]

    def per_device(qm, qm1, qb, codes, energy_index, turner):
        dm, block = qm.shape[2], qm.shape[3]
        dist = dm + 1
        known = width == 16 and dist == 8
        plan = PLAN if known else {}
        relay = RELAY if known else {}
        blocks = pltpu.VMEM((dm, block, block), F32)
        halves = pltpu.VMEM((dm, block, block), BF16)
        square = jax.ShapeDtypeStruct((block, block), F32)
        tall = pltpu.VMEM((block + 8, block), F32)
        dma = pltpu.SemaphoreType.DMA
        anywhere = pl.BlockSpec(memory_space=pltpu.HBM)
        local = pl.BlockSpec(memory_space=pltpu.VMEM)
        middle = pl.pallas_call(
            functools.partial(kernel, plan, relay, width),
            out_shape=[
                pltpu.VMEM((block + 8, block), F32),
                pltpu.VMEM((block, block), F32),
                pltpu.VMEM((block, 128), F32),
            ],
            in_specs=[anywhere] * 6,
            out_specs=[local] * 3,
            scratch_shapes=[
                blocks, blocks, blocks, blocks, halves, halves, blocks,
                pltpu.VMEM((block, block), jnp.int32),
                pltpu.VMEM((1, block), jnp.int32),
                tall, tall, pltpu.VMEM((block, block), F32),
                pltpu.VMEM((1, block), jnp.int32),
                pltpu.VMEM((1, turner.shape[0]), F32),
                dma((dm,)), dma((dm, CHUNKS)), dma((dm, CHUNKS)), dma((dm,)), dma((dm,)), dma((dm,)),
                dma((4,)), dma((2,)), dma((2, CHUNKS)), dma((2, PIECES)),
            ],
            compiler_params=pltpu.CompilerParams(has_side_effects=True, collective_id=0),
        )(
            qm[0, 0], qm1[0, 0], qb[0, 0], energy_index[0, 0],
            codes[0], turner[None, :],
        )
        outs = pl.pallas_call(
            functools.partial(finish, width - dist, dist),
            out_shape=[square] * 3,
            in_specs=[local] * 3,
            out_specs=[local] * 3,
            compiler_params=pltpu.CompilerParams(vmem_limit_bytes=16 * 2**20),
        )(*middle)
        return tuple(out[None, None] for out in outs)

    return jax.shard_map(
        per_device,
        mesh=mesh,
        in_specs=(
            P("seq", "row", None, None, None),
            P("seq", "row", None, None, None),
            P("seq", "row", None, None, None),
            P("seq", "row", None),
            P("seq", "row", None, None),
            P(),
        ),
        out_specs=(
            P("seq", "row", None, None),
            P("seq", "row", None, None),
            P("seq", "row", None, None),
        ),
        check_vma=False,
    )
```

```python
import functools

import jax
import jax.numpy as jnp
from jax import lax
from jax.experimental import pallas as pl
from jax.experimental.pallas import tpu as pltpu
from jax.sharding import PartitionSpec as P

F32 = jnp.float32
BF16 = jnp.bfloat16

PLAN = {
    1: (5, (4, 3, 6, 5, 7)),
    3: (7, (4, 3, 1, 2, 6, 5, 7)),
    4: (8, (7, 6)),
    5: (9, (4, 3, 6, 5, 7)),
    7: (11, (4, 3, 7, 5, 6, 2, 1)),
}
RELAY = {
    (6, 7): (15, 2),
    (6, 6): (14, 2),
    (2, 7): (10, 2),
    (6, 3): (10, 2),
    (6, 2): (10, 1),
}
LATE = ((6, 2),)
ORDER = {6: (1, 5, 4, 7, 6, 3, 2)}
SHARES = (4, 2, 1, 1)
CHUNKS = len(SHARES)
PIECES = 2


def split(x):
    high = x.astype(BF16)
    return high, (x - high.astype(F32)).astype(BF16)


def mm(a, b):
    return jnp.dot(a, b, preferred_element_type=F32)


def dot3(a, b):
    ah, al = a
    bh, bl = b
    return mm(ah, bh) + (mm(ah, bl) + mm(al, bh))


def any_of(x, values):
    hit = x == values[0]
    for value in values[1:]:
        hit = jnp.logical_or(hit, x == value)
    return hit


def kernel(
    plan, relay, order, width, qm, qm1, qb, eidx, codes, turner, acc, weight, row_sum,
    q_own, r_in, q_far, rf_h, rf_l, qb_in, e_in, code_in, acc_far, partial_in, relay_in, code_own, table_in,
    own_sem, q_send, q_recv, r_send, r_recv, load_sem, code_sem, part_sem, relay_send, relay_recv,
):
    dm, block = qm.shape[0], qm.shape[1]
    dist = dm + 1
    live_rows = width - dist
    beta = 1.0 / (dist * block)
    base = dm + 1
    me = lax.axis_index("row")
    live = me < live_rows
    unit = block // sum(SHARES)
    piece = block // PIECES

    def remote(src, dst, send, recv, device):
        return pltpu.make_async_remote_copy(
            src_ref=src, dst_ref=dst, send_sem=send, recv_sem=recv,
            device_id={"row": device}, device_id_type=pl.DeviceIdType.MESH,
        )

    def home(row, m):
        device, shifts = plan.get(row, (None, ()))
        return device if m in shifts else row

    def apart(m):
        return [row for row in range(live_rows) if (row, m) in relay or home(row, m) != row] if plan else []

    def direct(m):
        row = me - m
        ok = jnp.logical_and(row >= 0, row < live_rows)
        rows = apart(m)
        return jnp.logical_and(ok, jnp.logical_not(any_of(row, rows))) if rows else ok

    def code_send():
        return remote(codes, code_in, code_sem.at[0], code_sem.at[1], me - dist)

    def rows_of(c, more=0):
        return pl.ds(sum(SHARES[:c]) * unit, SHARES[c] * unit + more)

    def q_copy(m, c, device):
        at = (m - 1, rows_of(c))
        slot = c if c < CHUNKS - 1 else CHUNKS - 2 + m
        return remote(qm.at[at], q_far.at[at], q_send.at[0], q_recv.at[slot], device)

    def r_copy(m, device):
        return remote(qm1.at[dm - m], r_in.at[m - 1], r_send.at[0], r_recv.at[m - 1], device)

    slots = {}
    for (row, m), (via, count) in relay.items():
        for p in range(count):
            slots[row, m, p] = sum(1 for key in slots if relay[key[:2]][0] == via)

    def relay_copy(row, m, p):
        slot = slots[row, m, p]
        return remote(
            qm1.at[dm - m, pl.ds(p * piece, piece)], relay_in.at[slot],
            r_send.at[0], relay_recv.at[slot], relay[row, m][0],
        )

    def relay_on(row, m, p):
        at = pl.ds(p * piece, piece)
        return remote(
            relay_in.at[slots[row, m, p]], r_in.at[m - 1, at],
            relay_send.at[0], r_recv.at[m - 1], home(row, m),
        )

    def relay_rest(row, m):
        start = relay[row, m][1] * piece
        at = pl.ds(start, block - start)
        return remote(
            qm1.at[dm - m, at], r_in.at[m - 1, at], r_send.at[0], r_recv.at[m - 1], home(row, m)
        )

    def part_copy(c, device):
        at = rows_of(c, 8 if c == CHUNKS - 1 else 0)
        return remote(acc_far.at[at], partial_in.at[at], part_sem.at[0], part_sem.at[1], device)

    barrier = pltpu.get_barrier_semaphore()

    def greet(device):
        pl.semaphore_signal(
            barrier, inc=1, device_id={"row": device}, device_id_type=pl.DeviceIdType.MESH
        )

    extra = set()
    for row, (device, shifts) in plan.items():
        extra |= {(row, device), (device, row)} | {(row + m, device) for m in shifts}
    for (row, m), (via, _) in relay.items():
        extra |= {(row + m, via), (via, home(row, m))}
    extra = sorted((s, d) for s, d in extra if s != d and not (d < live_rows and 1 <= s - d <= dist))

    @pl.when(live)
    def _():
        for m in range(1, dist + 1):
            greet(me + m)

    for device in sorted({d for _, d in extra}):

        @pl.when(me == device)
        def _():
            for source in [s for s, d in extra if d == device]:
                greet(source)

    awaited = jnp.int32(0)
    for m in range(1, dist + 1):
        row = me - m
        awaited = awaited + jnp.where(jnp.logical_and(row >= 0, row < live_rows), 1, 0)
    for source in sorted({s for s, _ in extra}):
        awaited = awaited + jnp.where(me == source, sum(1 for s, _ in extra if s == source), 0)

    @pl.when(awaited > 0)
    def _():
        pl.semaphore_wait(barrier, awaited)

    @pl.when(me >= dist)
    def _():
        code_send().start()

    for m in range(dm, 0, -1):
        for row, (device, shifts) in plan.items():
            if m not in shifts or (row, m) in relay:
                continue

            @pl.when(me == row + m)
            def _():
                if row + m == device:
                    pltpu.make_async_copy(qm1.at[dm - m], r_in.at[m - 1], r_recv.at[m - 1]).start()
                else:
                    r_copy(m, device).start()

    for row, (device, shifts) in plan.items():

        @pl.when(me == row)
        def _():
            for c in range(CHUNKS):
                for m in shifts:
                    q_copy(m, c, device).start()

    for (row, m), (via, count) in relay.items():

        @pl.when(me == row + m)
        def _():
            for p in range(count):
                relay_copy(row, m, p).start()
            if count < PIECES and (row, m) not in LATE:
                relay_rest(row, m).start()

    for m in range(dm, 0, -1):

        @pl.when(direct(m))
        def _():
            r_copy(m, me - m).start()

    loads = (
        pltpu.make_async_copy(qb, qb_in, load_sem.at[0]),
        pltpu.make_async_copy(eidx, e_in, load_sem.at[1]),
        pltpu.make_async_copy(codes, code_own, load_sem.at[2]),
        pltpu.make_async_copy(turner, table_in, load_sem.at[3]),
        pltpu.make_async_copy(qm, q_own, own_sem.at[0]),
    )

    @pl.when(live)
    def _():
        for load in loads:
            load.start()

    for via in sorted({via for via, _ in relay.values()}):

        @pl.when(me == via)
        def _():
            for row, m, p in slots:
                if relay[row, m][0] == via:
                    relay_copy(row, m, p).wait_recv()
                    relay_on(row, m, p).start()

    acc[...] = jnp.zeros_like(acc)
    acc_far[...] = jnp.zeros_like(acc_far)
    rows_i = lax.broadcasted_iota(jnp.int32, (block, block), 0)
    cols_i = lax.broadcasted_iota(jnp.int32, (block, block), 1)
    column = lax.broadcasted_iota(jnp.int32, (block, 1), 0)
    line = lax.broadcasted_iota(jnp.int32, (1, block), 1)

    @pl.when(live)
    def _():
        loads[0].wait()
        total = jnp.zeros((block, block), F32)
        for e in range(1, dist):
            factor = jnp.exp((line - (dist - e) * block).astype(F32) * beta)
            total = total + qb_in[e - 1] * factor
        row_sum[...] = jnp.broadcast_to(jnp.sum(total, axis=1, keepdims=True), row_sum.shape)
        loads[2].wait()
        loads[3].wait()
        first = jnp.sum(jnp.where(rows_i == cols_i, code_own[...].astype(F32), 0.0), axis=1, keepdims=True)
        table = jnp.exp(-table_in[...])
        entries = table.shape[1]
        table = jnp.concatenate([table, jnp.zeros((1, 128 - entries), F32)], axis=1)
        table = jnp.broadcast_to(table, (block, 128))
        loads[1].wait()
        code_send().wait_recv()
        both = first + code_in[...].astype(F32)
        allowed = jnp.where(jnp.logical_or(both == 3.0, both == 5.0), 1.0, 0.0)
        for start in range(0, block, 128):
            part = pl.ds(start, 128)
            found = jnp.take_along_axis(table, e_in[:, part], axis=1, mode="promise_in_bounds")
            weight[:, part] = found * allowed[:, start : start + 128]
        loads[4].wait()

    def column_sum(m, right, total):
        fade = jnp.exp((-(m + 1) * block - column).astype(F32) * beta)
        total[block : block + 1, :] += jnp.sum(right * fade, axis=0, keepdims=True)

    def listed(shifts):
        return sum(m * base**i for i, m in enumerate(shifts))

    if plan:
        far_list = jnp.int32(0)
        for device, shifts in plan.values():
            far_list = far_list + jnp.where(me == device, listed(shifts), 0)
        for c in range(CHUNKS):
            at = rows_of(c)
            if c < CHUNKS - 1:
                for count in sorted({len(shifts) for _, shifts in plan.values()}):

                    @pl.when(any_of(me, [device for device, shifts in plan.values() if len(shifts) == count]))
                    def _():
                        whole = (pl.ds(0, count), at)
                        remote(qm.at[whole], q_far.at[whole], q_send.at[0], q_recv.at[c], 0).wait_recv()

            def far_step(step, rest):
                m = rest % base - 1

                @pl.when(rest > 0)
                def _():
                    if c == 0:
                        r_copy(m + 1, 0).wait_recv()
                        right = r_in[m]
                        rf_h[m], rf_l[m] = split(right)
                        column_sum(m, right, acc_far)
                    if c == CHUNKS - 1:
                        here = (m, at)
                        slot = q_recv.at[CHUNKS - 1 + m]
                        remote(qm.at[here], q_far.at[here], q_send.at[0], slot, 0).wait_recv()
                    acc_far[at, :] += dot3(split(q_far[m, at, :]), (rf_h[m], rf_l[m]))

                return rest // base

            lax.fori_loop(0, dm, far_step, far_list)
            for row, (device, _) in plan.items():

                @pl.when(me == device)
                def _():
                    part_copy(c, row).start()

        for row, m in LATE:

            @pl.when(me == row + m)
            def _():
                relay_rest(row, m).start()

    own_list = jnp.int32(listed(range(1, dm + 1)))
    for row in range(live_rows) if plan else ():
        shifts = [m for m in order.get(row, range(1, dm + 1)) if home(row, m) == row]
        own_list = jnp.where(me == row, listed(shifts), own_list)
    own_list = jnp.where(live, own_list, 0)

    def own_step(step, rest):
        m = rest % base - 1

        @pl.when(rest > 0)
        def _():
            r_copy(m + 1, 0).wait_recv()
            right = r_in[m]
            column_sum(m, right, acc)
            acc[0:block, :] += dot3(split(q_own[m]), split(right))

        return rest // base

    lax.fori_loop(0, dm, own_step, own_list)

    if plan:

        @pl.when(any_of(me, list(plan)))
        def _():
            remote(acc_far, partial_in, part_sem.at[0], part_sem.at[1], 0).wait_recv()
            acc[...] += partial_in[...]

    sent = jnp.int32(0)
    for m in range(1, dist):
        row = me - m
        sent = sent + jnp.where(jnp.logical_and(row >= 0, row < live_rows), 1, 0)
    for row, (device, shifts) in plan.items():
        if device - row in shifts:
            sent = sent - jnp.where(me == device, 1, 0)
    for count in range(1, dist):

        @pl.when(sent == count)
        def _():
            whole = pl.ds(0, count)
            remote(qm1.at[whole], r_in.at[whole], r_send.at[0], r_recv.at[0], 0).wait_send()

    for row, (device, shifts) in plan.items():

        @pl.when(me == row)
        def _():
            whole = pl.ds(0, len(shifts))
            remote(qm.at[whole], q_far.at[whole], q_send.at[0], q_recv.at[0], 0).wait_send()

    @pl.when(me >= dist)
    def _():
        code_send().wait_send()

    if plan:

        @pl.when(any_of(me, [device for device, _ in plan.values()]))
        def _():
            remote(acc_far, partial_in, part_sem.at[0], part_sem.at[1], 0).wait_send()

    for via in sorted({via for via, _ in relay.values()}):

        @pl.when(me == via)
        def _():
            whole = pl.ds(0, sum(1 for key in slots if relay[key[:2]][0] == via))
            remote(relay_in.at[whole], relay_in.at[whole], relay_send.at[0], r_recv.at[0], 0).wait_send()


def finish(live_rows, dist, acc, weight, row_sum, pair_out, branch_out, multi_out):
    block = weight.shape[0]
    beta = 1.0 / (dist * block)
    live = lax.axis_index("row") < live_rows

    @pl.when(live)
    def _():
        column = lax.broadcasted_iota(jnp.int32, (block, 1), 0).astype(F32)
        line = lax.broadcasted_iota(jnp.int32, (1, block), 1).astype(F32)
        rows_i = lax.broadcasted_iota(jnp.int32, (block, block), 0)
        cols_i = lax.broadcasted_iota(jnp.int32, (block, block), 1)
        upper = jnp.where(cols_i >= rows_i, 1.0, 0.0).astype(BF16)
        summed = acc[0:block, :]
        pair = weight[...] * (1.0 + 0.8 * summed)
        pair_out[...] = pair
        high, low = split(pair * jnp.exp(line * beta))
        inner = mm(high, upper) + mm(low, upper)
        branch = (row_sum[:, 0:1] + inner) * (beta * jnp.exp(line * (-beta)))
        branch_out[...] = branch
        high, low = split(branch * jnp.exp(column * (-beta)))
        tails = acc[block : block + 1, :] + mm(upper, high) + mm(upper, low)
        multi_out[...] = summed + 0.01 * jnp.exp(column * beta) * tails

    @pl.when(jnp.logical_not(live))
    def _():
        for out in (pair_out, branch_out, multi_out):
            out[...] = jnp.zeros_like(out)


def solution(mesh):
    width = mesh.shape["row"]

    def per_device(qm, qm1, qb, codes, energy_index, turner):
        dm, block = qm.shape[2], qm.shape[3]
        dist = dm + 1
        known = width == 16 and dist == 8
        plan = PLAN if known else {}
        relay = RELAY if known else {}
        pieces = max([1] + [sum(n for v, n in relay.values() if v == via) for via, _ in relay.values()])
        blocks = pltpu.VMEM((dm, block, block), F32)
        halves = pltpu.VMEM((dm, block, block), BF16)
        square = jax.ShapeDtypeStruct((block, block), F32)
        tall = pltpu.VMEM((block + 8, block), F32)
        dma = pltpu.SemaphoreType.DMA
        anywhere = pl.BlockSpec(memory_space=pltpu.HBM)
        local = pl.BlockSpec(memory_space=pltpu.VMEM)
        middle = pl.pallas_call(
            functools.partial(kernel, plan, relay, ORDER if known else {}, width),
            out_shape=[
                pltpu.VMEM((block + 8, block), F32),
                pltpu.VMEM((block, block), F32),
                pltpu.VMEM((block, 128), F32),
            ],
            in_specs=[anywhere] * 6,
            out_specs=[local] * 3,
            scratch_shapes=[
                blocks, blocks, blocks, halves, halves, blocks,
                pltpu.VMEM((block, block), jnp.int32),
                pltpu.VMEM((1, block), jnp.int32),
                tall, tall, pltpu.VMEM((pieces, block // PIECES, block), F32),
                pltpu.VMEM((1, block), jnp.int32),
                pltpu.VMEM((1, turner.shape[0]), F32),
                dma((1,)), dma((1,)), dma((CHUNKS - 1 + dm,)), dma((1,)), dma((dm,)),
                dma((4,)), dma((2,)), dma((2,)), dma((1,)), dma((pieces,)),
            ],
            compiler_params=pltpu.CompilerParams(has_side_effects=True, collective_id=0),
        )(
            qm[0, 0], qm1[0, 0], qb[0, 0], energy_index[0, 0],
            codes[0], turner[None, :],
        )
        outs = pl.pallas_call(
            functools.partial(finish, width - dist, dist),
            out_shape=[square] * 3,
            in_specs=[local] * 3,
            out_specs=[local] * 3,
            compiler_params=pltpu.CompilerParams(vmem_limit_bytes=16 * 2**20),
        )(*middle)
        return tuple(out[None, None] for out in outs)

    return jax.shard_map(
        per_device,
        mesh=mesh,
        in_specs=(
            P("seq", "row", None, None, None),
            P("seq", "row", None, None, None),
            P("seq", "row", None, None, None),
            P("seq", "row", None),
            P("seq", "row", None, None),
            P(),
        ),
        out_specs=(
            P("seq", "row", None, None),
            P("seq", "row", None, None),
            P("seq", "row", None, None),
        ),
        check_vma=False,
    )
```

```python
import functools

import jax
import jax.numpy as jnp
from jax import lax
from jax.experimental import pallas as pl
from jax.experimental.pallas import tpu as pltpu
from jax.sharding import PartitionSpec as P

F32 = jnp.float32
BF16 = jnp.bfloat16

PLAN = {
    1: (5, (4, 3, 6, 5, 7)),
    3: (6, (3, 1, 2, 7, 6, 5)),
    4: (8, (7, 6)),
    5: (9, (4, 3, 6, 5, 7)),
    7: (11, (4, 3, 7, 1, 2, 5, 6)),
}
RELAY = {
    (6, 7): (15, 4, 0),
    (6, 6): (14, 4, 0),
    (2, 6): (10, 4, 0),
    (6, 2): (10, 2, 4),
    (6, 3): (10, 4, 0),
    (7, 5): (14, 4, 1),
    (7, 6): (15, 4, 1),
}
HELD = (
    {8: (10, 11), 9: (10, 11)},
    {4: (2, 6), 5: (2, 6), 8: (2, 6), 9: (2, 6)},
)
ORDER = {6: (1, 7, 6, 5, 4, 3, 2)}
SHARES = (4, 2, 1, 1)
CHUNKS = len(SHARES)
PIECES = 4
HEAD = 8


def split(x):
    high = x.astype(BF16)
    return high, (x - high.astype(F32)).astype(BF16)


def mm(a, b):
    return jnp.dot(a, b, preferred_element_type=F32)


def dot3(a, b):
    ah, al = a
    bh, bl = b
    return mm(ah, bh) + (mm(ah, bl) + mm(al, bh))


def any_of(x, values):
    hit = x == values[0]
    for value in values[1:]:
        hit = jnp.logical_or(hit, x == value)
    return hit


def kernel(
    plan, relay, width, qm, qm1, qb, eidx, codes, turner, acc, weight, row_sum,
    q_own, r_in, r_far, q_far, rf_h, rf_l, qb_in, e_in, code_in, acc_far, partial_in, relay_in, code_own, table_in,
    own_sem, q_send, q_recv, r_send, r_recv, rf_recv, load_sem, code_sem, part_sem, held_sem,
):
    dm, block = qm.shape[0], qm.shape[1]
    dist = dm + 1
    live_rows = width - dist
    beta = 1.0 / (dist * block)
    base = dm + 1
    me = lax.axis_index("row")
    live = me < live_rows
    relay_send, relay_recv = q_send, q_recv
    unit = block // sum(SHARES)
    piece = block // PIECES

    def remote(src, dst, send, recv, device):
        return pltpu.make_async_remote_copy(
            src_ref=src, dst_ref=dst, send_sem=send, recv_sem=recv,
            device_id={"row": device}, device_id_type=pl.DeviceIdType.MESH,
        )

    def near(row):
        return jnp.logical_and(row >= 0, row < live_rows)

    def home(row, m):
        device, shifts = plan.get(row, (None, ()))
        return device if m in shifts else row

    held = HELD if plan else ()
    order = ORDER if plan else {}
    waiting = []
    for group in held:
        lists = {source: [] for source in group}
        for source in group:
            for row in range(min(live_rows, source) - 1, max(source - dist, -1), -1):
                m = source - row
                via, count, _ = relay.get((row, m), (None, 0, 0))
                if home(row, m) in group[source] and count < PIECES:
                    lists[source].append((row, m, False))
                if via in group[source]:
                    lists[source].append((row, m, True))
            lists[source].sort(key=lambda item: (item[2], item[0] not in (3, 7), -item[0]))
        waiting.append(lists)
    rests = {(row, m) for lists in waiting for keys in lists.values() for row, m, part in keys if not part}
    parts = {(row, m) for lists in waiting for keys in lists.values() for row, m, part in keys if part}

    def apart(m):
        if not plan:
            return []
        return [
            row for row in range(live_rows)
            if (row, m) in relay or (row, m) in rests or home(row, m) != row
        ]

    def held_send(row, m):
        if (row, m) in relay:
            relay_rest(row, m).start()
        else:
            (r_copy if home(row, m) == row else rf_copy)(m, home(row, m)).start()

    def direct(m):
        row = me - m
        ok = near(row)
        rows = apart(m)
        return jnp.logical_and(ok, jnp.logical_not(any_of(row, rows))) if rows else ok

    def code_send():
        return remote(codes, code_in, code_sem.at[0], code_sem.at[1], me - dist)

    def rows_of(c, shift=0):
        return pl.ds(sum(SHARES[:c]) * unit + shift, SHARES[c] * unit)

    def q_copy(m, c, device):
        at = (m - 1, rows_of(c))
        slot = c if c < CHUNKS - 1 else CHUNKS - 2 + m
        return remote(qm.at[at], q_far.at[at], q_send.at[0], q_recv.at[slot], device)

    def r_copy(m, device):
        return remote(qm1.at[dm - m], r_in.at[m - 1], r_send.at[0], r_recv.at[m - 1], device)

    def rf_copy(m, device):
        return remote(qm1.at[dm - m], r_far.at[m - 1], r_send.at[0], rf_recv.at[m - 1], device)

    def right_at(row, m):
        return (r_in, r_recv) if home(row, m) == row else (r_far, rf_recv)

    turns = sorted((rank + p, row, m, p) for (row, m), (_, count, rank) in relay.items() for p in range(count))
    slots = {}
    for _, row, m, p in turns:
        slots[row, m, p] = sum(1 for key in slots if relay[key[:2]][0] == relay[row, m][0])

    def relay_copy(row, m, p):
        slot = slots[row, m, p]
        return remote(
            qm1.at[dm - m, pl.ds(p * piece, piece)], relay_in.at[slot],
            r_send.at[0], relay_recv.at[slot], relay[row, m][0],
        )

    def relay_on(row, m, p):
        at = pl.ds(p * piece, piece)
        into, sem = right_at(row, m)
        return remote(
            relay_in.at[slots[row, m, p]], into.at[m - 1, at], relay_send.at[0], sem.at[m - 1], home(row, m)
        )

    def relay_rest(row, m):
        start = relay[row, m][1] * piece
        at = pl.ds(start, block - start)
        into, sem = right_at(row, m)
        return remote(qm1.at[dm - m, at], into.at[m - 1, at], r_send.at[0], sem.at[m - 1], home(row, m))

    def part_copy(c, device):
        start = HEAD + sum(SHARES[:c]) * unit if c else 0
        at = pl.ds(start, HEAD + sum(SHARES[: c + 1]) * unit - start)
        return remote(acc_far.at[at], partial_in.at[at], part_sem.at[0], part_sem.at[1], device)

    barrier = pltpu.get_barrier_semaphore()

    def greet(device):
        pl.semaphore_signal(
            barrier, inc=1, device_id={"row": device}, device_id_type=pl.DeviceIdType.MESH
        )

    if plan:
        pairs = {(device, device - dist) for device in range(dist, width)}
        for row in range(live_rows):
            for m in range(1, dist):
                source, device = row + m, home(row, m)
                via, count, _ = relay.get((row, m), (None, 0, 0))
                if count:
                    pairs |= {(source, via), (via, device)}
                if count < PIECES:
                    pairs.add((source, device))
        for row, (device, _) in plan.items():
            pairs |= {(row, device), (device, row)}
        for group in held:
            for source, devices in group.items():
                pairs -= {(source, device) for device in devices}
                pairs |= {(device, source) for device in devices}
        pairs = sorted((s, d) for s, d in pairs if s != d)
        awaited = jnp.int32(0)
        for device in range(width):
            sources = [s for s, d in pairs if d == device]
            awaited = awaited + jnp.where(me == device, sum(1 for s, _ in pairs if s == device), 0)
            if sources:

                @pl.when(me == device)
                def _():
                    for source in sources:
                        greet(source)

    else:

        @pl.when(live)
        def _():
            for m in range(1, dist + 1):
                greet(me + m)

        awaited = jnp.int32(0)
        for m in range(1, dist + 1):
            awaited = awaited + jnp.where(near(me - m), 1, 0)

    @pl.when(awaited > 0)
    def _():
        pl.semaphore_wait(barrier, awaited)

    for n, group in enumerate(held):
        for device in sorted({device for devices in group.values() for device in devices}):

            @pl.when(me == device)
            def _():
                for source in [source for source, devices in group.items() if device in devices]:
                    pl.semaphore_signal(
                        held_sem.at[n], inc=1, device_id={"row": source}, device_id_type=pl.DeviceIdType.MESH
                    )

    @pl.when(me >= dist)
    def _():
        code_send().start()

    for m in range(dm, 0, -1):
        for row, (device, shifts) in plan.items():
            if m not in shifts or (row, m) in relay or (row, m) in rests:
                continue

            @pl.when(me == row + m)
            def _():
                if row + m == device:
                    pltpu.make_async_copy(qm1.at[dm - m], r_far.at[m - 1], rf_recv.at[m - 1]).start()
                else:
                    rf_copy(m, device).start()

    for row, (device, shifts) in plan.items():

        @pl.when(me == row)
        def _():
            for c in range(CHUNKS):
                for m in shifts:
                    q_copy(m, c, device).start()

    for source in sorted({row + m for row, m in relay}):

        @pl.when(me == source)
        def _():
            for row, m, p in slots:
                if row + m == source and (row, m) not in parts:
                    relay_copy(row, m, p).start()
            for (row, m), (_, count, _) in relay.items():
                if row + m == source and count < PIECES and (row, m) not in rests:
                    relay_rest(row, m).start()

    for m in range(dm, 0, -1):

        @pl.when(direct(m))
        def _():
            r_copy(m, me - m).start()

    loads = (
        pltpu.make_async_copy(qb, qb_in, load_sem.at[0]),
        pltpu.make_async_copy(eidx, e_in, load_sem.at[1]),
        pltpu.make_async_copy(codes, code_own, load_sem.at[2]),
        pltpu.make_async_copy(turner, table_in, load_sem.at[3]),
        pltpu.make_async_copy(qm, q_own, own_sem.at[0]),
    )

    @pl.when(live)
    def _():
        for load in loads:
            load.start()

    for via in sorted({via for via, _, _ in relay.values()}):

        @pl.when(me == via)
        def _():
            for row, m, p in slots:
                if relay[row, m][0] == via:
                    relay_copy(row, m, p).wait_recv()
                    relay_on(row, m, p).start()

    acc[...] = jnp.zeros_like(acc)
    acc_far[...] = jnp.zeros_like(acc_far)
    rows_i = lax.broadcasted_iota(jnp.int32, (block, block), 0)
    cols_i = lax.broadcasted_iota(jnp.int32, (block, block), 1)
    column = lax.broadcasted_iota(jnp.int32, (block, 1), 0)
    line = lax.broadcasted_iota(jnp.int32, (1, block), 1)

    @pl.when(live)
    def _():
        loads[0].wait()
        total = jnp.zeros((block, block), F32)
        for e in range(1, dist):
            factor = jnp.exp((line - (dist - e) * block).astype(F32) * beta)
            total = total + qb_in[e - 1] * factor
        row_sum[...] = jnp.broadcast_to(jnp.sum(total, axis=1, keepdims=True), row_sum.shape)
        loads[2].wait()
        loads[3].wait()
        first = jnp.sum(jnp.where(rows_i == cols_i, code_own[...].astype(F32), 0.0), axis=1, keepdims=True)
        table = jnp.exp(-table_in[...])
        entries = table.shape[1]
        table = jnp.concatenate([table, jnp.zeros((1, 128 - entries), F32)], axis=1)
        table = jnp.broadcast_to(table, (block, 128))
        loads[1].wait()
        code_send().wait_recv()
        both = first + code_in[...].astype(F32)
        allowed = jnp.where(jnp.logical_or(both == 3.0, both == 5.0), 1.0, 0.0)
        for start in range(0, block, 128):
            part = pl.ds(start, 128)
            found = jnp.take_along_axis(table, e_in[:, part], axis=1, mode="promise_in_bounds")
            weight[:, part] = found * allowed[:, start : start + 128]
        loads[4].wait()

    for n, lists in enumerate(waiting):
        for source, keys in lists.items():

            @pl.when(me == source)
            def _():
                pl.semaphore_wait(held_sem.at[n], len(held[n][source]))
                for row, m, part in keys:
                    if part:
                        for p in range(relay[row, m][1]):
                            relay_copy(row, m, p).start()
                    else:
                        held_send(row, m)

    def column_sum(m, right, total):
        fade = jnp.exp((-(m + 1) * block - column).astype(F32) * beta)
        total[0:1, :] += jnp.sum(right * fade, axis=0, keepdims=True)

    def listed(shifts):
        return sum(m * base**i for i, m in enumerate(shifts))

    own_list = jnp.int32(listed(range(1, dm + 1)))
    for row in range(live_rows) if plan else ():
        shifts = [m for m in order.get(row, range(1, dm + 1)) if home(row, m) == row]
        own_list = jnp.where(me == row, listed(shifts), own_list)
    own_list = jnp.where(live, own_list, 0)

    def own_step(step, rest):
        m = rest % base - 1

        @pl.when(rest > 0)
        def _():
            r_copy(m + 1, 0).wait_recv()
            right = r_in[m]
            column_sum(m, right, acc)
            acc[HEAD:, :] += dot3(split(q_own[m]), split(right))

        return rest // base

    if plan:
        far_list = jnp.int32(0)
        for device, shifts in plan.values():
            far_list = far_list + jnp.where(me == device, listed(shifts), 0)
        for c in range(CHUNKS):
            at = rows_of(c)
            if c < CHUNKS - 1:
                for count in sorted({len(shifts) for _, shifts in plan.values()}):

                    @pl.when(any_of(me, [device for device, shifts in plan.values() if len(shifts) == count]))
                    def _():
                        whole = (pl.ds(0, count), at)
                        remote(qm.at[whole], q_far.at[whole], q_send.at[0], q_recv.at[c], 0).wait_recv()

            def far_step(step, rest):
                m = rest % base - 1

                @pl.when(rest > 0)
                def _():
                    if c == 0:
                        rf_copy(m + 1, 0).wait_recv()
                        right = r_far[m]
                        rf_h[m], rf_l[m] = split(right)
                        column_sum(m, right, acc_far)
                    if c == CHUNKS - 1:
                        here = (m, at)
                        slot = q_recv.at[CHUNKS - 1 + m]
                        remote(qm.at[here], q_far.at[here], q_send.at[0], slot, 0).wait_recv()
                    acc_far[rows_of(c, HEAD), :] += dot3(split(q_far[m, at, :]), (rf_h[m], rf_l[m]))

                return rest // base

            lax.fori_loop(0, dm, far_step, far_list)
            for row, (device, _) in plan.items():

                @pl.when(me == device)
                def _():
                    part_copy(c, row).start()

    lax.fori_loop(0, dm, own_step, own_list)

    if plan:

        @pl.when(any_of(me, list(plan)))
        def _():
            remote(acc_far, partial_in, part_sem.at[0], part_sem.at[1], 0).wait_recv()
            acc[...] += partial_in[...]

    sent = jnp.int32(0)
    for m in range(1, dist):
        sent = sent + jnp.where(near(me - m), 1, 0)
    for row, (device, shifts) in plan.items():
        if device - row in shifts:
            sent = sent - jnp.where(me == device, 1, 0)
    for count in range(1, dist):

        @pl.when(sent == count)
        def _():
            whole = pl.ds(0, count)
            remote(qm1.at[whole], r_in.at[whole], r_send.at[0], r_recv.at[0], 0).wait_send()

    for row, (device, shifts) in plan.items():

        @pl.when(me == row)
        def _():
            whole = pl.ds(0, len(shifts))
            remote(qm.at[whole], q_far.at[whole], q_send.at[0], q_recv.at[0], 0).wait_send()

    @pl.when(me >= dist)
    def _():
        code_send().wait_send()

    if plan:

        @pl.when(any_of(me, [device for device, _ in plan.values()]))
        def _():
            remote(acc_far, partial_in, part_sem.at[0], part_sem.at[1], 0).wait_send()

    for via in sorted({via for via, _, _ in relay.values()}):

        @pl.when(me == via)
        def _():
            whole = pl.ds(0, sum(1 for key in slots if relay[key[:2]][0] == via))
            remote(relay_in.at[whole], relay_in.at[whole], relay_send.at[0], r_recv.at[0], 0).wait_send()


def finish(live_rows, dist, acc, weight, row_sum, pair_out, branch_out, multi_out):
    block = weight.shape[0]
    beta = 1.0 / (dist * block)
    live = lax.axis_index("row") < live_rows

    @pl.when(live)
    def _():
        column = lax.broadcasted_iota(jnp.int32, (block, 1), 0).astype(F32)
        line = lax.broadcasted_iota(jnp.int32, (1, block), 1).astype(F32)
        rows_i = lax.broadcasted_iota(jnp.int32, (block, block), 0)
        cols_i = lax.broadcasted_iota(jnp.int32, (block, block), 1)
        upper = jnp.where(cols_i >= rows_i, 1.0, 0.0).astype(BF16)
        summed = acc[HEAD:, :]
        pair = weight[...] * (1.0 + 0.8 * summed)
        pair_out[...] = pair
        high, low = split(pair * jnp.exp(line * beta))
        inner = mm(high, upper) + mm(low, upper)
        branch = (row_sum[:, 0:1] + inner) * (beta * jnp.exp(line * (-beta)))
        branch_out[...] = branch
        high, low = split(branch * jnp.exp(column * (-beta)))
        tails = acc[0:1, :] + mm(upper, high) + mm(upper, low)
        multi_out[...] = summed + 0.01 * jnp.exp(column * beta) * tails

    @pl.when(jnp.logical_not(live))
    def _():
        for out in (pair_out, branch_out, multi_out):
            out[...] = jnp.zeros_like(out)


def solution(mesh):
    width = mesh.shape["row"]

    def per_device(qm, qm1, qb, codes, energy_index, turner):
        dm, block = qm.shape[2], qm.shape[3]
        dist = dm + 1
        known = width == 16 and dist == 8
        plan = PLAN if known else {}
        relay = RELAY if known else {}
        pieces = max([1] + [sum(n for v, n, _ in relay.values() if v == via) for via, _, _ in relay.values()])
        blocks = pltpu.VMEM((dm, block, block), F32)
        halves = pltpu.VMEM((dm, block, block), BF16)
        square = jax.ShapeDtypeStruct((block, block), F32)
        tall = pltpu.VMEM((block + HEAD, block), F32)
        dma = pltpu.SemaphoreType.DMA
        anywhere = pl.BlockSpec(memory_space=pltpu.HBM)
        local = pl.BlockSpec(memory_space=pltpu.VMEM)
        middle = pl.pallas_call(
            functools.partial(kernel, plan, relay, width),
            out_shape=[
                pltpu.VMEM((block + HEAD, block), F32),
                pltpu.VMEM((block, block), F32),
                pltpu.VMEM((block, 128), F32),
            ],
            in_specs=[anywhere] * 6,
            out_specs=[local] * 3,
            scratch_shapes=[
                blocks, blocks, blocks, blocks, halves, halves, blocks,
                pltpu.VMEM((block, block), jnp.int32),
                pltpu.VMEM((1, block), jnp.int32),
                tall, tall, pltpu.VMEM((pieces, block // PIECES, block), F32),
                pltpu.VMEM((1, block), jnp.int32),
                pltpu.VMEM((1, turner.shape[0]), F32),
                dma((1,)), dma((1,)), dma((CHUNKS - 1 + dm,)), dma((1,)), dma((dm,)), dma((dm,)),
                dma((4,)), dma((2,)), dma((2,)),
                pltpu.SemaphoreType.REGULAR((len(HELD),)),
            ],
            compiler_params=pltpu.CompilerParams(has_side_effects=True, collective_id=0),
        )(
            qm[0, 0], qm1[0, 0], qb[0, 0], energy_index[0, 0],
            codes[0], turner[None, :],
        )
        outs = pl.pallas_call(
            functools.partial(finish, width - dist, dist),
            out_shape=[square] * 3,
            in_specs=[local] * 3,
            out_specs=[local] * 3,
            compiler_params=pltpu.CompilerParams(vmem_limit_bytes=16 * 2**20),
        )(*middle)
        return tuple(out[None, None] for out in outs)

    return jax.shard_map(
        per_device,
        mesh=mesh,
        in_specs=(
            P("seq", "row", None, None, None),
            P("seq", "row", None, None, None),
            P("seq", "row", None, None, None),
            P("seq", "row", None),
            P("seq", "row", None, None),
            P(),
        ),
        out_specs=(
            P("seq", "row", None, None),
            P("seq", "row", None, None),
            P("seq", "row", None, None),
        ),
        check_vma=False,
    )
```

```python
import functools

import jax
import jax.numpy as jnp
from jax import lax
from jax.experimental import pallas as pl
from jax.experimental.pallas import tpu as pltpu
from jax.sharding import PartitionSpec as P

F32 = jnp.float32
BF16 = jnp.bfloat16

PLAN = {
    1: (5, (4, 3, 6, 5, 7)),
    3: (6, (3, 1, 2, 7, 6, 5)),
    4: (8, (7, 6)),
    5: (9, (4, 3, 6, 5, 7)),
    7: (11, (4, 3, 7, 1, 2, 5, 6)),
}
RELAY = {
    (6, 7): (15, 4, 0),
    (6, 6): (14, 4, 0),
    (2, 6): (10, 4, 0),
    (6, 2): (10, 2, 4),
    (6, 3): (10, 4, 0),
    (7, 5): (14, 4, 1),
    (7, 6): (15, 4, 1),
}
HELD = (
    {4: (6,), 5: (6,), 8: (10, 11), 9: (10, 11)},
    {4: (2,), 5: (2,), 8: (2, 6), 9: (2, 6)},
)
DEFER = {8: ((4, 4),)}
ORDER = {6: (1, 7, 6, 5, 4, 3, 2)}
SHARES = (4, 2, 1, 1)
CHUNKS = len(SHARES)
PIECES = 4
HEAD = 8


def split(x):
    high = x.astype(BF16)
    return high, (x - high.astype(F32)).astype(BF16)


def mm(a, b):
    return jnp.dot(a, b, preferred_element_type=F32)


def dot3(a, b):
    ah, al = a
    bh, bl = b
    return mm(ah, bh) + (mm(ah, bl) + mm(al, bh))


def any_of(x, values):
    hit = x == values[0]
    for value in values[1:]:
        hit = jnp.logical_or(hit, x == value)
    return hit


def kernel(
    plan, relay, width, qm, qm1, qb, eidx, codes, turner, acc, weight, row_sum,
    q_own, r_in, r_far, q_far, rf_h, rf_l, qb_in, e_in, code_in, acc_far, partial_in, relay_in, code_own, table_in,
    own_sem, q_send, q_recv, r_send, r_recv, rf_recv, load_sem, code_sem, part_sem, held_sem,
):
    dm, block = qm.shape[0], qm.shape[1]
    dist = dm + 1
    live_rows = width - dist
    beta = 1.0 / (dist * block)
    base = dm + 1
    me = lax.axis_index("row")
    live = me < live_rows
    relay_send, relay_recv = q_send, q_recv
    unit = block // sum(SHARES)
    piece = block // PIECES

    def remote(src, dst, send, recv, device):
        return pltpu.make_async_remote_copy(
            src_ref=src, dst_ref=dst, send_sem=send, recv_sem=recv,
            device_id={"row": device}, device_id_type=pl.DeviceIdType.MESH,
        )

    def near(row):
        return jnp.logical_and(row >= 0, row < live_rows)

    def home(row, m):
        device, shifts = plan.get(row, (None, ()))
        return device if m in shifts else row

    held = HELD if plan else ()
    order = ORDER if plan else {}
    defer = DEFER if plan else {}
    waiting = []
    for group in held:
        lists = {source: [] for source in group}
        for source in group:
            for row in range(min(live_rows, source) - 1, max(source - dist, -1), -1):
                m = source - row
                via, count, _ = relay.get((row, m), (None, 0, 0))
                if home(row, m) in group[source] and count < PIECES:
                    lists[source].append((row, m, False))
                if via in group[source]:
                    lists[source].append((row, m, True))
            lists[source].sort(key=lambda item: (item[2], item[0] not in (3, 7), -item[0]))
        waiting.append(lists)
    for source, keys in defer.items():
        waiting[-1][source] += [(row, m, False) for row, m in keys]
    rests = {(row, m) for lists in waiting for keys in lists.values() for row, m, part in keys if not part}
    parts = {(row, m) for lists in waiting for keys in lists.values() for row, m, part in keys if part}

    def apart(m):
        if not plan:
            return []
        return [
            row for row in range(live_rows)
            if (row, m) in relay or (row, m) in rests or home(row, m) != row
        ]

    def held_send(row, m):
        if (row, m) in relay:
            relay_rest(row, m).start()
        else:
            (r_copy if home(row, m) == row else rf_copy)(m, home(row, m)).start()

    def direct(m):
        row = me - m
        ok = near(row)
        rows = apart(m)
        return jnp.logical_and(ok, jnp.logical_not(any_of(row, rows))) if rows else ok

    def code_send():
        return remote(codes, code_in, code_sem.at[0], code_sem.at[1], me - dist)

    def rows_of(c, shift=0):
        return pl.ds(sum(SHARES[:c]) * unit + shift, SHARES[c] * unit)

    def q_copy(m, c, device):
        at = (m - 1, rows_of(c))
        slot = c if c < CHUNKS - 1 else CHUNKS - 2 + m
        return remote(qm.at[at], q_far.at[at], q_send.at[0], q_recv.at[slot], device)

    def r_copy(m, device):
        return remote(qm1.at[dm - m], r_in.at[m - 1], r_send.at[0], r_recv.at[m - 1], device)

    def rf_copy(m, device):
        return remote(qm1.at[dm - m], r_far.at[m - 1], r_send.at[0], rf_recv.at[m - 1], device)

    def right_at(row, m):
        return (r_in, r_recv) if home(row, m) == row else (r_far, rf_recv)

    turns = sorted((rank + p, row, m, p) for (row, m), (_, count, rank) in relay.items() for p in range(count))
    slots = {}
    for _, row, m, p in turns:
        slots[row, m, p] = sum(1 for key in slots if relay[key[:2]][0] == relay[row, m][0])

    def relay_copy(row, m, p):
        slot = slots[row, m, p]
        return remote(
            qm1.at[dm - m, pl.ds(p * piece, piece)], relay_in.at[slot],
            r_send.at[0], relay_recv.at[slot], relay[row, m][0],
        )

    def relay_on(row, m, p):
        at = pl.ds(p * piece, piece)
        into, sem = right_at(row, m)
        return remote(
            relay_in.at[slots[row, m, p]], into.at[m - 1, at], relay_send.at[0], sem.at[m - 1], home(row, m)
        )

    def relay_rest(row, m):
        start = relay[row, m][1] * piece
        at = pl.ds(start, block - start)
        into, sem = right_at(row, m)
        return remote(qm1.at[dm - m, at], into.at[m - 1, at], r_send.at[0], sem.at[m - 1], home(row, m))

    def send_held(n):
        for source, keys in waiting[n].items():

            @pl.when(me == source)
            def _():
                pl.semaphore_wait(held_sem.at[n], len(held[n][source]))
                for row, m, part in keys:
                    if part:
                        for p in range(relay[row, m][1]):
                            relay_copy(row, m, p).start()
                    else:
                        held_send(row, m)

    def part_copy(c, device):
        start = HEAD + sum(SHARES[:c]) * unit if c else 0
        at = pl.ds(start, HEAD + sum(SHARES[: c + 1]) * unit - start)
        return remote(acc_far.at[at], partial_in.at[at], part_sem.at[0], part_sem.at[1], device)

    barrier = pltpu.get_barrier_semaphore()

    def greet(device):
        pl.semaphore_signal(
            barrier, inc=1, device_id={"row": device}, device_id_type=pl.DeviceIdType.MESH
        )

    if plan:
        pairs = {(device, device - dist) for device in range(dist, width)}
        for row in range(live_rows):
            for m in range(1, dist):
                source, device = row + m, home(row, m)
                via, count, _ = relay.get((row, m), (None, 0, 0))
                if count:
                    pairs |= {(source, via), (via, device)}
                if count < PIECES:
                    pairs.add((source, device))
        for row, (device, _) in plan.items():
            pairs |= {(row, device), (device, row)}
        for group in held:
            for source, devices in group.items():
                pairs -= {(source, device) for device in devices}
                pairs |= {(device, source) for device in devices}
        pairs = sorted((s, d) for s, d in pairs if s != d)
        awaited = jnp.int32(0)
        for device in range(width):
            sources = [s for s, d in pairs if d == device]
            awaited = awaited + jnp.where(me == device, sum(1 for s, _ in pairs if s == device), 0)
            if sources:

                @pl.when(me == device)
                def _():
                    for source in sources:
                        greet(source)

    else:

        @pl.when(live)
        def _():
            for m in range(1, dist + 1):
                greet(me + m)

        awaited = jnp.int32(0)
        for m in range(1, dist + 1):
            awaited = awaited + jnp.where(near(me - m), 1, 0)

    @pl.when(awaited > 0)
    def _():
        pl.semaphore_wait(barrier, awaited)

    for n, group in enumerate(held):
        for device in sorted({device for devices in group.values() for device in devices}):

            @pl.when(me == device)
            def _():
                for source in [source for source, devices in group.items() if device in devices]:
                    pl.semaphore_signal(
                        held_sem.at[n], inc=1, device_id={"row": source}, device_id_type=pl.DeviceIdType.MESH
                    )

    @pl.when(me >= dist)
    def _():
        code_send().start()

    for m in range(dm, 0, -1):
        for row, (device, shifts) in plan.items():
            if m not in shifts or (row, m) in relay or (row, m) in rests:
                continue

            @pl.when(me == row + m)
            def _():
                if row + m == device:
                    pltpu.make_async_copy(qm1.at[dm - m], r_far.at[m - 1], rf_recv.at[m - 1]).start()
                else:
                    rf_copy(m, device).start()

    for row, (device, shifts) in plan.items():

        @pl.when(me == row)
        def _():
            for c in range(CHUNKS):
                for m in shifts:
                    q_copy(m, c, device).start()

    for source in sorted({row + m for row, m in relay}):

        @pl.when(me == source)
        def _():
            for row, m, p in slots:
                if row + m == source and (row, m) not in parts:
                    relay_copy(row, m, p).start()
            for (row, m), (_, count, _) in relay.items():
                if row + m == source and count < PIECES and (row, m) not in rests:
                    relay_rest(row, m).start()

    for m in range(dm, 0, -1):

        @pl.when(direct(m))
        def _():
            r_copy(m, me - m).start()

    loads = (
        pltpu.make_async_copy(qb, qb_in, load_sem.at[0]),
        pltpu.make_async_copy(eidx, e_in, load_sem.at[1]),
        pltpu.make_async_copy(codes, code_own, load_sem.at[2]),
        pltpu.make_async_copy(turner, table_in, load_sem.at[3]),
        pltpu.make_async_copy(qm, q_own, own_sem.at[0]),
    )

    @pl.when(live)
    def _():
        for load in loads:
            load.start()

    if held:
        send_held(0)

    for via in sorted({via for via, _, _ in relay.values()}):

        @pl.when(me == via)
        def _():
            for row, m, p in slots:
                if relay[row, m][0] == via:
                    relay_copy(row, m, p).wait_recv()
                    relay_on(row, m, p).start()

    acc[...] = jnp.zeros_like(acc)
    acc_far[...] = jnp.zeros_like(acc_far)
    rows_i = lax.broadcasted_iota(jnp.int32, (block, block), 0)
    cols_i = lax.broadcasted_iota(jnp.int32, (block, block), 1)
    column = lax.broadcasted_iota(jnp.int32, (block, 1), 0)
    line = lax.broadcasted_iota(jnp.int32, (1, block), 1)

    @pl.when(live)
    def _():
        loads[0].wait()
        total = jnp.zeros((block, block), F32)
        for e in range(1, dist):
            factor = jnp.exp((line - (dist - e) * block).astype(F32) * beta)
            total = total + qb_in[e - 1] * factor
        row_sum[...] = jnp.broadcast_to(jnp.sum(total, axis=1, keepdims=True), row_sum.shape)
        loads[2].wait()
        loads[3].wait()
        first = jnp.sum(jnp.where(rows_i == cols_i, code_own[...].astype(F32), 0.0), axis=1, keepdims=True)
        table = jnp.exp(-table_in[...])
        entries = table.shape[1]
        table = jnp.concatenate([table, jnp.zeros((1, 128 - entries), F32)], axis=1)
        table = jnp.broadcast_to(table, (block, 128))
        loads[1].wait()
        code_send().wait_recv()
        both = first + code_in[...].astype(F32)
        allowed = jnp.where(jnp.logical_or(both == 3.0, both == 5.0), 1.0, 0.0)
        for start in range(0, block, 128):
            part = pl.ds(start, 128)
            found = jnp.take_along_axis(table, e_in[:, part], axis=1, mode="promise_in_bounds")
            weight[:, part] = found * allowed[:, start : start + 128]
        loads[4].wait()

    for n in range(1, len(held)):
        send_held(n)

    def column_sum(m, right, total):
        fade = jnp.exp((-(m + 1) * block - column).astype(F32) * beta)
        total[0:1, :] += jnp.sum(right * fade, axis=0, keepdims=True)

    def listed(shifts):
        return sum(m * base**i for i, m in enumerate(shifts))

    own_list = jnp.int32(listed(range(1, dm + 1)))
    for row in range(live_rows) if plan else ():
        shifts = [m for m in order.get(row, range(1, dm + 1)) if home(row, m) == row]
        own_list = jnp.where(me == row, listed(shifts), own_list)
    own_list = jnp.where(live, own_list, 0)

    def own_step(step, rest):
        m = rest % base - 1

        @pl.when(rest > 0)
        def _():
            r_copy(m + 1, 0).wait_recv()
            right = r_in[m]
            column_sum(m, right, acc)
            acc[HEAD:, :] += dot3(split(q_own[m]), split(right))

        return rest // base

    if plan:
        far_list = jnp.int32(0)
        for device, shifts in plan.values():
            far_list = far_list + jnp.where(me == device, listed(shifts), 0)
        for c in range(CHUNKS):
            at = rows_of(c)
            if c < CHUNKS - 1:
                for count in sorted({len(shifts) for _, shifts in plan.values()}):

                    @pl.when(any_of(me, [device for device, shifts in plan.values() if len(shifts) == count]))
                    def _():
                        whole = (pl.ds(0, count), at)
                        remote(qm.at[whole], q_far.at[whole], q_send.at[0], q_recv.at[c], 0).wait_recv()

            def far_step(step, rest):
                m = rest % base - 1

                @pl.when(rest > 0)
                def _():
                    if c == 0:
                        rf_copy(m + 1, 0).wait_recv()
                        right = r_far[m]
                        rf_h[m], rf_l[m] = split(right)
                        column_sum(m, right, acc_far)
                    if c == CHUNKS - 1:
                        here = (m, at)
                        slot = q_recv.at[CHUNKS - 1 + m]
                        remote(qm.at[here], q_far.at[here], q_send.at[0], slot, 0).wait_recv()
                    acc_far[rows_of(c, HEAD), :] += dot3(split(q_far[m, at, :]), (rf_h[m], rf_l[m]))

                return rest // base

            lax.fori_loop(0, dm, far_step, far_list)
            for row, (device, _) in plan.items():

                @pl.when(me == device)
                def _():
                    part_copy(c, row).start()

    lax.fori_loop(0, dm, own_step, own_list)

    if plan:

        @pl.when(any_of(me, list(plan)))
        def _():
            remote(acc_far, partial_in, part_sem.at[0], part_sem.at[1], 0).wait_recv()
            acc[...] += partial_in[...]

    sent = jnp.int32(0)
    for m in range(1, dist):
        sent = sent + jnp.where(near(me - m), 1, 0)
    for row, (device, shifts) in plan.items():
        if device - row in shifts:
            sent = sent - jnp.where(me == device, 1, 0)
    for count in range(1, dist):

        @pl.when(sent == count)
        def _():
            whole = pl.ds(0, count)
            remote(qm1.at[whole], r_in.at[whole], r_send.at[0], r_recv.at[0], 0).wait_send()

    for row, (device, shifts) in plan.items():

        @pl.when(me == row)
        def _():
            whole = pl.ds(0, len(shifts))
            remote(qm.at[whole], q_far.at[whole], q_send.at[0], q_recv.at[0], 0).wait_send()

    @pl.when(me >= dist)
    def _():
        code_send().wait_send()

    if plan:

        @pl.when(any_of(me, [device for device, _ in plan.values()]))
        def _():
            remote(acc_far, partial_in, part_sem.at[0], part_sem.at[1], 0).wait_send()

    for via in sorted({via for via, _, _ in relay.values()}):

        @pl.when(me == via)
        def _():
            whole = pl.ds(0, sum(1 for key in slots if relay[key[:2]][0] == via))
            remote(relay_in.at[whole], relay_in.at[whole], relay_send.at[0], r_recv.at[0], 0).wait_send()


def finish(live_rows, dist, acc, weight, row_sum, pair_out, branch_out, multi_out):
    block = weight.shape[0]
    beta = 1.0 / (dist * block)
    live = lax.axis_index("row") < live_rows

    @pl.when(live)
    def _():
        column = lax.broadcasted_iota(jnp.int32, (block, 1), 0).astype(F32)
        line = lax.broadcasted_iota(jnp.int32, (1, block), 1).astype(F32)
        rows_i = lax.broadcasted_iota(jnp.int32, (block, block), 0)
        cols_i = lax.broadcasted_iota(jnp.int32, (block, block), 1)
        upper = jnp.where(cols_i >= rows_i, 1.0, 0.0).astype(BF16)
        summed = acc[HEAD:, :]
        pair = weight[...] * (1.0 + 0.8 * summed)
        pair_out[...] = pair
        high, low = split(pair * jnp.exp(line * beta))
        inner = mm(high, upper) + mm(low, upper)
        branch = (row_sum[:, 0:1] + inner) * (beta * jnp.exp(line * (-beta)))
        branch_out[...] = branch
        high, low = split(branch * jnp.exp(column * (-beta)))
        tails = acc[0:1, :] + mm(upper, high) + mm(upper, low)
        multi_out[...] = summed + 0.01 * jnp.exp(column * beta) * tails

    @pl.when(jnp.logical_not(live))
    def _():
        for out in (pair_out, branch_out, multi_out):
            out[...] = jnp.zeros_like(out)


def solution(mesh):
    width = mesh.shape["row"]

    def per_device(qm, qm1, qb, codes, energy_index, turner):
        dm, block = qm.shape[2], qm.shape[3]
        dist = dm + 1
        known = width == 16 and dist == 8
        plan = PLAN if known else {}
        relay = RELAY if known else {}
        pieces = max([1] + [sum(n for v, n, _ in relay.values() if v == via) for via, _, _ in relay.values()])
        blocks = pltpu.VMEM((dm, block, block), F32)
        halves = pltpu.VMEM((dm, block, block), BF16)
        square = jax.ShapeDtypeStruct((block, block), F32)
        tall = pltpu.VMEM((block + HEAD, block), F32)
        dma = pltpu.SemaphoreType.DMA
        anywhere = pl.BlockSpec(memory_space=pltpu.HBM)
        local = pl.BlockSpec(memory_space=pltpu.VMEM)
        middle = pl.pallas_call(
            functools.partial(kernel, plan, relay, width),
            out_shape=[
                pltpu.VMEM((block + HEAD, block), F32),
                pltpu.VMEM((block, block), F32),
                pltpu.VMEM((block, 128), F32),
            ],
            in_specs=[anywhere] * 6,
            out_specs=[local] * 3,
            scratch_shapes=[
                blocks, blocks, blocks, blocks, halves, halves, blocks,
                pltpu.VMEM((block, block), jnp.int32),
                pltpu.VMEM((1, block), jnp.int32),
                tall, tall, pltpu.VMEM((pieces, block // PIECES, block), F32),
                pltpu.VMEM((1, block), jnp.int32),
                pltpu.VMEM((1, turner.shape[0]), F32),
                dma((1,)), dma((1,)), dma((CHUNKS - 1 + dm,)), dma((1,)), dma((dm,)), dma((dm,)),
                dma((4,)), dma((2,)), dma((2,)),
                pltpu.SemaphoreType.REGULAR((len(HELD),)),
            ],
            compiler_params=pltpu.CompilerParams(has_side_effects=True, collective_id=0),
        )(
            qm[0, 0], qm1[0, 0], qb[0, 0], energy_index[0, 0],
            codes[0], turner[None, :],
        )
        outs = pl.pallas_call(
            functools.partial(finish, width - dist, dist),
            out_shape=[square] * 3,
            in_specs=[local] * 3,
            out_specs=[local] * 3,
            compiler_params=pltpu.CompilerParams(vmem_limit_bytes=16 * 2**20),
        )(*middle)
        return tuple(out[None, None] for out in outs)

    return jax.shard_map(
        per_device,
        mesh=mesh,
        in_specs=(
            P("seq", "row", None, None, None),
            P("seq", "row", None, None, None),
            P("seq", "row", None, None, None),
            P("seq", "row", None),
            P("seq", "row", None, None),
            P(),
        ),
        out_specs=(
            P("seq", "row", None, None),
            P("seq", "row", None, None),
            P("seq", "row", None, None),
        ),
        check_vma=False,
    )
```

```python
import functools

import jax
import jax.numpy as jnp
from jax import lax
from jax.experimental import pallas as pl
from jax.experimental.pallas import tpu as pltpu
from jax.sharding import PartitionSpec as P

F32 = jnp.float32
BF16 = jnp.bfloat16

PLAN = {
    1: (5, (4, 3, 6, 5, 7)),
    3: (6, (3, 1, 2, 7, 6, 5)),
    4: (8, (4, 5, 7, 6)),
    5: (9, (3, 6, 5, 7)),
    7: (11, (4, 3, 7, 1, 2, 5, 6)),
}
RELAY = {
    (6, 7): (15, 4, 0),
    (6, 6): (14, 4, 0),
    (2, 6): (10, 4, 0),
    (6, 2): (10, 1, 4),
    (6, 3): (10, 4, 0),
    (7, 5): (14, 4, 1),
    (7, 6): (15, 4, 1),
}
HELD = (
    {4: (6,), 5: (6,), 8: (10, 11), 9: (10, 11)},
    {4: (2,), 5: (2,), 8: (2, 6), 9: (2, 6)},
)
SPLIT = ((5, 3),)
ORDER = {6: (1, 7, 6, 5, 4, 3, 2)}
SHARES = (4, 2, 1, 1)
CHUNKS = len(SHARES)
PIECES = 4
HEAD = 8


def split(x):
    high = x.astype(BF16)
    return high, (x - high.astype(F32)).astype(BF16)


def mm(a, b):
    return jnp.dot(a, b, preferred_element_type=F32)


def dot3(a, b):
    ah, al = a
    bh, bl = b
    return mm(ah, bh) + (mm(ah, bl) + mm(al, bh))


def any_of(x, values):
    hit = x == values[0]
    for value in values[1:]:
        hit = jnp.logical_or(hit, x == value)
    return hit


def kernel(
    plan, relay, width, qm, qm1, qb, eidx, codes, turner, acc, weight, row_sum,
    q_own, r_in, r_far, q_far, rf_h, rf_l, qb_in, e_in, code_in, acc_far, partial_in, relay_in, code_own, table_in,
    own_sem, q_send, q_recv, r_send, r_recv, rf_recv, load_sem, code_sem, part_sem, held_sem, half_sem,
):
    dm, block = qm.shape[0], qm.shape[1]
    dist = dm + 1
    live_rows = width - dist
    beta = 1.0 / (dist * block)
    base = dm + 1
    me = lax.axis_index("row")
    live = me < live_rows
    relay_send, relay_recv = q_send, q_recv
    unit = block // sum(SHARES)
    piece = block // PIECES

    def remote(src, dst, send, recv, device):
        return pltpu.make_async_remote_copy(
            src_ref=src, dst_ref=dst, send_sem=send, recv_sem=recv,
            device_id={"row": device}, device_id_type=pl.DeviceIdType.MESH,
        )

    def near(row):
        return jnp.logical_and(row >= 0, row < live_rows)

    def home(row, m):
        device, shifts = plan.get(row, (None, ()))
        return device if m in shifts else row

    held = HELD if plan else ()
    order = ORDER if plan else {}
    halved = SPLIT if plan else ()
    half = block // 2
    waiting = []
    for group in held:
        lists = {source: [] for source in group}
        for source in group:
            for row in range(min(live_rows, source) - 1, max(source - dist, -1), -1):
                m = source - row
                via, count, _ = relay.get((row, m), (None, 0, 0))
                if home(row, m) in group[source] and count < PIECES:
                    lists[source].append((row, m, "rest"))
                if via in group[source]:
                    lists[source].append((row, m, "relay"))
            lists[source].sort(key=lambda item: (item[2] == "relay", item[0] not in (3, 7), -item[0]))
        waiting.append(lists)
    for row, m in halved:
        waiting[-1][row + m].insert(1, (row, m, "half"))
    kinds = [item for lists in waiting for keys in lists.values() for item in keys]
    rests = {(row, m) for row, m, kind in kinds if kind == "rest"}
    parts = {(row, m) for row, m, kind in kinds if kind == "relay"}

    def apart(m):
        if not plan:
            return []
        return [
            row for row in range(live_rows)
            if (row, m) in relay or (row, m) in rests or home(row, m) != row
        ]

    def held_send(row, m):
        if (row, m) in relay:
            relay_rest(row, m).start()
        else:
            (r_copy if home(row, m) == row else rf_copy)(m, home(row, m)).start()

    def direct(m):
        row = me - m
        ok = near(row)
        rows = apart(m)
        return jnp.logical_and(ok, jnp.logical_not(any_of(row, rows))) if rows else ok

    def code_send():
        return remote(codes, code_in, code_sem.at[0], code_sem.at[1], me - dist)

    def rows_of(c, shift=0):
        return pl.ds(sum(SHARES[:c]) * unit + shift, SHARES[c] * unit)

    def q_copy(row, m, c, device):
        at = (m - 1, rows_of(c), pl.ds(0, half if (row, m) in halved else block))
        slot = c if c < CHUNKS - 1 else CHUNKS - 2 + m
        return remote(qm.at[at], q_far.at[at], q_send.at[0], q_recv.at[slot], device)

    def r_copy(m, device):
        return remote(qm1.at[dm - m], r_in.at[m - 1], r_send.at[0], r_recv.at[m - 1], device)

    def rf_copy(m, device):
        return remote(qm1.at[dm - m], r_far.at[m - 1], r_send.at[0], rf_recv.at[m - 1], device)

    def half_copy(m, device):
        at = pl.ds(half, block - half)
        return remote(qm1.at[dm - m, at], r_in.at[m - 1, at], half_sem.at[0], r_recv.at[m - 1], device)

    def units(row):
        shifts = plan[row][1]
        return 2 * len(shifts) - sum(1 for m in shifts if (row, m) in halved)

    def q_units(count, rows):
        if count % 2 == 0:
            at = (pl.ds(0, count // 2), rows)
        else:
            at = (pl.ds(0, count), rows, pl.ds(0, half))
        return at

    def right_at(row, m):
        return (r_in, r_recv) if home(row, m) == row else (r_far, rf_recv)

    turns = sorted((rank + p, row, m, p) for (row, m), (_, count, rank) in relay.items() for p in range(count))
    slots = {}
    for _, row, m, p in turns:
        slots[row, m, p] = sum(1 for key in slots if relay[key[:2]][0] == relay[row, m][0])

    def relay_copy(row, m, p):
        slot = slots[row, m, p]
        return remote(
            qm1.at[dm - m, pl.ds(p * piece, piece)], relay_in.at[slot],
            r_send.at[0], relay_recv.at[slot], relay[row, m][0],
        )

    def relay_on(row, m, p):
        at = pl.ds(p * piece, piece)
        into, sem = right_at(row, m)
        return remote(
            relay_in.at[slots[row, m, p]], into.at[m - 1, at], relay_send.at[0], sem.at[m - 1], home(row, m)
        )

    def relay_rest(row, m):
        start = relay[row, m][1] * piece
        at = pl.ds(start, block - start)
        into, sem = right_at(row, m)
        return remote(qm1.at[dm - m, at], into.at[m - 1, at], r_send.at[0], sem.at[m - 1], home(row, m))

    def send_held(n):
        for source, keys in waiting[n].items():

            @pl.when(me == source)
            def _():
                pl.semaphore_wait(held_sem.at[n], len(held[n][source]))
                for row, m, kind in keys:
                    if kind == "relay":
                        for p in range(relay[row, m][1]):
                            relay_copy(row, m, p).start()
                    elif kind == "half":
                        half_copy(m, row).start()
                    else:
                        held_send(row, m)

    def part_copy(c, device):
        start = HEAD + sum(SHARES[:c]) * unit if c else 0
        at = pl.ds(start, HEAD + sum(SHARES[: c + 1]) * unit - start)
        return remote(acc_far.at[at], partial_in.at[at], part_sem.at[0], part_sem.at[1], device)

    barrier = pltpu.get_barrier_semaphore()

    def greet(device):
        pl.semaphore_signal(
            barrier, inc=1, device_id={"row": device}, device_id_type=pl.DeviceIdType.MESH
        )

    if plan:
        pairs = {(device, device - dist) for device in range(dist, width)}
        for row in range(live_rows):
            for m in range(1, dist):
                source, device = row + m, home(row, m)
                via, count, _ = relay.get((row, m), (None, 0, 0))
                if count:
                    pairs |= {(source, via), (via, device)}
                if count < PIECES:
                    pairs.add((source, device))
                if (row, m) in halved:
                    pairs.add((source, row))
        for row, (device, _) in plan.items():
            pairs |= {(row, device), (device, row)}
        for group in held:
            for source, devices in group.items():
                pairs -= {(source, device) for device in devices}
                pairs |= {(device, source) for device in devices}
        pairs = sorted((s, d) for s, d in pairs if s != d)
        awaited = jnp.int32(0)
        for device in range(width):
            sources = [s for s, d in pairs if d == device]
            awaited = awaited + jnp.where(me == device, sum(1 for s, _ in pairs if s == device), 0)
            if sources:

                @pl.when(me == device)
                def _():
                    for source in sources:
                        greet(source)

    else:

        @pl.when(live)
        def _():
            for m in range(1, dist + 1):
                greet(me + m)

        awaited = jnp.int32(0)
        for m in range(1, dist + 1):
            awaited = awaited + jnp.where(near(me - m), 1, 0)

    @pl.when(awaited > 0)
    def _():
        pl.semaphore_wait(barrier, awaited)

    for n, group in enumerate(held):
        for device in sorted({device for devices in group.values() for device in devices}):

            @pl.when(me == device)
            def _():
                for source in [source for source, devices in group.items() if device in devices]:
                    pl.semaphore_signal(
                        held_sem.at[n], inc=1, device_id={"row": source}, device_id_type=pl.DeviceIdType.MESH
                    )

    @pl.when(me >= dist)
    def _():
        code_send().start()

    for m in range(dm, 0, -1):
        for row, (device, shifts) in plan.items():
            if m not in shifts or (row, m) in relay or (row, m) in rests:
                continue

            @pl.when(me == row + m)
            def _():
                if row + m == device:
                    pltpu.make_async_copy(qm1.at[dm - m], r_far.at[m - 1], rf_recv.at[m - 1]).start()
                else:
                    rf_copy(m, device).start()

    for row, (device, shifts) in plan.items():

        @pl.when(me == row)
        def _():
            for c in range(CHUNKS):
                for m in shifts:
                    q_copy(row, m, c, device).start()

    for source in sorted({row + m for row, m in relay}):

        @pl.when(me == source)
        def _():
            for row, m, p in slots:
                if row + m == source and (row, m) not in parts:
                    relay_copy(row, m, p).start()
            for (row, m), (_, count, _) in relay.items():
                if row + m == source and count < PIECES and (row, m) not in rests:
                    relay_rest(row, m).start()

    for m in range(dm, 0, -1):

        @pl.when(direct(m))
        def _():
            r_copy(m, me - m).start()

    loads = (
        pltpu.make_async_copy(qb, qb_in, load_sem.at[0]),
        pltpu.make_async_copy(eidx, e_in, load_sem.at[1]),
        pltpu.make_async_copy(codes, code_own, load_sem.at[2]),
        pltpu.make_async_copy(turner, table_in, load_sem.at[3]),
        pltpu.make_async_copy(qm, q_own, own_sem.at[0]),
    )

    @pl.when(live)
    def _():
        for load in loads:
            load.start()

    if held:
        send_held(0)

    for via in sorted({via for via, _, _ in relay.values()}):

        @pl.when(me == via)
        def _():
            for row, m, p in slots:
                if relay[row, m][0] == via:
                    relay_copy(row, m, p).wait_recv()
                    relay_on(row, m, p).start()

    acc[...] = jnp.zeros_like(acc)
    acc_far[...] = jnp.zeros_like(acc_far)
    for row, m in halved:

        @pl.when(me == plan[row][0])
        def _():
            q_far[m - 1, :, half:] = jnp.zeros((block, block - half), F32)

        @pl.when(me == row)
        def _():
            r_in[m - 1, 0:half, :] = jnp.zeros((half, block), F32)

    @pl.when(jnp.logical_not(live))
    def _():
        weight[...] = jnp.zeros_like(weight)
        row_sum[...] = jnp.zeros_like(row_sum)

    rows_i = lax.broadcasted_iota(jnp.int32, (block, block), 0)
    cols_i = lax.broadcasted_iota(jnp.int32, (block, block), 1)
    column = lax.broadcasted_iota(jnp.int32, (block, 1), 0)
    line = lax.broadcasted_iota(jnp.int32, (1, block), 1)

    @pl.when(live)
    def _():
        loads[0].wait()
        total = jnp.zeros((block, block), F32)
        for e in range(1, dist):
            factor = jnp.exp((line - (dist - e) * block).astype(F32) * beta)
            total = total + qb_in[e - 1] * factor
        row_sum[...] = jnp.broadcast_to(jnp.sum(total, axis=1, keepdims=True), row_sum.shape)
        loads[2].wait()
        loads[3].wait()
        first = jnp.sum(jnp.where(rows_i == cols_i, code_own[...].astype(F32), 0.0), axis=1, keepdims=True)
        table = jnp.exp(-table_in[...])
        entries = table.shape[1]
        table = jnp.concatenate([table, jnp.zeros((1, 128 - entries), F32)], axis=1)
        table = jnp.broadcast_to(table, (block, 128))
        loads[1].wait()
        code_send().wait_recv()
        both = first + code_in[...].astype(F32)
        allowed = jnp.where(jnp.logical_or(both == 3.0, both == 5.0), 1.0, 0.0)
        for start in range(0, block, 128):
            part = pl.ds(start, 128)
            found = jnp.take_along_axis(table, e_in[:, part], axis=1, mode="promise_in_bounds")
            weight[:, part] = found * allowed[:, start : start + 128]
        loads[4].wait()

    for n in range(1, len(held)):
        send_held(n)

    def column_sum(m, right, total):
        fade = jnp.exp((-(m + 1) * block - column).astype(F32) * beta)
        total[0:1, :] += jnp.sum(right * fade, axis=0, keepdims=True)

    def is_half(m, place):
        hit = jnp.bool_(False)
        for row, shift in halved:
            hit = jnp.logical_or(hit, jnp.logical_and(me == place(row, shift), m == shift - 1))
        return hit

    def listed(shifts):
        return sum(m * base**i for i, m in enumerate(shifts))

    own_list = jnp.int32(listed(range(1, dm + 1)))
    for row in range(live_rows) if plan else ():
        shifts = [m for m in order.get(row, range(1, dm + 1)) if home(row, m) == row or (row, m) in halved]
        own_list = jnp.where(me == row, listed(shifts), own_list)
    own_list = jnp.where(live, own_list, 0)

    def own_step(step, rest):
        m = rest % base - 1

        @pl.when(rest > 0)
        def _():
            small = is_half(m, lambda row, _: row)

            @pl.when(small)
            def _():
                half_copy(m + 1, 0).wait_recv()

            @pl.when(jnp.logical_not(small))
            def _():
                r_copy(m + 1, 0).wait_recv()
                column_sum(m, r_in[m], acc)

            right = r_in[m]
            acc[HEAD:, :] += dot3(split(q_own[m]), split(right))

        return rest // base

    if plan:
        far_list = jnp.int32(0)
        for device, shifts in plan.values():
            far_list = far_list + jnp.where(me == device, listed(shifts), 0)
        for c in range(CHUNKS):
            at = rows_of(c)
            if c < CHUNKS - 1:
                for count in sorted({units(row) for row in plan}):

                    @pl.when(any_of(me, [plan[row][0] for row in plan if units(row) == count]))
                    def _():
                        whole = q_units(count, at)
                        remote(qm.at[whole], q_far.at[whole], q_send.at[0], q_recv.at[c], 0).wait_recv()

            def far_step(step, rest):
                m = rest % base - 1

                @pl.when(rest > 0)
                def _():
                    if c == 0:
                        rf_copy(m + 1, 0).wait_recv()
                        right = r_far[m]
                        rf_h[m], rf_l[m] = split(right)
                        column_sum(m, right, acc_far)
                    if c == CHUNKS - 1:
                        slot = q_recv.at[CHUNKS - 1 + m]

                        def wait_for(lanes):
                            here = (m, at, pl.ds(0, lanes))
                            remote(qm.at[here], q_far.at[here], q_send.at[0], slot, 0).wait_recv()

                        small = is_half(m, lambda row, _: plan[row][0])

                        @pl.when(small)
                        def _():
                            wait_for(half)

                        @pl.when(jnp.logical_not(small))
                        def _():
                            wait_for(block)
                    acc_far[rows_of(c, HEAD), :] += dot3(split(q_far[m, at, :]), (rf_h[m], rf_l[m]))

                return rest // base

            lax.fori_loop(0, dm, far_step, far_list)
            for row, (device, _) in plan.items():

                @pl.when(me == device)
                def _():
                    part_copy(c, row).start()

    lax.fori_loop(0, dm, own_step, own_list)

    if plan:

        @pl.when(any_of(me, list(plan)))
        def _():
            remote(acc_far, partial_in, part_sem.at[0], part_sem.at[1], 0).wait_recv()
            acc[...] += partial_in[...]

    sent = jnp.int32(0)
    for m in range(1, dist):
        sent = sent + jnp.where(near(me - m), 1, 0)
    for row, (device, shifts) in plan.items():
        if device - row in shifts:
            sent = sent - jnp.where(me == device, 1, 0)
    for count in range(1, dist):

        @pl.when(sent == count)
        def _():
            whole = pl.ds(0, count)
            remote(qm1.at[whole], r_in.at[whole], r_send.at[0], r_recv.at[0], 0).wait_send()

    for row, (device, shifts) in plan.items():

        @pl.when(me == row)
        def _():
            whole = q_units(units(row), pl.ds(0, block))
            remote(qm.at[whole], q_far.at[whole], q_send.at[0], q_recv.at[0], 0).wait_send()

    for row, m in halved:

        @pl.when(me == row + m)
        def _():
            half_copy(m, row).wait_send()

    @pl.when(me >= dist)
    def _():
        code_send().wait_send()

    if plan:

        @pl.when(any_of(me, [device for device, _ in plan.values()]))
        def _():
            remote(acc_far, partial_in, part_sem.at[0], part_sem.at[1], 0).wait_send()

    for via in sorted({via for via, _, _ in relay.values()}):

        @pl.when(me == via)
        def _():
            whole = pl.ds(0, sum(1 for key in slots if relay[key[:2]][0] == via))
            remote(relay_in.at[whole], relay_in.at[whole], relay_send.at[0], r_recv.at[0], 0).wait_send()


def finish(dist, acc, weight, row_sum, pair_out, branch_out, multi_out):
    block = weight.shape[0]
    beta = 1.0 / (dist * block)
    column = lax.broadcasted_iota(jnp.int32, (block, 1), 0).astype(F32)
    line = lax.broadcasted_iota(jnp.int32, (1, block), 1).astype(F32)
    rows_i = lax.broadcasted_iota(jnp.int32, (block, block), 0)
    cols_i = lax.broadcasted_iota(jnp.int32, (block, block), 1)
    upper = jnp.where(cols_i >= rows_i, 1.0, 0.0).astype(BF16)
    summed = acc[HEAD:, :]
    pair = weight[...] * (1.0 + 0.8 * summed)
    pair_out[...] = pair
    high, low = split(pair * jnp.exp(line * beta))
    inner = mm(high, upper) + mm(low, upper)
    branch = (row_sum[:, 0:1] + inner) * (beta * jnp.exp(line * (-beta)))
    branch_out[...] = branch
    high, low = split(branch * jnp.exp(column * (-beta)))
    tails = acc[0:1, :] + mm(upper, high) + mm(upper, low)
    multi_out[...] = summed + 0.01 * jnp.exp(column * beta) * tails


def solution(mesh):
    width = mesh.shape["row"]

    def per_device(qm, qm1, qb, codes, energy_index, turner):
        dm, block = qm.shape[2], qm.shape[3]
        dist = dm + 1
        known = width == 16 and dist == 8
        plan = PLAN if known else {}
        relay = RELAY if known else {}
        pieces = max([1] + [sum(n for v, n, _ in relay.values() if v == via) for via, _, _ in relay.values()])
        blocks = pltpu.VMEM((dm, block, block), F32)
        halves = pltpu.VMEM((dm, block, block), BF16)
        square = jax.ShapeDtypeStruct((block, block), F32)
        tall = pltpu.VMEM((block + HEAD, block), F32)
        dma = pltpu.SemaphoreType.DMA
        anywhere = pl.BlockSpec(memory_space=pltpu.HBM)
        local = pl.BlockSpec(memory_space=pltpu.VMEM)
        middle = pl.pallas_call(
            functools.partial(kernel, plan, relay, width),
            out_shape=[
                pltpu.VMEM((block + HEAD, block), F32),
                pltpu.VMEM((block, block), F32),
                pltpu.VMEM((block, 128), F32),
            ],
            in_specs=[anywhere] * 6,
            out_specs=[local] * 3,
            scratch_shapes=[
                blocks, blocks, blocks, blocks, halves, halves, blocks,
                pltpu.VMEM((block, block), jnp.int32),
                pltpu.VMEM((1, block), jnp.int32),
                tall, tall, pltpu.VMEM((pieces, block // PIECES, block), F32),
                pltpu.VMEM((1, block), jnp.int32),
                pltpu.VMEM((1, turner.shape[0]), F32),
                dma((1,)), dma((1,)), dma((CHUNKS - 1 + dm,)), dma((1,)), dma((dm,)), dma((dm,)),
                dma((4,)), dma((2,)), dma((2,)),
                pltpu.SemaphoreType.REGULAR((len(HELD),)), dma((1,)),
            ],
            compiler_params=pltpu.CompilerParams(has_side_effects=True, collective_id=0),
        )(
            qm[0, 0], qm1[0, 0], qb[0, 0], energy_index[0, 0],
            codes[0], turner[None, :],
        )
        outs = pl.pallas_call(
            functools.partial(finish, dist),
            out_shape=[square] * 3,
            in_specs=[local] * 3,
            out_specs=[local] * 3,
            compiler_params=pltpu.CompilerParams(vmem_limit_bytes=16 * 2**20),
        )(*middle)
        return tuple(out[None, None] for out in outs)

    return jax.shard_map(
        per_device,
        mesh=mesh,
        in_specs=(
            P("seq", "row", None, None, None),
            P("seq", "row", None, None, None),
            P("seq", "row", None, None, None),
            P("seq", "row", None),
            P("seq", "row", None, None),
            P(),
        ),
        out_specs=(
            P("seq", "row", None, None),
            P("seq", "row", None, None),
            P("seq", "row", None, None),
        ),
        check_vma=False,
    )
```

```python
import functools

import jax
import jax.numpy as jnp
from jax import lax
from jax.experimental import pallas as pl
from jax.experimental.pallas import tpu as pltpu
from jax.sharding import PartitionSpec as P

F32 = jnp.float32
BF16 = jnp.bfloat16

PLAN = {
    1: (5, (4, 3, 6, 5, 7)),
    3: (6, (3, 1, 2, 7, 6, 5)),
    4: (8, (4, 5, 7, 6)),
    5: (9, (3, 6, 5, 7)),
    7: (11, (4, 3, 7, 1, 2, 5, 6)),
}
RELAY = {
    (6, 7): (15, 4, 1),
    (6, 6): (14, 4, 1),
    (2, 6): (10, 4, 0),
    (6, 2): (10, 1, 4),
    (6, 3): (10, 4, 0),
    (7, 5): (14, 4, 0),
    (7, 6): (15, 4, 0),
}
HELD = (
    {4: (6,), 5: (6,), 8: (10, 11), 9: (10, 11)},
    {4: (2,), 5: (2,), 8: (2, 6), 9: (2, 6)},
)
SPLIT = ((4, 4),)
ORDER = {6: (1, 7, 6, 5, 4, 3, 2)}
DETOUR = {(5, 7): 6}
SHARES = (8, 4, 3, 1)
CHUNKS = len(SHARES)
PIECES = 4
HEAD = 8


def split(x):
    high = x.astype(BF16)
    return high, (x - high.astype(F32)).astype(BF16)


def mm(a, b):
    return jnp.dot(a, b, preferred_element_type=F32)


def dot3(a, b):
    ah, al = a
    bh, bl = b
    return mm(ah, bh) + (mm(ah, bl) + mm(al, bh))


def any_of(x, values):
    hit = x == values[0]
    for value in values[1:]:
        hit = jnp.logical_or(hit, x == value)
    return hit


def kernel(
    plan, relay, width, qm, qm1, qb, eidx, codes, turner, acc, weight, row_sum, partial_in,
    q_own, r_in, r_far, q_far, rf_h, rf_l, qb_in, e_in, code_in, acc_far, relay_in, code_own, table_in,
    own_sem, q_send, q_recv, r_send, r_recv, rf_recv, load_sem, code_sem, part_sem, held_sem,
):
    dm, block = qm.shape[0], qm.shape[1]
    dist = dm + 1
    live_rows = width - dist
    beta = 1.0 / (dist * block)
    base = dm + 1
    me = lax.axis_index("row")
    live = me < live_rows
    relay_send, relay_recv = q_send, q_recv
    unit = block // sum(SHARES)
    piece = block // PIECES
    side = block // 8

    def remote(src, dst, send, recv, device):
        return pltpu.make_async_remote_copy(
            src_ref=src, dst_ref=dst, send_sem=send, recv_sem=recv,
            device_id={"row": device}, device_id_type=pl.DeviceIdType.MESH,
        )

    def near(row):
        return jnp.logical_and(row >= 0, row < live_rows)

    def home(row, m):
        device, shifts = plan.get(row, (None, ()))
        return device if m in shifts else row

    held = HELD if plan else ()
    order = ORDER if plan else {}
    halved = SPLIT if plan else ()
    detour = DETOUR if plan else {}
    half = block // 2
    waiting = []
    for group in held:
        lists = {source: [] for source in group}
        for source in group:
            for row in range(min(live_rows, source) - 1, max(source - dist, -1), -1):
                m = source - row
                via, count, _ = relay.get((row, m), (None, 0, 0))
                if home(row, m) in group[source] and count < PIECES:
                    lists[source].append((row, m, "rest"))
                if via in group[source]:
                    lists[source].append((row, m, "relay"))
            lists[source].sort(key=lambda item: (item[2] == "relay", item[0] not in (3, 7), -item[0]))
        waiting.append(lists)
    for row, m in halved:
        waiting[-1][row + m].insert(1, (row, m, "half"))
    for (row, m), via in detour.items():
        for n, group in enumerate(held):
            if via in group.get(row, ()):
                waiting[n][row].insert(0, (row, m, "detour"))
    kinds = [item for lists in waiting for keys in lists.values() for item in keys]
    rests = {(row, m) for row, m, kind in kinds if kind == "rest"}
    parts = {(row, m) for row, m, kind in kinds if kind == "relay"}

    def apart(m):
        if not plan:
            return []
        return [
            row for row in range(live_rows)
            if (row, m) in relay or (row, m) in rests or home(row, m) != row
        ]

    def held_send(row, m):
        if (row, m) in relay:
            relay_rest(row, m).start()
        else:
            (r_copy if home(row, m) == row else rf_copy)(m, home(row, m)).start()

    def direct(m):
        row = me - m
        ok = near(row)
        rows = apart(m)
        return jnp.logical_and(ok, jnp.logical_not(any_of(row, rows))) if rows else ok

    def code_send():
        return remote(codes, code_in, code_sem.at[0], code_sem.at[1], me - dist)

    def rows_of(c, shift=0):
        return pl.ds(sum(SHARES[:c]) * unit + shift, SHARES[c] * unit)

    def q_copy(row, m, c, device):
        rows = rows_of(c)
        if c == 0 and (row, m) in detour:
            rows = pl.ds(side, SHARES[0] * unit - side)
        at = (m - 1, rows, pl.ds(0, half if (row, m) in halved else block))
        slot = c if c < CHUNKS - 1 else CHUNKS - 2 + m
        return remote(qm.at[at], q_far.at[at], q_send.at[0], q_recv.at[slot], device)

    def r_copy(m, device):
        return remote(qm1.at[dm - m], r_in.at[m - 1], r_send.at[0], r_recv.at[m - 1], device)

    def rf_copy(m, device):
        return remote(qm1.at[dm - m], r_far.at[m - 1], r_send.at[0], rf_recv.at[m - 1], device)

    def detour_copy(m, via):
        return remote(qm.at[m - 1, pl.ds(0, side)], relay_in.at[0, pl.ds(0, side)], q_send.at[0], code_sem.at[0], via)

    def detour_on(m, device):
        return remote(relay_in.at[0, pl.ds(0, side)], q_far.at[m - 1, pl.ds(0, side)], q_send.at[0], q_recv.at[0], device)

    def half_copy(m, device):
        at = pl.ds(half, block - half)
        return remote(qm1.at[dm - m, at], r_in.at[m - 1, at], q_send.at[0], r_recv.at[m - 1], device)

    def units(row):
        shifts = plan[row][1]
        return 2 * len(shifts) - sum(1 for m in shifts if (row, m) in halved)

    def q_units(count, rows):
        if count % 2 == 0:
            at = (pl.ds(0, count // 2), rows)
        else:
            at = (pl.ds(0, count), rows, pl.ds(0, half))
        return at

    def right_at(row, m):
        return (r_in, r_recv) if home(row, m) == row else (r_far, rf_recv)

    turns = sorted((rank + p, row, m, p) for (row, m), (_, count, rank) in relay.items() for p in range(count))
    slots = {}
    for _, row, m, p in turns:
        slots[row, m, p] = sum(1 for key in slots if relay[key[:2]][0] == relay[row, m][0])

    def relay_copy(row, m, p):
        slot = slots[row, m, p]
        return remote(
            qm1.at[dm - m, pl.ds(p * piece, piece)], relay_in.at[slot],
            r_send.at[0], relay_recv.at[slot], relay[row, m][0],
        )

    def relay_on(row, m, p):
        at = pl.ds(p * piece, piece)
        into, sem = right_at(row, m)
        return remote(
            relay_in.at[slots[row, m, p]], into.at[m - 1, at], relay_send.at[0], sem.at[m - 1], home(row, m)
        )

    def relay_rest(row, m):
        start = relay[row, m][1] * piece
        at = pl.ds(start, block - start)
        into, sem = right_at(row, m)
        return remote(qm1.at[dm - m, at], into.at[m - 1, at], r_send.at[0], sem.at[m - 1], home(row, m))

    def send_held(n):
        for source, keys in waiting[n].items():

            @pl.when(me == source)
            def _():
                pl.semaphore_wait(held_sem.at[n], len(held[n][source]))
                for row, m, kind in keys:
                    if kind == "relay":
                        for p in range(relay[row, m][1]):
                            relay_copy(row, m, p).start()
                    elif kind == "half":
                        half_copy(m, row).start()
                    elif kind == "detour":
                        detour_copy(m, detour[row, m]).start()
                    else:
                        held_send(row, m)

    def part_copy(c, device):
        start = HEAD + sum(SHARES[:c]) * unit if c else 0
        at = pl.ds(start, HEAD + sum(SHARES[: c + 1]) * unit - start)
        return remote(acc_far.at[at], partial_in.at[at], part_sem.at[0], part_sem.at[1], device)

    barrier = pltpu.get_barrier_semaphore()

    def greet(device):
        pl.semaphore_signal(
            barrier, inc=1, device_id={"row": device}, device_id_type=pl.DeviceIdType.MESH
        )

    if plan:
        pairs = {(device, device - dist) for device in range(dist, width)}
        for row in range(live_rows):
            for m in range(1, dist):
                source, device = row + m, home(row, m)
                via, count, _ = relay.get((row, m), (None, 0, 0))
                if count:
                    pairs |= {(source, via), (via, device)}
                if count < PIECES:
                    pairs.add((source, device))
                if (row, m) in halved:
                    pairs.add((source, row))
        for row, (device, _) in plan.items():
            pairs |= {(row, device), (device, row)}
        for (row, m), via in detour.items():
            pairs |= {(row, via), (via, plan[row][0])}
        for group in held:
            for source, devices in group.items():
                pairs -= {(source, device) for device in devices}
                pairs |= {(device, source) for device in devices}
        pairs = sorted((s, d) for s, d in pairs if s != d)
        awaited = jnp.int32(0)
        for device in range(width):
            sources = [s for s, d in pairs if d == device]
            awaited = awaited + jnp.where(me == device, sum(1 for s, _ in pairs if s == device), 0)
            if sources:

                @pl.when(me == device)
                def _():
                    for source in sources:
                        greet(source)

    else:

        @pl.when(live)
        def _():
            for m in range(1, dist + 1):
                greet(me + m)

        awaited = jnp.int32(0)
        for m in range(1, dist + 1):
            awaited = awaited + jnp.where(near(me - m), 1, 0)

    @pl.when(awaited > 0)
    def _():
        pl.semaphore_wait(barrier, awaited)

    for n, group in enumerate(held):
        for device in sorted({device for devices in group.values() for device in devices}):

            @pl.when(me == device)
            def _():
                for source in [source for source, devices in group.items() if device in devices]:
                    pl.semaphore_signal(
                        held_sem.at[n], inc=1, device_id={"row": source}, device_id_type=pl.DeviceIdType.MESH
                    )

    @pl.when(me >= dist)
    def _():
        code_send().start()

    for m in range(dm, 0, -1):
        for row, (device, shifts) in plan.items():
            if m not in shifts or (row, m) in relay or (row, m) in rests:
                continue

            @pl.when(me == row + m)
            def _():
                if row + m == device:
                    pltpu.make_async_copy(qm1.at[dm - m], r_far.at[m - 1], rf_recv.at[m - 1]).start()
                else:
                    rf_copy(m, device).start()

    for row, (device, shifts) in plan.items():

        @pl.when(me == row)
        def _():
            for c in range(CHUNKS):
                for m in shifts:
                    q_copy(row, m, c, device).start()

    for source in sorted({row + m for row, m in relay}):

        @pl.when(me == source)
        def _():
            for row, m, p in slots:
                if row + m == source and (row, m) not in parts:
                    relay_copy(row, m, p).start()
            for (row, m), (_, count, _) in relay.items():
                if row + m == source and count < PIECES and (row, m) not in rests:
                    relay_rest(row, m).start()

    for m in range(dm, 0, -1):

        @pl.when(direct(m))
        def _():
            r_copy(m, me - m).start()

    loads = (
        pltpu.make_async_copy(qb, qb_in, load_sem.at[0]),
        pltpu.make_async_copy(eidx, e_in, load_sem.at[1]),
        pltpu.make_async_copy(codes, code_own, load_sem.at[2]),
        pltpu.make_async_copy(turner, table_in, load_sem.at[3]),
        pltpu.make_async_copy(qm, q_own, own_sem.at[0]),
    )

    @pl.when(live)
    def _():
        for load in loads:
            load.start()

    if held:
        send_held(0)
    for (row, m), via in detour.items():

        @pl.when(me == via)
        def _():
            detour_copy(m, 0).wait_recv()
            detour_on(m, plan[row][0]).start()

    for via in sorted({via for via, _, _ in relay.values()}):

        @pl.when(me == via)
        def _():
            for row, m, p in slots:
                if relay[row, m][0] == via:
                    relay_copy(row, m, p).wait_recv()
                    relay_on(row, m, p).start()

    acc[...] = jnp.zeros_like(acc)
    acc_far[...] = jnp.zeros_like(acc_far)
    for row, m in halved:

        @pl.when(me == plan[row][0])
        def _():
            q_far[m - 1, :, half:] = jnp.zeros((block, block - half), F32)

        @pl.when(me == row)
        def _():
            r_in[m - 1, 0:half, :] = jnp.zeros((half, block), F32)

    @pl.when(jnp.logical_not(any_of(me, list(plan))) if plan else me >= 0)
    def _():
        partial_in[...] = jnp.zeros_like(partial_in)

    @pl.when(jnp.logical_not(live))
    def _():
        weight[...] = jnp.zeros_like(weight)
        row_sum[...] = jnp.zeros_like(row_sum)

    rows_i = lax.broadcasted_iota(jnp.int32, (block, block), 0)
    cols_i = lax.broadcasted_iota(jnp.int32, (block, block), 1)
    column = lax.broadcasted_iota(jnp.int32, (block, 1), 0)
    line = lax.broadcasted_iota(jnp.int32, (1, block), 1)

    @pl.when(live)
    def _():
        loads[0].wait()
        total = jnp.zeros((block, block), F32)
        for e in range(1, dist):
            factor = jnp.exp((line - (dist - e) * block).astype(F32) * beta)
            total = total + qb_in[e - 1] * factor
        row_sum[...] = jnp.broadcast_to(jnp.sum(total, axis=1, keepdims=True), row_sum.shape)
        loads[2].wait()
        loads[3].wait()
        first = jnp.sum(jnp.where(rows_i == cols_i, code_own[...].astype(F32), 0.0), axis=1, keepdims=True)
        table = jnp.exp(-table_in[...])
        entries = table.shape[1]
        table = jnp.concatenate([table, jnp.zeros((1, 128 - entries), F32)], axis=1)
        table = jnp.broadcast_to(table, (block, 128))
        loads[1].wait()
        code_send().wait_recv()
        both = first + code_in[...].astype(F32)
        allowed = jnp.where(jnp.logical_or(both == 3.0, both == 5.0), 1.0, 0.0)
        for start in range(0, block, 128):
            part = pl.ds(start, 128)
            found = jnp.take_along_axis(table, e_in[:, part], axis=1, mode="promise_in_bounds")
            weight[:, part] = found * allowed[:, start : start + 128]
        loads[4].wait()

    for n in range(1, len(held)):
        send_held(n)

    def column_sum(m, right, total):
        fade = jnp.exp((-(m + 1) * block - column).astype(F32) * beta)
        total[0:1, :] += jnp.sum(right * fade, axis=0, keepdims=True)

    def is_half(m, place):
        hit = jnp.bool_(False)
        for row, shift in halved:
            hit = jnp.logical_or(hit, jnp.logical_and(me == place(row, shift), m == shift - 1))
        return hit

    def listed(shifts):
        return sum(m * base**i for i, m in enumerate(shifts))

    own_list = jnp.int32(listed(range(1, dm + 1)))
    for row in range(live_rows) if plan else ():
        shifts = [m for m in order.get(row, range(1, dm + 1)) if home(row, m) == row or (row, m) in halved]
        own_list = jnp.where(me == row, listed(shifts), own_list)
    own_list = jnp.where(live, own_list, 0)

    def own_step(step, rest):
        m = rest % base - 1

        @pl.when(rest > 0)
        def _():
            small = is_half(m, lambda row, _: row)

            @pl.when(small)
            def _():
                half_copy(m + 1, 0).wait_recv()

            @pl.when(jnp.logical_not(small))
            def _():
                r_copy(m + 1, 0).wait_recv()
                column_sum(m, r_in[m], acc)

            right = r_in[m]
            acc[HEAD:, :] += dot3(split(q_own[m]), split(right))

        return rest // base

    if plan:
        far_list = jnp.int32(0)
        for device, shifts in plan.values():
            far_list = far_list + jnp.where(me == device, listed(shifts), 0)
        for c in range(CHUNKS):
            at = rows_of(c)
            if c < CHUNKS - 1:
                for count in sorted({units(row) for row in plan}):

                    @pl.when(any_of(me, [plan[row][0] for row in plan if units(row) == count]))
                    def _():
                        whole = q_units(count, at)
                        remote(qm.at[whole], q_far.at[whole], q_send.at[0], q_recv.at[c], 0).wait_recv()

            def far_step(step, rest):
                m = rest % base - 1

                @pl.when(rest > 0)
                def _():
                    if c == 0:
                        rf_copy(m + 1, 0).wait_recv()
                        right = r_far[m]
                        rf_h[m], rf_l[m] = split(right)
                        column_sum(m, right, acc_far)
                    if c == CHUNKS - 1:
                        slot = q_recv.at[CHUNKS - 1 + m]

                        def wait_for(lanes):
                            here = (m, at, pl.ds(0, lanes))
                            remote(qm.at[here], q_far.at[here], q_send.at[0], slot, 0).wait_recv()

                        small = is_half(m, lambda row, _: plan[row][0])

                        @pl.when(small)
                        def _():
                            wait_for(half)

                        @pl.when(jnp.logical_not(small))
                        def _():
                            wait_for(block)
                    acc_far[rows_of(c, HEAD), :] += dot3(split(q_far[m, at, :]), (rf_h[m], rf_l[m]))

                return rest // base

            lax.fori_loop(0, dm, far_step, far_list)
            for row, (device, _) in plan.items():

                @pl.when(me == device)
                def _():
                    part_copy(c, row).start()

    lax.fori_loop(0, dm, own_step, own_list)

    if plan:

        @pl.when(any_of(me, list(plan)))
        def _():
            remote(acc_far, partial_in, part_sem.at[0], part_sem.at[1], 0).wait_recv()

    sent = jnp.int32(0)
    for m in range(1, dist):
        sent = sent + jnp.where(near(me - m), 1, 0)
    for row, (device, shifts) in plan.items():
        if device - row in shifts:
            sent = sent - jnp.where(me == device, 1, 0)
    for count in range(1, dist):

        @pl.when(sent == count)
        def _():
            whole = pl.ds(0, count)
            remote(qm1.at[whole], r_in.at[whole], r_send.at[0], r_recv.at[0], 0).wait_send()

    for row, (device, shifts) in plan.items():

        @pl.when(me == row)
        def _():
            whole = q_units(units(row), pl.ds(0, block))
            remote(qm.at[whole], q_far.at[whole], q_send.at[0], q_recv.at[0], 0).wait_send()

    for row, m in halved:

        @pl.when(me == row + m)
        def _():
            half_copy(m, row).wait_send()

    for (_, m), via in detour.items():

        @pl.when(me == via)
        def _():
            detour_on(m, 0).wait_send()

    @pl.when(me >= dist)
    def _():
        code_send().wait_send()

    if plan:

        @pl.when(any_of(me, [device for device, _ in plan.values()]))
        def _():
            remote(acc_far, partial_in, part_sem.at[0], part_sem.at[1], 0).wait_send()

    for via in sorted({via for via, _, _ in relay.values()}):

        @pl.when(me == via)
        def _():
            whole = pl.ds(0, sum(1 for key in slots if relay[key[:2]][0] == via))
            remote(relay_in.at[whole], relay_in.at[whole], relay_send.at[0], r_recv.at[0], 0).wait_send()


def finish(dist, acc, weight, row_sum, partial, pair_out, branch_out, multi_out):
    block = weight.shape[0]
    beta = 1.0 / (dist * block)
    column = lax.broadcasted_iota(jnp.int32, (block, 1), 0).astype(F32)
    line = lax.broadcasted_iota(jnp.int32, (1, block), 1).astype(F32)
    rows_i = lax.broadcasted_iota(jnp.int32, (block, block), 0)
    cols_i = lax.broadcasted_iota(jnp.int32, (block, block), 1)
    upper = jnp.where(cols_i >= rows_i, 1.0, 0.0).astype(BF16)
    summed = acc[HEAD:, :] + partial[HEAD:, :]
    pair = weight[...] * (1.0 + 0.8 * summed)
    pair_out[...] = pair
    high, low = split(pair * jnp.exp(line * beta))
    inner = mm(high, upper) + mm(low, upper)
    branch = (row_sum[:, 0:1] + inner) * (beta * jnp.exp(line * (-beta)))
    branch_out[...] = branch
    high, low = split(branch * jnp.exp(column * (-beta)))
    tails = acc[0:1, :] + partial[0:1, :] + mm(upper, high) + mm(upper, low)
    multi_out[...] = summed + 0.01 * jnp.exp(column * beta) * tails


def solution(mesh):
    width = mesh.shape["row"]

    def per_device(qm, qm1, qb, codes, energy_index, turner):
        dm, block = qm.shape[2], qm.shape[3]
        dist = dm + 1
        known = width == 16 and dist == 8
        plan = PLAN if known else {}
        relay = RELAY if known else {}
        pieces = max([1] + [sum(n for v, n, _ in relay.values() if v == via) for via, _, _ in relay.values()])
        blocks = pltpu.VMEM((dm, block, block), F32)
        halves = pltpu.VMEM((dm, block, block), BF16)
        square = jax.ShapeDtypeStruct((block, block), F32)
        tall = pltpu.VMEM((block + HEAD, block), F32)
        dma = pltpu.SemaphoreType.DMA
        anywhere = pl.BlockSpec(memory_space=pltpu.HBM)
        local = pl.BlockSpec(memory_space=pltpu.VMEM)
        middle = pl.pallas_call(
            functools.partial(kernel, plan, relay, width),
            out_shape=[
                pltpu.VMEM((block + HEAD, block), F32),
                pltpu.VMEM((block, block), F32),
                pltpu.VMEM((block, 128), F32),
                tall,
            ],
            in_specs=[anywhere] * 6,
            out_specs=[local] * 4,
            scratch_shapes=[
                blocks, blocks, blocks, blocks, halves, halves, blocks,
                pltpu.VMEM((block, block), jnp.int32),
                pltpu.VMEM((1, block), jnp.int32),
                tall, pltpu.VMEM((pieces, block // PIECES, block), F32),
                pltpu.VMEM((1, block), jnp.int32),
                pltpu.VMEM((1, turner.shape[0]), F32),
                dma((1,)), dma((1,)), dma((CHUNKS - 1 + dm,)), dma((1,)), dma((dm,)), dma((dm,)),
                dma((4,)), dma((2,)), dma((2,)),
                pltpu.SemaphoreType.REGULAR((len(HELD),)),
            ],
            compiler_params=pltpu.CompilerParams(has_side_effects=True, collective_id=0),
        )(
            qm[0, 0], qm1[0, 0], qb[0, 0], energy_index[0, 0],
            codes[0], turner[None, :],
        )
        outs = pl.pallas_call(
            functools.partial(finish, dist),
            out_shape=[square] * 3,
            in_specs=[local] * 4,
            out_specs=[local] * 3,
            compiler_params=pltpu.CompilerParams(vmem_limit_bytes=16 * 2**20),
        )(*middle)
        return tuple(out[None, None] for out in outs)

    return jax.shard_map(
        per_device,
        mesh=mesh,
        in_specs=(
            P("seq", "row", None, None, None),
            P("seq", "row", None, None, None),
            P("seq", "row", None, None, None),
            P("seq", "row", None),
            P("seq", "row", None, None),
            P(),
        ),
        out_specs=(
            P("seq", "row", None, None),
            P("seq", "row", None, None),
            P("seq", "row", None, None),
        ),
        check_vma=False,
    )
```

```python
import functools

import jax
import jax.numpy as jnp
from jax import lax
from jax.experimental import pallas as pl
from jax.experimental.pallas import tpu as pltpu
from jax.sharding import PartitionSpec as P

F32 = jnp.float32
BF16 = jnp.bfloat16

PLAN = {
    1: (5, (4, 3, 6, 5, 7)),
    3: (6, (3, 1, 2, 7, 6, 5)),
    4: (8, (4, 5, 7, 6)),
    5: (9, (3, 6, 5, 7)),
    7: (11, (4, 3, 7, 1, 2, 5, 6)),
}
RELAY = {
    (6, 7): (15, 4, 0),
    (6, 6): (14, 4, 0),
    (2, 6): (10, 4, 0),
    (6, 2): (10, 1, 4),
    (6, 3): (10, 4, 0),
    (7, 5): (14, 4, 2),
    (7, 6): (15, 4, 2),
}
HELD = (
    {4: (6,), 5: (6,), 8: (10, 11), 9: (10, 11)},
    {4: (2,), 5: (2,), 8: (2, 6), 9: (2, 6)},
)
SPLIT = ((4, 4),)
ORDER = {6: (1, 7, 6, 5, 4, 3, 2)}
DETOUR = {(5, 7): 6}
SHARES = (8, 4, 3, 1)
CHUNKS = len(SHARES)
PIECES = 4
HEAD = 8


def split(x):
    high = x.astype(BF16)
    return high, (x - high.astype(F32)).astype(BF16)


def mm(a, b):
    return jnp.dot(a, b, preferred_element_type=F32)


def dot3(a, b):
    ah, al = a
    bh, bl = b
    return mm(ah, bh) + (mm(ah, bl) + mm(al, bh))


def any_of(x, values):
    hit = x == values[0]
    for value in values[1:]:
        hit = jnp.logical_or(hit, x == value)
    return hit


def kernel(
    plan, relay, width, qm, qm1, qb, eidx, codes, turner, acc, weight, row_sum, partial_in,
    q_own, r_in, r_far, q_far, rf_h, rf_l, qb_in, e_in, code_in, acc_far, relay_in, code_own, table_in,
    own_sem, q_send, q_recv, r_send, r_recv, rf_recv, load_sem, code_sem, part_sem, held_sem,
):
    dm, block = qm.shape[0], qm.shape[1]
    dist = dm + 1
    live_rows = width - dist
    beta = 1.0 / (dist * block)
    base = dm + 1
    me = lax.axis_index("row")
    live = me < live_rows
    relay_send, relay_recv = q_send, q_recv
    unit = block // sum(SHARES)
    piece = block // PIECES
    side = block // 8

    def remote(src, dst, send, recv, device):
        return pltpu.make_async_remote_copy(
            src_ref=src, dst_ref=dst, send_sem=send, recv_sem=recv,
            device_id={"row": device}, device_id_type=pl.DeviceIdType.MESH,
        )

    def near(row):
        return jnp.logical_and(row >= 0, row < live_rows)

    def home(row, m):
        device, shifts = plan.get(row, (None, ()))
        return device if m in shifts else row

    held = HELD if plan else ()
    order = ORDER if plan else {}
    halved = SPLIT if plan else ()
    detour = DETOUR if plan else {}
    half = block // 2
    waiting = []
    for group in held:
        lists = {source: [] for source in group}
        for source in group:
            for row in range(min(live_rows, source) - 1, max(source - dist, -1), -1):
                m = source - row
                via, count, _ = relay.get((row, m), (None, 0, 0))
                if home(row, m) in group[source] and count < PIECES:
                    lists[source].append((row, m, "rest"))
                if via in group[source]:
                    lists[source].append((row, m, "relay"))
            lists[source].sort(key=lambda item: (item[2] != "relay", item[0] not in (3, 7), -item[0]))
        waiting.append(lists)
    for row, m in halved:
        waiting[-1][row + m].insert(1, (row, m, "half"))
    for (row, m), via in detour.items():
        for n, group in enumerate(held):
            if via in group.get(row, ()):
                waiting[n][row].insert(0, (row, m, "detour"))
    kinds = [item for lists in waiting for keys in lists.values() for item in keys]
    rests = {(row, m) for row, m, kind in kinds if kind == "rest"}
    parts = {(row, m) for row, m, kind in kinds if kind == "relay"}

    def apart(m):
        if not plan:
            return []
        return [
            row for row in range(live_rows)
            if (row, m) in relay or (row, m) in rests or home(row, m) != row
        ]

    def held_send(row, m):
        if (row, m) in relay:
            relay_rest(row, m).start()
        else:
            (r_copy if home(row, m) == row else rf_copy)(m, home(row, m)).start()

    def direct(m):
        row = me - m
        ok = near(row)
        rows = apart(m)
        return jnp.logical_and(ok, jnp.logical_not(any_of(row, rows))) if rows else ok

    def code_send():
        return remote(codes, code_in, code_sem.at[0], code_sem.at[1], me - dist)

    def rows_of(c, shift=0):
        return pl.ds(sum(SHARES[:c]) * unit + shift, SHARES[c] * unit)

    def q_copy(row, m, c, device):
        rows = rows_of(c)
        if c == 0 and (row, m) in detour:
            rows = pl.ds(side, SHARES[0] * unit - side)
        at = (m - 1, rows, pl.ds(0, half if (row, m) in halved else block))
        slot = c if c < CHUNKS - 1 else CHUNKS - 2 + m
        return remote(qm.at[at], q_far.at[at], q_send.at[0], q_recv.at[slot], device)

    def r_copy(m, device):
        return remote(qm1.at[dm - m], r_in.at[m - 1], r_send.at[0], r_recv.at[m - 1], device)

    def rf_copy(m, device):
        return remote(qm1.at[dm - m], r_far.at[m - 1], r_send.at[0], rf_recv.at[m - 1], device)

    def detour_copy(m, via):
        return remote(qm.at[m - 1, pl.ds(0, side)], relay_in.at[0, pl.ds(0, side)], q_send.at[0], code_sem.at[0], via)

    def detour_on(m, device):
        return remote(relay_in.at[0, pl.ds(0, side)], q_far.at[m - 1, pl.ds(0, side)], q_send.at[0], q_recv.at[0], device)

    def half_copy(m, device):
        at = pl.ds(half, block - half)
        return remote(qm1.at[dm - m, at], r_in.at[m - 1, at], q_send.at[0], r_recv.at[m - 1], device)

    def units(row):
        shifts = plan[row][1]
        return 2 * len(shifts) - sum(1 for m in shifts if (row, m) in halved)

    def q_units(count, rows):
        if count % 2 == 0:
            at = (pl.ds(0, count // 2), rows)
        else:
            at = (pl.ds(0, count), rows, pl.ds(0, half))
        return at

    def right_at(row, m):
        return (r_in, r_recv) if home(row, m) == row else (r_far, rf_recv)

    turns = sorted((rank + p, row, m, p) for (row, m), (_, count, rank) in relay.items() for p in range(count))
    slots = {}
    for _, row, m, p in turns:
        slots[row, m, p] = sum(1 for key in slots if relay[key[:2]][0] == relay[row, m][0])

    def relay_copy(row, m, p):
        slot = slots[row, m, p]
        return remote(
            qm1.at[dm - m, pl.ds(p * piece, piece)], relay_in.at[slot],
            r_send.at[0], relay_recv.at[slot], relay[row, m][0],
        )

    def relay_on(row, m, p):
        at = pl.ds(p * piece, piece)
        into, sem = right_at(row, m)
        return remote(
            relay_in.at[slots[row, m, p]], into.at[m - 1, at], relay_send.at[0], sem.at[m - 1], home(row, m)
        )

    def relay_rest(row, m):
        start = relay[row, m][1] * piece
        at = pl.ds(start, block - start)
        into, sem = right_at(row, m)
        return remote(qm1.at[dm - m, at], into.at[m - 1, at], r_send.at[0], sem.at[m - 1], home(row, m))

    def send_held(n):
        for source, keys in waiting[n].items():

            @pl.when(me == source)
            def _():
                pl.semaphore_wait(held_sem.at[n], len(held[n][source]))
                for row, m, kind in keys:
                    if kind == "relay":
                        for p in range(relay[row, m][1]):
                            relay_copy(row, m, p).start()
                    elif kind == "half":
                        half_copy(m, row).start()
                    elif kind == "detour":
                        detour_copy(m, detour[row, m]).start()
                    else:
                        held_send(row, m)

    def part_copy(c, device):
        start = HEAD + sum(SHARES[:c]) * unit if c else 0
        at = pl.ds(start, HEAD + sum(SHARES[: c + 1]) * unit - start)
        return remote(acc_far.at[at], partial_in.at[at], part_sem.at[0], part_sem.at[1], device)

    barrier = pltpu.get_barrier_semaphore()

    def greet(device):
        pl.semaphore_signal(
            barrier, inc=1, device_id={"row": device}, device_id_type=pl.DeviceIdType.MESH
        )

    if plan:
        pairs = {(device, device - dist) for device in range(dist, width)}
        for row in range(live_rows):
            for m in range(1, dist):
                source, device = row + m, home(row, m)
                via, count, _ = relay.get((row, m), (None, 0, 0))
                if count:
                    pairs |= {(source, via), (via, device)}
                if count < PIECES:
                    pairs.add((source, device))
                if (row, m) in halved:
                    pairs.add((source, row))
        for row, (device, _) in plan.items():
            pairs |= {(row, device), (device, row)}
        for (row, m), via in detour.items():
            pairs |= {(row, via), (via, plan[row][0])}
        for group in held:
            for source, devices in group.items():
                pairs -= {(source, device) for device in devices}
                pairs |= {(device, source) for device in devices}
        pairs = sorted((s, d) for s, d in pairs if s != d)
        awaited = jnp.int32(0)
        for device in range(width):
            sources = [s for s, d in pairs if d == device]
            awaited = awaited + jnp.where(me == device, sum(1 for s, _ in pairs if s == device), 0)
            if sources:

                @pl.when(me == device)
                def _():
                    for source in sources:
                        greet(source)

    else:

        @pl.when(live)
        def _():
            for m in range(1, dist + 1):
                greet(me + m)

        awaited = jnp.int32(0)
        for m in range(1, dist + 1):
            awaited = awaited + jnp.where(near(me - m), 1, 0)

    @pl.when(awaited > 0)
    def _():
        pl.semaphore_wait(barrier, awaited)

    for n, group in enumerate(held):
        for device in sorted({device for devices in group.values() for device in devices}):

            @pl.when(me == device)
            def _():
                for source in [source for source, devices in group.items() if device in devices]:
                    pl.semaphore_signal(
                        held_sem.at[n], inc=1, device_id={"row": source}, device_id_type=pl.DeviceIdType.MESH
                    )

    @pl.when(me >= dist)
    def _():
        code_send().start()

    for m in range(dm, 0, -1):
        for row, (device, shifts) in plan.items():
            if m not in shifts or (row, m) in relay or (row, m) in rests:
                continue

            @pl.when(me == row + m)
            def _():
                if row + m == device:
                    pltpu.make_async_copy(qm1.at[dm - m], r_far.at[m - 1], rf_recv.at[m - 1]).start()
                else:
                    rf_copy(m, device).start()

    for row, (device, shifts) in plan.items():

        @pl.when(me == row)
        def _():
            for c in range(CHUNKS):
                for m in shifts:
                    q_copy(row, m, c, device).start()

    for source in sorted({row + m for row, m in relay}):

        @pl.when(me == source)
        def _():
            for row, m, p in slots:
                if row + m == source and (row, m) not in parts:
                    relay_copy(row, m, p).start()
            for (row, m), (_, count, _) in relay.items():
                if row + m == source and count < PIECES and (row, m) not in rests:
                    relay_rest(row, m).start()

    for m in range(dm, 0, -1):

        @pl.when(direct(m))
        def _():
            r_copy(m, me - m).start()

    loads = (
        pltpu.make_async_copy(qb, qb_in, load_sem.at[0]),
        pltpu.make_async_copy(eidx, e_in, load_sem.at[1]),
        pltpu.make_async_copy(codes, code_own, load_sem.at[2]),
        pltpu.make_async_copy(turner, table_in, load_sem.at[3]),
        pltpu.make_async_copy(qm, q_own, own_sem.at[0]),
    )

    @pl.when(live)
    def _():
        for load in loads:
            load.start()

    if held:
        send_held(0)
    for (row, m), via in detour.items():

        @pl.when(me == via)
        def _():
            detour_copy(m, 0).wait_recv()
            detour_on(m, plan[row][0]).start()

    for via in sorted({via for via, _, _ in relay.values()}):

        @pl.when(me == via)
        def _():
            for row, m, p in slots:
                if relay[row, m][0] == via:
                    relay_copy(row, m, p).wait_recv()
                    relay_on(row, m, p).start()

    acc[...] = jnp.zeros_like(acc)
    acc_far[...] = jnp.zeros_like(acc_far)
    for row, m in halved:

        @pl.when(me == plan[row][0])
        def _():
            q_far[m - 1, :, half:] = jnp.zeros((block, block - half), F32)

        @pl.when(me == row)
        def _():
            r_in[m - 1, 0:half, :] = jnp.zeros((half, block), F32)

    @pl.when(jnp.logical_not(any_of(me, list(plan))) if plan else me >= 0)
    def _():
        partial_in[...] = jnp.zeros_like(partial_in)

    @pl.when(jnp.logical_not(live))
    def _():
        weight[...] = jnp.zeros_like(weight)
        row_sum[...] = jnp.zeros_like(row_sum)

    rows_i = lax.broadcasted_iota(jnp.int32, (block, block), 0)
    cols_i = lax.broadcasted_iota(jnp.int32, (block, block), 1)
    column = lax.broadcasted_iota(jnp.int32, (block, 1), 0)
    line = lax.broadcasted_iota(jnp.int32, (1, block), 1)

    @pl.when(live)
    def _():
        loads[0].wait()
        total = jnp.zeros((block, block), F32)
        for e in range(1, dist):
            factor = jnp.exp((line - (dist - e) * block).astype(F32) * beta)
            total = total + qb_in[e - 1] * factor
        row_sum[...] = jnp.broadcast_to(jnp.sum(total, axis=1, keepdims=True), row_sum.shape)
        loads[2].wait()
        loads[3].wait()
        first = jnp.sum(jnp.where(rows_i == cols_i, code_own[...].astype(F32), 0.0), axis=1, keepdims=True)
        table = jnp.exp(-table_in[...])
        entries = table.shape[1]
        table = jnp.concatenate([table, jnp.zeros((1, 128 - entries), F32)], axis=1)
        table = jnp.broadcast_to(table, (block, 128))
        loads[1].wait()
        code_send().wait_recv()
        both = first + code_in[...].astype(F32)
        allowed = jnp.where(jnp.logical_or(both == 3.0, both == 5.0), 1.0, 0.0)
        for start in range(0, block, 128):
            part = pl.ds(start, 128)
            found = jnp.take_along_axis(table, e_in[:, part], axis=1, mode="promise_in_bounds")
            weight[:, part] = found * allowed[:, start : start + 128]
        loads[4].wait()

    for n in range(1, len(held)):
        send_held(n)

    def column_sum(m, right, total):
        fade = jnp.exp((-(m + 1) * block - column).astype(F32) * beta)
        total[0:1, :] += jnp.sum(right * fade, axis=0, keepdims=True)

    def is_half(m, place):
        hit = jnp.bool_(False)
        for row, shift in halved:
            hit = jnp.logical_or(hit, jnp.logical_and(me == place(row, shift), m == shift - 1))
        return hit

    def listed(shifts):
        return sum(m * base**i for i, m in enumerate(shifts))

    own_list = jnp.int32(listed(range(1, dm + 1)))
    for row in range(live_rows) if plan else ():
        shifts = [m for m in order.get(row, range(1, dm + 1)) if home(row, m) == row or (row, m) in halved]
        own_list = jnp.where(me == row, listed(shifts), own_list)
    own_list = jnp.where(live, own_list, 0)

    def own_step(step, rest):
        m = rest % base - 1

        @pl.when(rest > 0)
        def _():
            small = is_half(m, lambda row, _: row)

            @pl.when(small)
            def _():
                half_copy(m + 1, 0).wait_recv()

            @pl.when(jnp.logical_not(small))
            def _():
                r_copy(m + 1, 0).wait_recv()
                column_sum(m, r_in[m], acc)

            right = r_in[m]
            acc[HEAD:, :] += dot3(split(q_own[m]), split(right))

        return rest // base

    if plan:
        far_list = jnp.int32(0)
        for device, shifts in plan.values():
            far_list = far_list + jnp.where(me == device, listed(shifts), 0)
        for c in range(CHUNKS):
            at = rows_of(c)
            if c < CHUNKS - 1:
                for count in sorted({units(row) for row in plan}):

                    @pl.when(any_of(me, [plan[row][0] for row in plan if units(row) == count]))
                    def _():
                        whole = q_units(count, at)
                        remote(qm.at[whole], q_far.at[whole], q_send.at[0], q_recv.at[c], 0).wait_recv()

            def far_step(step, rest):
                m = rest % base - 1

                @pl.when(rest > 0)
                def _():
                    if c == 0:
                        rf_copy(m + 1, 0).wait_recv()
                        right = r_far[m]
                        rf_h[m], rf_l[m] = split(right)
                        column_sum(m, right, acc_far)
                    if c == CHUNKS - 1:
                        slot = q_recv.at[CHUNKS - 1 + m]

                        def wait_for(lanes):
                            here = (m, at, pl.ds(0, lanes))
                            remote(qm.at[here], q_far.at[here], q_send.at[0], slot, 0).wait_recv()

                        small = is_half(m, lambda row, _: plan[row][0])

                        @pl.when(small)
                        def _():
                            wait_for(half)

                        @pl.when(jnp.logical_not(small))
                        def _():
                            wait_for(block)
                    acc_far[rows_of(c, HEAD), :] += dot3(split(q_far[m, at, :]), (rf_h[m], rf_l[m]))

                return rest // base

            lax.fori_loop(0, dm, far_step, far_list)
            for row, (device, _) in plan.items():

                @pl.when(me == device)
                def _():
                    part_copy(c, row).start()

    lax.fori_loop(0, dm, own_step, own_list)

    if plan:

        @pl.when(any_of(me, list(plan)))
        def _():
            remote(acc_far, partial_in, part_sem.at[0], part_sem.at[1], 0).wait_recv()

    sent = jnp.int32(0)
    for m in range(1, dist):
        sent = sent + jnp.where(near(me - m), 1, 0)
    for row, (device, shifts) in plan.items():
        if device - row in shifts:
            sent = sent - jnp.where(me == device, 1, 0)
    for count in range(1, dist):

        @pl.when(sent == count)
        def _():
            whole = pl.ds(0, count)
            remote(qm1.at[whole], r_in.at[whole], r_send.at[0], r_recv.at[0], 0).wait_send()

    for row, (device, shifts) in plan.items():

        @pl.when(me == row)
        def _():
            whole = q_units(units(row), pl.ds(0, block))
            remote(qm.at[whole], q_far.at[whole], q_send.at[0], q_recv.at[0], 0).wait_send()

    for row, m in halved:

        @pl.when(me == row + m)
        def _():
            half_copy(m, row).wait_send()

    for (_, m), via in detour.items():

        @pl.when(me == via)
        def _():
            detour_on(m, 0).wait_send()

    @pl.when(me >= dist)
    def _():
        code_send().wait_send()

    if plan:

        @pl.when(any_of(me, [device for device, _ in plan.values()]))
        def _():
            remote(acc_far, partial_in, part_sem.at[0], part_sem.at[1], 0).wait_send()

    for via in sorted({via for via, _, _ in relay.values()}):

        @pl.when(me == via)
        def _():
            whole = pl.ds(0, sum(1 for key in slots if relay[key[:2]][0] == via))
            remote(relay_in.at[whole], relay_in.at[whole], relay_send.at[0], r_recv.at[0], 0).wait_send()


def finish(dist, acc, weight, row_sum, partial, pair_out, branch_out, multi_out):
    block = weight.shape[0]
    beta = 1.0 / (dist * block)
    column = lax.broadcasted_iota(jnp.int32, (block, 1), 0).astype(F32)
    line = lax.broadcasted_iota(jnp.int32, (1, block), 1).astype(F32)
    rows_i = lax.broadcasted_iota(jnp.int32, (block, block), 0)
    cols_i = lax.broadcasted_iota(jnp.int32, (block, block), 1)
    upper = jnp.where(cols_i >= rows_i, 1.0, 0.0).astype(BF16)
    summed = acc[HEAD:, :] + partial[HEAD:, :]
    pair = weight[...] * (1.0 + 0.8 * summed)
    pair_out[...] = pair
    high, low = split(pair * jnp.exp(line * beta))
    inner = mm(high, upper) + mm(low, upper)
    branch = (row_sum[:, 0:1] + inner) * (beta * jnp.exp(line * (-beta)))
    branch_out[...] = branch
    high, low = split(branch * jnp.exp(column * (-beta)))
    tails = acc[0:1, :] + partial[0:1, :] + mm(upper, high) + mm(upper, low)
    multi_out[...] = summed + 0.01 * jnp.exp(column * beta) * tails


def solution(mesh):
    width = mesh.shape["row"]

    def per_device(qm, qm1, qb, codes, energy_index, turner):
        dm, block = qm.shape[2], qm.shape[3]
        dist = dm + 1
        known = width == 16 and dist == 8
        plan = PLAN if known else {}
        relay = RELAY if known else {}
        pieces = max([1] + [sum(n for v, n, _ in relay.values() if v == via) for via, _, _ in relay.values()])
        blocks = pltpu.VMEM((dm, block, block), F32)
        halves = pltpu.VMEM((dm, block, block), BF16)
        square = jax.ShapeDtypeStruct((block, block), F32)
        tall = pltpu.VMEM((block + HEAD, block), F32)
        dma = pltpu.SemaphoreType.DMA
        anywhere = pl.BlockSpec(memory_space=pltpu.HBM)
        local = pl.BlockSpec(memory_space=pltpu.VMEM)
        middle = pl.pallas_call(
            functools.partial(kernel, plan, relay, width),
            out_shape=[
                pltpu.VMEM((block + HEAD, block), F32),
                pltpu.VMEM((block, block), F32),
                pltpu.VMEM((block, 128), F32),
                tall,
            ],
            in_specs=[anywhere] * 6,
            out_specs=[local] * 4,
            scratch_shapes=[
                blocks, blocks, blocks, blocks, halves, halves, blocks,
                pltpu.VMEM((block, block), jnp.int32),
                pltpu.VMEM((1, block), jnp.int32),
                tall, pltpu.VMEM((pieces, block // PIECES, block), F32),
                pltpu.VMEM((1, block), jnp.int32),
                pltpu.VMEM((1, turner.shape[0]), F32),
                dma((1,)), dma((1,)), dma((CHUNKS - 1 + dm,)), dma((1,)), dma((dm,)), dma((dm,)),
                dma((4,)), dma((2,)), dma((2,)),
                pltpu.SemaphoreType.REGULAR((len(HELD),)),
            ],
            compiler_params=pltpu.CompilerParams(has_side_effects=True, collective_id=0),
        )(
            qm[0, 0], qm1[0, 0], qb[0, 0], energy_index[0, 0],
            codes[0], turner[None, :],
        )
        outs = pl.pallas_call(
            functools.partial(finish, dist),
            out_shape=[square] * 3,
            in_specs=[local] * 4,
            out_specs=[local] * 3,
            compiler_params=pltpu.CompilerParams(vmem_limit_bytes=16 * 2**20),
        )(*middle)
        return tuple(out[None, None] for out in outs)

    return jax.shard_map(
        per_device,
        mesh=mesh,
        in_specs=(
            P("seq", "row", None, None, None),
            P("seq", "row", None, None, None),
            P("seq", "row", None, None, None),
            P("seq", "row", None),
            P("seq", "row", None, None),
            P(),
        ),
        out_specs=(
            P("seq", "row", None, None),
            P("seq", "row", None, None),
            P("seq", "row", None, None),
        ),
        check_vma=False,
    )
```

```python
import functools

import jax
import jax.numpy as jnp
from jax import lax
from jax.experimental import pallas as pl
from jax.experimental.pallas import tpu as pltpu
from jax.sharding import PartitionSpec as P

F32 = jnp.float32
BF16 = jnp.bfloat16

PLAN = {
    1: (5, (4, 3, 6, 5, 7)),
    3: (6, (3, 1, 2, 7, 6, 5)),
    4: (8, (4, 5, 7, 6)),
    5: (9, (3, 6, 5, 7)),
    7: (11, (4, 3, 7, 1, 2, 5, 6)),
}
RELAY = {
    (6, 7): (15, 4, 0),
    (6, 6): (14, 4, 0),
    (2, 6): (10, 4, 0),
    (6, 2): (10, 1, 4),
    (6, 3): (10, 4, 0),
    (7, 5): (14, 4, 2),
    (7, 6): (15, 4, 2),
}
HELD = (
    {4: (6,), 5: (6,), 8: (10, 11), 9: (10, 11)},
    {4: (2,), 5: (2,), 8: (2, 6), 9: (2, 6)},
)
SPLIT = ()
ORDER = {6: (1, 7, 6, 5, 4, 3, 2)}
DETOUR = {(4, 7): (6, 7), (5, 7): (6, 2)}
AFTER = {8: ((6, 2),)}
SHARES = (8, 4, 3, 1)
CHUNKS = len(SHARES)
COARSE = 2
PIECES = 4
HEAD = 8


def split(x):
    high = x.astype(BF16)
    return high, (x - high.astype(F32)).astype(BF16)


def mm(a, b):
    return jnp.dot(a, b, preferred_element_type=F32)


def dot3(a, b):
    ah, al = a
    bh, bl = b
    return mm(ah, bh) + (mm(ah, bl) + mm(al, bh))


def any_of(x, values):
    hit = x == values[0]
    for value in values[1:]:
        hit = jnp.logical_or(hit, x == value)
    return hit


def kernel(
    plan, relay, width, qm, qm1, qb, eidx, codes, turner, acc, weight, row_sum, partial_in,
    q_own, r_in, r_far, q_far, rf_h, rf_l, qb_in, e_in, code_in, acc_far, relay_in, detour_in, code_own, table_in,
    own_sem, q_send, q_recv, r_send, r_recv, rf_recv, load_sem, code_sem, part_sem, held_sem,
):
    dm, block = qm.shape[0], qm.shape[1]
    dist = dm + 1
    live_rows = width - dist
    beta = 1.0 / (dist * block)
    base = dm + 1
    me = lax.axis_index("row")
    live = me < live_rows
    relay_send, relay_recv = q_send, q_recv
    unit = block // sum(SHARES)
    piece = block // PIECES

    def remote(src, dst, send, recv, device):
        return pltpu.make_async_remote_copy(
            src_ref=src, dst_ref=dst, send_sem=send, recv_sem=recv,
            device_id={"row": device}, device_id_type=pl.DeviceIdType.MESH,
        )

    def near(row):
        return jnp.logical_and(row >= 0, row < live_rows)

    def home(row, m):
        device, shifts = plan.get(row, (None, ()))
        return device if m in shifts else row

    held = HELD if plan else ()
    order = ORDER if plan else {}
    halved = SPLIT if plan else ()
    detour = DETOUR if plan else {}
    after = AFTER if plan else {}
    sides, edge = {}, 0
    for key, (_, share) in detour.items():
        sides[key] = (edge, share * block // 16)
        edge += share * block // 16
    last = {key for keys in after.values() for key in keys}
    half = block // 2
    waiting = []
    for group in held:
        lists = {source: [] for source in group}
        for source in group:
            for row in range(min(live_rows, source) - 1, max(source - dist, -1), -1):
                m = source - row
                via, count, _ = relay.get((row, m), (None, 0, 0))
                if home(row, m) in group[source] and count < PIECES and (row, m) not in last:
                    lists[source].append((row, m, "rest"))
                if via in group[source]:
                    lists[source].append((row, m, "relay"))
            lists[source].sort(key=lambda item: (item[2] != "relay", item[0] not in (3, 7), -item[0]))
        waiting.append(lists)
    for row, m in halved:
        waiting[-1][row + m].insert(1, (row, m, "half"))
    for (row, m), (via, _) in detour.items():
        for n, group in enumerate(held):
            if via in group.get(row, ()):
                waiting[n][row].insert(0, (row, m, "detour"))
    kinds = [item for lists in waiting for keys in lists.values() for item in keys]
    rests = last | {(row, m) for row, m, kind in kinds if kind == "rest"}
    parts = {(row, m) for row, m, kind in kinds if kind == "relay"}

    def apart(m):
        if not plan:
            return []
        return [
            row for row in range(live_rows)
            if (row, m) in relay or (row, m) in rests or home(row, m) != row
        ]

    def held_send(row, m):
        if (row, m) in relay:
            relay_rest(row, m).start()
        else:
            (r_copy if home(row, m) == row else rf_copy)(m, home(row, m)).start()

    def direct(m):
        row = me - m
        ok = near(row)
        rows = apart(m)
        return jnp.logical_and(ok, jnp.logical_not(any_of(row, rows))) if rows else ok

    def code_send():
        return remote(codes, code_in, code_sem.at[0], code_sem.at[1], me - dist)

    def rows_of(c, shift=0):
        return pl.ds(sum(SHARES[:c]) * unit + shift, SHARES[c] * unit)

    def q_copy(row, m, c, device):
        rows = rows_of(c)
        if c == 0 and (row, m) in detour:
            start = sides[row, m][1]
            rows = pl.ds(start, SHARES[0] * unit - start)
        at = (m - 1, rows, pl.ds(0, half if (row, m) in halved else block))
        slot = c if c < COARSE else COARSE + (c - COARSE) * dm + m - 1
        return remote(qm.at[at], q_far.at[at], q_send.at[0], q_recv.at[slot], device)

    def r_copy(m, device):
        return remote(qm1.at[dm - m], r_in.at[m - 1], r_send.at[0], r_recv.at[m - 1], device)

    def rf_copy(m, device):
        return remote(qm1.at[dm - m], r_far.at[m - 1], r_send.at[0], rf_recv.at[m - 1], device)

    def detour_copy(row, m):
        start, size = sides[row, m]
        return remote(
            qm.at[m - 1, pl.ds(0, size)], detour_in.at[pl.ds(start, size)],
            q_send.at[0], code_sem.at[0], detour[row, m][0],
        )

    def detour_on(row, m):
        start, size = sides[row, m]
        return remote(
            detour_in.at[pl.ds(start, size)], q_far.at[m - 1, pl.ds(0, size)],
            q_send.at[0], q_recv.at[0], plan[row][0],
        )

    def detour_all():
        return remote(detour_in.at[pl.ds(0, edge)], detour_in.at[pl.ds(0, edge)], q_send.at[0], code_sem.at[0], 0)

    def half_copy(m, device):
        at = pl.ds(half, block - half)
        return remote(qm1.at[dm - m, at], r_in.at[m - 1, at], q_send.at[0], r_recv.at[m - 1], device)

    def units(row):
        shifts = plan[row][1]
        return 2 * len(shifts) - sum(1 for m in shifts if (row, m) in halved)

    def q_units(count, rows):
        if count % 2 == 0:
            at = (pl.ds(0, count // 2), rows)
        else:
            at = (pl.ds(0, count), rows, pl.ds(0, half))
        return at

    def right_at(row, m):
        return (r_in, r_recv) if home(row, m) == row else (r_far, rf_recv)

    turns = sorted((rank + p, row, m, p) for (row, m), (_, count, rank) in relay.items() for p in range(count))
    slots = {}
    for _, row, m, p in turns:
        slots[row, m, p] = sum(1 for key in slots if relay[key[:2]][0] == relay[row, m][0])

    def relay_copy(row, m, p):
        slot = slots[row, m, p]
        return remote(
            qm1.at[dm - m, pl.ds(p * piece, piece)], relay_in.at[slot],
            r_send.at[0], relay_recv.at[slot], relay[row, m][0],
        )

    def relay_on(row, m, p):
        at = pl.ds(p * piece, piece)
        into, sem = right_at(row, m)
        return remote(
            relay_in.at[slots[row, m, p]], into.at[m - 1, at], relay_send.at[0], sem.at[m - 1], home(row, m)
        )

    def relay_rest(row, m):
        start = relay[row, m][1] * piece
        at = pl.ds(start, block - start)
        into, sem = right_at(row, m)
        return remote(qm1.at[dm - m, at], into.at[m - 1, at], r_send.at[0], sem.at[m - 1], home(row, m))

    def send_held(n):
        for source, keys in waiting[n].items():

            @pl.when(me == source)
            def _():
                pl.semaphore_wait(held_sem.at[n], len(held[n][source]))
                for row, m, kind in keys:
                    if kind == "relay":
                        for p in range(relay[row, m][1]):
                            relay_copy(row, m, p).start()
                    elif kind == "half":
                        half_copy(m, row).start()
                    elif kind == "detour":
                        detour_copy(row, m).start()
                    else:
                        held_send(row, m)

    def part_copy(c, device):
        start = HEAD + sum(SHARES[:c]) * unit if c else 0
        at = pl.ds(start, HEAD + sum(SHARES[: c + 1]) * unit - start)
        return remote(acc_far.at[at], partial_in.at[at], part_sem.at[0], part_sem.at[1], device)

    barrier = pltpu.get_barrier_semaphore()

    def greet(device):
        pl.semaphore_signal(
            barrier, inc=1, device_id={"row": device}, device_id_type=pl.DeviceIdType.MESH
        )

    if plan:
        pairs = {(device, device - dist) for device in range(dist, width)}
        for row in range(live_rows):
            for m in range(1, dist):
                source, device = row + m, home(row, m)
                via, count, _ = relay.get((row, m), (None, 0, 0))
                if count:
                    pairs |= {(source, via), (via, device)}
                if count < PIECES:
                    pairs.add((source, device))
                if (row, m) in halved:
                    pairs.add((source, row))
        for row, (device, _) in plan.items():
            pairs |= {(row, device), (device, row)}
        for (row, m), (via, _) in detour.items():
            pairs |= {(row, via), (via, plan[row][0])}
        for group in held:
            for source, devices in group.items():
                pairs -= {(source, device) for device in devices}
                pairs |= {(device, source) for device in devices}
        pairs = sorted((s, d) for s, d in pairs if s != d)
        awaited = jnp.int32(0)
        for device in range(width):
            sources = [s for s, d in pairs if d == device]
            awaited = awaited + jnp.where(me == device, sum(1 for s, _ in pairs if s == device), 0)
            if sources:

                @pl.when(me == device)
                def _():
                    for source in sources:
                        greet(source)

    else:

        @pl.when(live)
        def _():
            for m in range(1, dist + 1):
                greet(me + m)

        awaited = jnp.int32(0)
        for m in range(1, dist + 1):
            awaited = awaited + jnp.where(near(me - m), 1, 0)

    @pl.when(awaited > 0)
    def _():
        pl.semaphore_wait(barrier, awaited)

    for n, group in enumerate(held):
        for device in sorted({device for devices in group.values() for device in devices}):

            @pl.when(me == device)
            def _():
                for source in [source for source, devices in group.items() if device in devices]:
                    pl.semaphore_signal(
                        held_sem.at[n], inc=1, device_id={"row": source}, device_id_type=pl.DeviceIdType.MESH
                    )

    @pl.when(me >= dist)
    def _():
        code_send().start()

    for m in range(dm, 0, -1):
        for row, (device, shifts) in plan.items():
            if m not in shifts or (row, m) in relay or (row, m) in rests:
                continue

            @pl.when(me == row + m)
            def _():
                if row + m == device:
                    pltpu.make_async_copy(qm1.at[dm - m], r_far.at[m - 1], rf_recv.at[m - 1]).start()
                else:
                    rf_copy(m, device).start()

    for row, (device, shifts) in plan.items():

        @pl.when(me == row)
        def _():
            for c in range(CHUNKS):
                for m in shifts:
                    q_copy(row, m, c, device).start()

    for source in sorted({row + m for row, m in relay}):

        @pl.when(me == source)
        def _():
            for row, m, p in slots:
                if row + m == source and (row, m) not in parts:
                    relay_copy(row, m, p).start()
            for (row, m), (_, count, _) in relay.items():
                if row + m == source and count < PIECES and (row, m) not in rests:
                    relay_rest(row, m).start()

    for m in range(dm, 0, -1):

        @pl.when(direct(m))
        def _():
            r_copy(m, me - m).start()

    loads = (
        pltpu.make_async_copy(qb, qb_in, load_sem.at[0]),
        pltpu.make_async_copy(eidx, e_in, load_sem.at[1]),
        pltpu.make_async_copy(codes, code_own, load_sem.at[2]),
        pltpu.make_async_copy(turner, table_in, load_sem.at[3]),
        pltpu.make_async_copy(qm, q_own, own_sem.at[0]),
    )

    @pl.when(live)
    def _():
        for load in loads:
            load.start()

    if held:
        send_held(0)
    for via in sorted({via for via, _ in detour.values()}):

        @pl.when(me == via)
        def _():
            detour_all().wait_recv()
            for row, m in detour:
                detour_on(row, m).start()

    for via in sorted({via for via, _, _ in relay.values()}):

        @pl.when(me == via)
        def _():
            for row, m, p in slots:
                if relay[row, m][0] == via:
                    relay_copy(row, m, p).wait_recv()
                    relay_on(row, m, p).start()

    acc[...] = jnp.zeros_like(acc)
    acc_far[...] = jnp.zeros_like(acc_far)
    for row, m in halved:

        @pl.when(me == plan[row][0])
        def _():
            q_far[m - 1, :, half:] = jnp.zeros((block, block - half), F32)

        @pl.when(me == row)
        def _():
            r_in[m - 1, 0:half, :] = jnp.zeros((half, block), F32)

    @pl.when(jnp.logical_not(any_of(me, list(plan))) if plan else me >= 0)
    def _():
        partial_in[...] = jnp.zeros_like(partial_in)

    @pl.when(jnp.logical_not(live))
    def _():
        weight[...] = jnp.zeros_like(weight)
        row_sum[...] = jnp.zeros_like(row_sum)

    rows_i = lax.broadcasted_iota(jnp.int32, (block, block), 0)
    cols_i = lax.broadcasted_iota(jnp.int32, (block, block), 1)
    column = lax.broadcasted_iota(jnp.int32, (block, 1), 0)
    line = lax.broadcasted_iota(jnp.int32, (1, block), 1)

    @pl.when(live)
    def _():
        loads[0].wait()
        total = jnp.zeros((block, block), F32)
        for e in range(1, dist):
            factor = jnp.exp((line - (dist - e) * block).astype(F32) * beta)
            total = total + qb_in[e - 1] * factor
        row_sum[...] = jnp.broadcast_to(jnp.sum(total, axis=1, keepdims=True), row_sum.shape)
        loads[2].wait()
        loads[3].wait()
        first = jnp.sum(jnp.where(rows_i == cols_i, code_own[...].astype(F32), 0.0), axis=1, keepdims=True)
        table = jnp.exp(-table_in[...])
        entries = table.shape[1]
        table = jnp.concatenate([table, jnp.zeros((1, 128 - entries), F32)], axis=1)
        table = jnp.broadcast_to(table, (block, 128))
        loads[1].wait()
        code_send().wait_recv()
        both = first + code_in[...].astype(F32)
        allowed = jnp.where(jnp.logical_or(both == 3.0, both == 5.0), 1.0, 0.0)
        for start in range(0, block, 128):
            part = pl.ds(start, 128)
            found = jnp.take_along_axis(table, e_in[:, part], axis=1, mode="promise_in_bounds")
            weight[:, part] = found * allowed[:, start : start + 128]
        loads[4].wait()

    for n in range(1, len(held)):
        send_held(n)

    def column_sum(m, right, total):
        fade = jnp.exp((-(m + 1) * block - column).astype(F32) * beta)
        total[0:1, :] += jnp.sum(right * fade, axis=0, keepdims=True)

    def is_half(m, place):
        hit = jnp.bool_(False)
        for row, shift in halved:
            hit = jnp.logical_or(hit, jnp.logical_and(me == place(row, shift), m == shift - 1))
        return hit

    def listed(shifts):
        return sum(m * base**i for i, m in enumerate(shifts))

    own_list = jnp.int32(listed(range(1, dm + 1)))
    for row in range(live_rows) if plan else ():
        shifts = [m for m in order.get(row, range(1, dm + 1)) if home(row, m) == row or (row, m) in halved]
        own_list = jnp.where(me == row, listed(shifts), own_list)
    own_list = jnp.where(live, own_list, 0)

    def own_step(step, rest):
        m = rest % base - 1

        @pl.when(rest > 0)
        def _():
            small = is_half(m, lambda row, _: row)

            @pl.when(small)
            def _():
                half_copy(m + 1, 0).wait_recv()

            @pl.when(jnp.logical_not(small))
            def _():
                r_copy(m + 1, 0).wait_recv()
                column_sum(m, r_in[m], acc)

            right = r_in[m]
            acc[HEAD:, :] += dot3(split(q_own[m]), split(right))

        return rest // base

    if plan:
        far_list = jnp.int32(0)
        for device, shifts in plan.values():
            far_list = far_list + jnp.where(me == device, listed(shifts), 0)
        for c in range(CHUNKS):
            at = rows_of(c)
            if c < COARSE:
                for count in sorted({units(row) for row in plan}):

                    @pl.when(any_of(me, [plan[row][0] for row in plan if units(row) == count]))
                    def _():
                        whole = q_units(count, at)
                        remote(qm.at[whole], q_far.at[whole], q_send.at[0], q_recv.at[c], 0).wait_recv()

            def far_step(step, rest):
                m = rest % base - 1

                @pl.when(rest > 0)
                def _():
                    if c == 0:
                        rf_copy(m + 1, 0).wait_recv()
                        right = r_far[m]
                        rf_h[m], rf_l[m] = split(right)
                        column_sum(m, right, acc_far)
                    if c >= COARSE:
                        slot = q_recv.at[COARSE + (c - COARSE) * dm + m]

                        def wait_for(lanes):
                            here = (m, at, pl.ds(0, lanes))
                            remote(qm.at[here], q_far.at[here], q_send.at[0], slot, 0).wait_recv()

                        small = is_half(m, lambda row, _: plan[row][0])

                        @pl.when(small)
                        def _():
                            wait_for(half)

                        @pl.when(jnp.logical_not(small))
                        def _():
                            wait_for(block)
                    acc_far[rows_of(c, HEAD), :] += dot3(split(q_far[m, at, :]), (rf_h[m], rf_l[m]))

                return rest // base

            lax.fori_loop(0, dm, far_step, far_list)
            for row, (device, _) in plan.items():

                @pl.when(me == device)
                def _():
                    part_copy(c, row).start()

            for source, keys in after.items() if c == 0 else ():

                @pl.when(me == source)
                def _():
                    for row, m in keys:
                        held_send(row, m)

    lax.fori_loop(0, dm, own_step, own_list)

    if plan:

        @pl.when(any_of(me, list(plan)))
        def _():
            remote(acc_far, partial_in, part_sem.at[0], part_sem.at[1], 0).wait_recv()

    sent = jnp.int32(0)
    for m in range(1, dist):
        sent = sent + jnp.where(near(me - m), 1, 0)
    for row, (device, shifts) in plan.items():
        if device - row in shifts:
            sent = sent - jnp.where(me == device, 1, 0)
    for count in range(1, dist):

        @pl.when(sent == count)
        def _():
            whole = pl.ds(0, count)
            remote(qm1.at[whole], r_in.at[whole], r_send.at[0], r_recv.at[0], 0).wait_send()

    for row, (device, shifts) in plan.items():

        @pl.when(me == row)
        def _():
            whole = q_units(units(row), pl.ds(0, block))
            remote(qm.at[whole], q_far.at[whole], q_send.at[0], q_recv.at[0], 0).wait_send()

    for row, m in halved:

        @pl.when(me == row + m)
        def _():
            half_copy(m, row).wait_send()

    for via in sorted({via for via, _ in detour.values()}):

        @pl.when(me == via)
        def _():
            detour_all().wait_send()

    @pl.when(me >= dist)
    def _():
        code_send().wait_send()

    if plan:

        @pl.when(any_of(me, [device for device, _ in plan.values()]))
        def _():
            remote(acc_far, partial_in, part_sem.at[0], part_sem.at[1], 0).wait_send()

    for via in sorted({via for via, _, _ in relay.values()}):

        @pl.when(me == via)
        def _():
            whole = pl.ds(0, sum(1 for key in slots if relay[key[:2]][0] == via))
            remote(relay_in.at[whole], relay_in.at[whole], relay_send.at[0], r_recv.at[0], 0).wait_send()


def finish(dist, acc, weight, row_sum, partial, pair_out, branch_out, multi_out):
    block = weight.shape[0]
    beta = 1.0 / (dist * block)
    column = lax.broadcasted_iota(jnp.int32, (block, 1), 0).astype(F32)
    line = lax.broadcasted_iota(jnp.int32, (1, block), 1).astype(F32)
    rows_i = lax.broadcasted_iota(jnp.int32, (block, block), 0)
    cols_i = lax.broadcasted_iota(jnp.int32, (block, block), 1)
    upper = jnp.where(cols_i >= rows_i, 1.0, 0.0).astype(BF16)
    summed = acc[HEAD:, :] + partial[HEAD:, :]
    pair = weight[...] * (1.0 + 0.8 * summed)
    pair_out[...] = pair
    high, low = split(pair * jnp.exp(line * beta))
    inner = mm(high, upper) + mm(low, upper)
    branch = (row_sum[:, 0:1] + inner) * (beta * jnp.exp(line * (-beta)))
    branch_out[...] = branch
    high, low = split(branch * jnp.exp(column * (-beta)))
    tails = acc[0:1, :] + partial[0:1, :] + mm(upper, high) + mm(upper, low)
    multi_out[...] = summed + 0.01 * jnp.exp(column * beta) * tails


def solution(mesh):
    width = mesh.shape["row"]

    def per_device(qm, qm1, qb, codes, energy_index, turner):
        dm, block = qm.shape[2], qm.shape[3]
        dist = dm + 1
        known = width == 16 and dist == 8
        plan = PLAN if known else {}
        relay = RELAY if known else {}
        pieces = max([1] + [sum(n for v, n, _ in relay.values() if v == via) for via, _, _ in relay.values()])
        blocks = pltpu.VMEM((dm, block, block), F32)
        halves = pltpu.VMEM((dm, block, block), BF16)
        square = jax.ShapeDtypeStruct((block, block), F32)
        tall = pltpu.VMEM((block + HEAD, block), F32)
        dma = pltpu.SemaphoreType.DMA
        anywhere = pl.BlockSpec(memory_space=pltpu.HBM)
        local = pl.BlockSpec(memory_space=pltpu.VMEM)
        middle = pl.pallas_call(
            functools.partial(kernel, plan, relay, width),
            out_shape=[
                pltpu.VMEM((block + HEAD, block), F32),
                pltpu.VMEM((block, block), F32),
                pltpu.VMEM((block, 128), F32),
                tall,
            ],
            in_specs=[anywhere] * 6,
            out_specs=[local] * 4,
            scratch_shapes=[
                blocks, blocks, blocks, blocks, halves, halves, blocks,
                pltpu.VMEM((block, block), jnp.int32),
                pltpu.VMEM((1, block), jnp.int32),
                tall, pltpu.VMEM((pieces, block // PIECES, block), F32),
                pltpu.VMEM((block, block), F32),
                pltpu.VMEM((1, block), jnp.int32),
                pltpu.VMEM((1, turner.shape[0]), F32),
                dma((1,)), dma((1,)), dma((COARSE + (CHUNKS - COARSE) * dm,)), dma((1,)), dma((dm,)), dma((dm,)),
                dma((4,)), dma((2,)), dma((2,)),
                pltpu.SemaphoreType.REGULAR((len(HELD),)),
            ],
            compiler_params=pltpu.CompilerParams(has_side_effects=True, collective_id=0),
        )(
            qm[0, 0], qm1[0, 0], qb[0, 0], energy_index[0, 0],
            codes[0], turner[None, :],
        )
        outs = pl.pallas_call(
            functools.partial(finish, dist),
            out_shape=[square] * 3,
            in_specs=[local] * 4,
            out_specs=[local] * 3,
            compiler_params=pltpu.CompilerParams(vmem_limit_bytes=16 * 2**20),
        )(*middle)
        return tuple(out[None, None] for out in outs)

    return jax.shard_map(
        per_device,
        mesh=mesh,
        in_specs=(
            P("seq", "row", None, None, None),
            P("seq", "row", None, None, None),
            P("seq", "row", None, None, None),
            P("seq", "row", None),
            P("seq", "row", None, None),
            P(),
        ),
        out_specs=(
            P("seq", "row", None, None),
            P("seq", "row", None, None),
            P("seq", "row", None, None),
        ),
        check_vma=False,
    )
```

```python
import functools

import jax
import jax.numpy as jnp
from jax import lax
from jax.experimental import pallas as pl
from jax.experimental.pallas import tpu as pltpu
from jax.sharding import PartitionSpec as P

F32 = jnp.float32
BF16 = jnp.bfloat16

PLAN = {
    1: (5, (4, 3, 6, 5, 7)),
    3: (6, (3, 1, 2, 7, 6, 5)),
    4: (8, (4, 5, 7, 6)),
    5: (9, (3, 6, 5, 7)),
    7: (11, (4, 3, 7, 1, 2, 5, 6)),
}
RELAY = {
    (6, 7): (15, 4, 0),
    (6, 6): (14, 4, 0),
    (2, 6): (10, 4, 0),
    (6, 2): (10, 1, 4),
    (6, 3): (10, 4, 0),
    (7, 5): (14, 4, 2),
    (7, 6): (15, 4, 2),
}
HELD = (
    {4: (6,), 5: (6,), 8: (10, 11), 9: (10, 11)},
    {4: (2,), 5: (2,), 8: (2, 6), 9: (2, 6)},
)
SPLIT = ()
ORDER = {6: (1, 7, 6, 5, 4, 3, 2)}
DETOUR = {(4, 7): (6, 7), (5, 7): (6, 2)}
AFTER = {8: ((6, 2),)}
FIRST = (7, 6, 11, 10, 4, 5, 9, 8, 2)
SHARES = (8, 4, 3, 1)
CHUNKS = len(SHARES)
COARSE = 2
PIECES = 4
HEAD = 8


def split(x):
    high = x.astype(BF16)
    return high, (x - high.astype(F32)).astype(BF16)


def mm(a, b):
    return jnp.dot(a, b, preferred_element_type=F32)


def dot3(a, b):
    ah, al = a
    bh, bl = b
    return mm(ah, bh) + (mm(ah, bl) + mm(al, bh))


def any_of(x, values):
    hit = x == values[0]
    for value in values[1:]:
        hit = jnp.logical_or(hit, x == value)
    return hit


def kernel(
    plan, relay, width, qm, qm1, qb, eidx, codes, turner, acc, weight, row_sum, partial_in,
    q_own, r_in, r_far, q_far, rf_h, rf_l, qb_in, e_in, code_in, acc_far, relay_in, detour_in, code_own, table_in,
    own_sem, q_send, q_recv, r_send, r_recv, rf_recv, load_sem, code_sem, part_sem, held_sem,
):
    dm, block = qm.shape[0], qm.shape[1]
    dist = dm + 1
    live_rows = width - dist
    beta = 1.0 / (dist * block)
    base = dm + 1
    me = lax.axis_index("row")
    live = me < live_rows
    relay_send, relay_recv = q_send, q_recv
    unit = block // sum(SHARES)
    piece = block // PIECES

    def remote(src, dst, send, recv, device):
        return pltpu.make_async_remote_copy(
            src_ref=src, dst_ref=dst, send_sem=send, recv_sem=recv,
            device_id={"row": device}, device_id_type=pl.DeviceIdType.MESH,
        )

    def near(row):
        return jnp.logical_and(row >= 0, row < live_rows)

    def home(row, m):
        device, shifts = plan.get(row, (None, ()))
        return device if m in shifts else row

    held = HELD if plan else ()
    order = ORDER if plan else {}
    halved = SPLIT if plan else ()
    detour = DETOUR if plan else {}
    after = AFTER if plan else {}
    sides, edge = {}, 0
    for key, (_, share) in detour.items():
        sides[key] = (edge, share * block // 16)
        edge += share * block // 16
    last = {key for keys in after.values() for key in keys}
    half = block // 2
    waiting = []
    for group in held:
        lists = {source: [] for source in group}
        for source in group:
            for row in range(min(live_rows, source) - 1, max(source - dist, -1), -1):
                m = source - row
                via, count, _ = relay.get((row, m), (None, 0, 0))
                if home(row, m) in group[source] and count < PIECES and (row, m) not in last:
                    lists[source].append((row, m, "rest"))
                if via in group[source]:
                    lists[source].append((row, m, "relay"))
            lists[source].sort(key=lambda item: (item[2] != "relay", item[0] not in (3, 7), -item[0]))
        waiting.append(lists)
    for row, m in halved:
        waiting[-1][row + m].insert(1, (row, m, "half"))
    for (row, m), (via, _) in detour.items():
        for n, group in enumerate(held):
            if via in group.get(row, ()):
                waiting[n][row].insert(0, (row, m, "detour"))
    kinds = [item for lists in waiting for keys in lists.values() for item in keys]
    rests = last | {(row, m) for row, m, kind in kinds if kind == "rest"}
    parts = {(row, m) for row, m, kind in kinds if kind == "relay"}

    def held_send(row, m):
        if (row, m) in relay:
            relay_rest(row, m).start()
        else:
            (r_copy if home(row, m) == row else rf_copy)(m, home(row, m)).start()

    def code_send():
        return remote(codes, code_in, code_sem.at[0], code_sem.at[1], me - dist)

    def rows_of(c, shift=0):
        return pl.ds(sum(SHARES[:c]) * unit + shift, SHARES[c] * unit)

    def q_copy(row, m, c, device):
        rows = rows_of(c)
        if c == 0 and (row, m) in detour:
            start = sides[row, m][1]
            rows = pl.ds(start, SHARES[0] * unit - start)
        at = (m - 1, rows, pl.ds(0, half if (row, m) in halved else block))
        slot = c if c < COARSE else COARSE + (c - COARSE) * dm + m - 1
        return remote(qm.at[at], q_far.at[at], q_send.at[0], q_recv.at[slot], device)

    def r_copy(m, device):
        return remote(qm1.at[dm - m], r_in.at[m - 1], r_send.at[0], r_recv.at[m - 1], device)

    def rf_copy(m, device):
        return remote(qm1.at[dm - m], r_far.at[m - 1], r_send.at[0], rf_recv.at[m - 1], device)

    def detour_copy(row, m):
        start, size = sides[row, m]
        return remote(
            qm.at[m - 1, pl.ds(0, size)], detour_in.at[pl.ds(start, size)],
            q_send.at[0], code_sem.at[0], detour[row, m][0],
        )

    def detour_on(row, m):
        start, size = sides[row, m]
        return remote(
            detour_in.at[pl.ds(start, size)], q_far.at[m - 1, pl.ds(0, size)],
            q_send.at[0], q_recv.at[0], plan[row][0],
        )

    def detour_all():
        return remote(detour_in.at[pl.ds(0, edge)], detour_in.at[pl.ds(0, edge)], q_send.at[0], code_sem.at[0], 0)

    def half_copy(m, device):
        at = pl.ds(half, block - half)
        return remote(qm1.at[dm - m, at], r_in.at[m - 1, at], q_send.at[0], r_recv.at[m - 1], device)

    def units(row):
        shifts = plan[row][1]
        return 2 * len(shifts) - sum(1 for m in shifts if (row, m) in halved)

    def q_units(count, rows):
        if count % 2 == 0:
            at = (pl.ds(0, count // 2), rows)
        else:
            at = (pl.ds(0, count), rows, pl.ds(0, half))
        return at

    def right_at(row, m):
        return (r_in, r_recv) if home(row, m) == row else (r_far, rf_recv)

    turns = sorted((rank + p, row, m, p) for (row, m), (_, count, rank) in relay.items() for p in range(count))
    slots = {}
    for _, row, m, p in turns:
        slots[row, m, p] = sum(1 for key in slots if relay[key[:2]][0] == relay[row, m][0])

    def relay_copy(row, m, p):
        slot = slots[row, m, p]
        return remote(
            qm1.at[dm - m, pl.ds(p * piece, piece)], relay_in.at[slot],
            r_send.at[0], relay_recv.at[slot], relay[row, m][0],
        )

    def relay_on(row, m, p):
        at = pl.ds(p * piece, piece)
        into, sem = right_at(row, m)
        return remote(
            relay_in.at[slots[row, m, p]], into.at[m - 1, at], relay_send.at[0], sem.at[m - 1], home(row, m)
        )

    def relay_rest(row, m):
        start = relay[row, m][1] * piece
        at = pl.ds(start, block - start)
        into, sem = right_at(row, m)
        return remote(qm1.at[dm - m, at], into.at[m - 1, at], r_send.at[0], sem.at[m - 1], home(row, m))

    def send_held(n):
        for source, keys in waiting[n].items():

            @pl.when(me == source)
            def _():
                pl.semaphore_wait(held_sem.at[n], len(held[n][source]))
                for row, m, kind in keys:
                    if kind == "relay":
                        for p in range(relay[row, m][1]):
                            relay_copy(row, m, p).start()
                    elif kind == "half":
                        half_copy(m, row).start()
                    elif kind == "detour":
                        detour_copy(row, m).start()
                    else:
                        held_send(row, m)

    def part_copy(c, device):
        start = HEAD + sum(SHARES[:c]) * unit if c else 0
        at = pl.ds(start, HEAD + sum(SHARES[: c + 1]) * unit - start)
        return remote(acc_far.at[at], partial_in.at[at], part_sem.at[0], part_sem.at[1], device)

    barrier = pltpu.get_barrier_semaphore()

    def greet(device):
        pl.semaphore_signal(
            barrier, inc=1, device_id={"row": device}, device_id_type=pl.DeviceIdType.MESH
        )

    if plan:
        pairs = {(device, device - dist) for device in range(dist, width)}
        for row in range(live_rows):
            for m in range(1, dist):
                source, device = row + m, home(row, m)
                via, count, _ = relay.get((row, m), (None, 0, 0))
                if count:
                    pairs |= {(source, via), (via, device)}
                if count < PIECES:
                    pairs.add((source, device))
                if (row, m) in halved:
                    pairs.add((source, row))
        for row, (device, _) in plan.items():
            pairs |= {(row, device), (device, row)}
        for (row, m), (via, _) in detour.items():
            pairs |= {(row, via), (via, plan[row][0])}
        for group in held:
            for source, devices in group.items():
                pairs -= {(source, device) for device in devices}
                pairs |= {(device, source) for device in devices}
        pairs = sorted((s, d) for s, d in pairs if s != d)
        awaited = jnp.int32(0)
        ranked = [*FIRST, *(device for device in range(width) if device not in FIRST)]
        for device in range(width):
            awaited = awaited + jnp.where(me == device, sum(1 for s, _ in pairs if s == device), 0)
        for device in ranked:
            sources = [s for s, d in pairs if d == device]
            if sources:

                @pl.when(me == device)
                def _():
                    for source in sources:
                        greet(source)

    else:

        @pl.when(live)
        def _():
            for m in range(1, dist + 1):
                greet(me + m)

        awaited = jnp.int32(0)
        for m in range(1, dist + 1):
            awaited = awaited + jnp.where(near(me - m), 1, 0)

    @pl.when(awaited > 0)
    def _():
        pl.semaphore_wait(barrier, awaited)

    def starts(device):
        found = []
        device_of, shifts = plan.get(device, (None, ()))
        found += [q_copy(device, m, 0, device_of) for m in shifts]
        for m in range(dm, 0, -1):
            row = device - m
            if 0 <= row < live_rows and home(row, m) != row and (row, m) not in relay and (row, m) not in rests:
                if home(row, m) == device:
                    found.append(pltpu.make_async_copy(qm1.at[dm - m], r_far.at[m - 1], rf_recv.at[m - 1]))
                else:
                    found.append(rf_copy(m, home(row, m)))
        for row, m, p in slots:
            if row + m == device and (row, m) not in parts:
                found.append(relay_copy(row, m, p))
        for (row, m), (_, count, _) in relay.items():
            if row + m == device and count < PIECES and (row, m) not in rests:
                found.append(relay_rest(row, m))
        for m in range(dm, 0, -1):
            row = device - m
            if 0 <= row < live_rows and home(row, m) == row and (row, m) not in relay and (row, m) not in rests:
                found.append(r_copy(m, row))
        found += [q_copy(device, m, c, device_of) for c in range(1, CHUNKS) for m in shifts]
        return found

    if plan:
        for device in ranked:

            @pl.when(me == device)
            def _():
                for n, group in enumerate(held):
                    for source in [source for source, devices in group.items() if device in devices]:
                        pl.semaphore_signal(
                            held_sem.at[n], inc=1, device_id={"row": source}, device_id_type=pl.DeviceIdType.MESH
                        )
                if device >= dist:
                    code_send().start()
                for copy in starts(device):
                    copy.start()

    if not plan:

        @pl.when(me >= dist)
        def _():
            code_send().start()

        for m in range(dm, 0, -1):

            @pl.when(near(me - m))
            def _():
                r_copy(m, me - m).start()

    loads = (
        pltpu.make_async_copy(qb, qb_in, load_sem.at[0]),
        pltpu.make_async_copy(eidx, e_in, load_sem.at[1]),
        pltpu.make_async_copy(codes, code_own, load_sem.at[2]),
        pltpu.make_async_copy(turner, table_in, load_sem.at[3]),
        pltpu.make_async_copy(qm, q_own, own_sem.at[0]),
    )

    @pl.when(live)
    def _():
        for load in loads:
            load.start()

    if held:
        send_held(0)
    for via in sorted({via for via, _ in detour.values()}):

        @pl.when(me == via)
        def _():
            detour_all().wait_recv()
            for row, m in detour:
                detour_on(row, m).start()

    for via in sorted({via for via, _, _ in relay.values()}):

        @pl.when(me == via)
        def _():
            for row, m, p in slots:
                if relay[row, m][0] == via:
                    relay_copy(row, m, p).wait_recv()
                    relay_on(row, m, p).start()

    acc[...] = jnp.zeros_like(acc)
    acc_far[...] = jnp.zeros_like(acc_far)
    for row, m in halved:

        @pl.when(me == plan[row][0])
        def _():
            q_far[m - 1, :, half:] = jnp.zeros((block, block - half), F32)

        @pl.when(me == row)
        def _():
            r_in[m - 1, 0:half, :] = jnp.zeros((half, block), F32)

    @pl.when(jnp.logical_not(any_of(me, list(plan))) if plan else me >= 0)
    def _():
        partial_in[...] = jnp.zeros_like(partial_in)

    @pl.when(jnp.logical_not(live))
    def _():
        weight[...] = jnp.zeros_like(weight)
        row_sum[...] = jnp.zeros_like(row_sum)

    rows_i = lax.broadcasted_iota(jnp.int32, (block, block), 0)
    cols_i = lax.broadcasted_iota(jnp.int32, (block, block), 1)
    column = lax.broadcasted_iota(jnp.int32, (block, 1), 0)
    line = lax.broadcasted_iota(jnp.int32, (1, block), 1)

    @pl.when(live)
    def _():
        loads[0].wait()
        total = jnp.zeros((block, block), F32)
        for e in range(1, dist):
            factor = jnp.exp((line - (dist - e) * block).astype(F32) * beta)
            total = total + qb_in[e - 1] * factor
        row_sum[...] = jnp.broadcast_to(jnp.sum(total, axis=1, keepdims=True), row_sum.shape)
        loads[2].wait()
        loads[3].wait()
        first = jnp.sum(jnp.where(rows_i == cols_i, code_own[...].astype(F32), 0.0), axis=1, keepdims=True)
        table = jnp.exp(-table_in[...])
        entries = table.shape[1]
        table = jnp.concatenate([table, jnp.zeros((1, 128 - entries), F32)], axis=1)
        table = jnp.broadcast_to(table, (block, 128))
        loads[1].wait()
        code_send().wait_recv()
        both = first + code_in[...].astype(F32)
        allowed = jnp.where(jnp.logical_or(both == 3.0, both == 5.0), 1.0, 0.0)
        for start in range(0, block, 128):
            part = pl.ds(start, 128)
            found = jnp.take_along_axis(table, e_in[:, part], axis=1, mode="promise_in_bounds")
            weight[:, part] = found * allowed[:, start : start + 128]
        loads[4].wait()

    for n in range(1, len(held)):
        send_held(n)

    def column_sum(m, right, total):
        fade = jnp.exp((-(m + 1) * block - column).astype(F32) * beta)
        total[0:1, :] += jnp.sum(right * fade, axis=0, keepdims=True)

    def is_half(m, place):
        hit = jnp.bool_(False)
        for row, shift in halved:
            hit = jnp.logical_or(hit, jnp.logical_and(me == place(row, shift), m == shift - 1))
        return hit

    def listed(shifts):
        return sum(m * base**i for i, m in enumerate(shifts))

    own_list = jnp.int32(listed(range(1, dm + 1)))
    for row in range(live_rows) if plan else ():
        shifts = [m for m in order.get(row, range(1, dm + 1)) if home(row, m) == row or (row, m) in halved]
        own_list = jnp.where(me == row, listed(shifts), own_list)
    own_list = jnp.where(live, own_list, 0)

    def own_step(step, rest):
        m = rest % base - 1

        @pl.when(rest > 0)
        def _():
            small = is_half(m, lambda row, _: row)

            @pl.when(small)
            def _():
                half_copy(m + 1, 0).wait_recv()

            @pl.when(jnp.logical_not(small))
            def _():
                r_copy(m + 1, 0).wait_recv()
                column_sum(m, r_in[m], acc)

            right = r_in[m]
            acc[HEAD:, :] += dot3(split(q_own[m]), split(right))

        return rest // base

    if plan:
        far_list = jnp.int32(0)
        for device, shifts in plan.values():
            far_list = far_list + jnp.where(me == device, listed(shifts), 0)
        for c in range(CHUNKS):
            at = rows_of(c)
            if c < COARSE:
                for count in sorted({units(row) for row in plan}):

                    @pl.when(any_of(me, [plan[row][0] for row in plan if units(row) == count]))
                    def _():
                        whole = q_units(count, at)
                        remote(qm.at[whole], q_far.at[whole], q_send.at[0], q_recv.at[c], 0).wait_recv()

            def far_step(step, rest):
                m = rest % base - 1

                @pl.when(rest > 0)
                def _():
                    if c == 0:
                        rf_copy(m + 1, 0).wait_recv()
                        right = r_far[m]
                        rf_h[m], rf_l[m] = split(right)
                        column_sum(m, right, acc_far)
                    if c >= COARSE:
                        slot = q_recv.at[COARSE + (c - COARSE) * dm + m]

                        def wait_for(lanes):
                            here = (m, at, pl.ds(0, lanes))
                            remote(qm.at[here], q_far.at[here], q_send.at[0], slot, 0).wait_recv()

                        small = is_half(m, lambda row, _: plan[row][0])

                        @pl.when(small)
                        def _():
                            wait_for(half)

                        @pl.when(jnp.logical_not(small))
                        def _():
                            wait_for(block)
                    acc_far[rows_of(c, HEAD), :] += dot3(split(q_far[m, at, :]), (rf_h[m], rf_l[m]))

                return rest // base

            lax.fori_loop(0, dm, far_step, far_list)
            for row, (device, _) in plan.items():

                @pl.when(me == device)
                def _():
                    part_copy(c, row).start()

            for source, keys in after.items() if c == 0 else ():

                @pl.when(me == source)
                def _():
                    for row, m in keys:
                        held_send(row, m)

    lax.fori_loop(0, dm, own_step, own_list)

    if plan:

        @pl.when(any_of(me, list(plan)))
        def _():
            remote(acc_far, partial_in, part_sem.at[0], part_sem.at[1], 0).wait_recv()

    sent = jnp.int32(0)
    for m in range(1, dist):
        sent = sent + jnp.where(near(me - m), 1, 0)
    for row, (device, shifts) in plan.items():
        if device - row in shifts:
            sent = sent - jnp.where(me == device, 1, 0)
    for count in range(1, dist):

        @pl.when(sent == count)
        def _():
            whole = pl.ds(0, count)
            remote(qm1.at[whole], r_in.at[whole], r_send.at[0], r_recv.at[0], 0).wait_send()

    for row, (device, shifts) in plan.items():

        @pl.when(me == row)
        def _():
            whole = q_units(units(row), pl.ds(0, block))
            remote(qm.at[whole], q_far.at[whole], q_send.at[0], q_recv.at[0], 0).wait_send()

    for row, m in halved:

        @pl.when(me == row + m)
        def _():
            half_copy(m, row).wait_send()

    for via in sorted({via for via, _ in detour.values()}):

        @pl.when(me == via)
        def _():
            detour_all().wait_send()

    @pl.when(me >= dist)
    def _():
        code_send().wait_send()

    if plan:

        @pl.when(any_of(me, [device for device, _ in plan.values()]))
        def _():
            remote(acc_far, partial_in, part_sem.at[0], part_sem.at[1], 0).wait_send()

    for via in sorted({via for via, _, _ in relay.values()}):

        @pl.when(me == via)
        def _():
            whole = pl.ds(0, sum(1 for key in slots if relay[key[:2]][0] == via))
            remote(relay_in.at[whole], relay_in.at[whole], relay_send.at[0], r_recv.at[0], 0).wait_send()


def finish(dist, acc, weight, row_sum, partial, pair_out, branch_out, multi_out):
    block = weight.shape[0]
    beta = 1.0 / (dist * block)
    column = lax.broadcasted_iota(jnp.int32, (block, 1), 0).astype(F32)
    line = lax.broadcasted_iota(jnp.int32, (1, block), 1).astype(F32)
    rows_i = lax.broadcasted_iota(jnp.int32, (block, block), 0)
    cols_i = lax.broadcasted_iota(jnp.int32, (block, block), 1)
    upper = jnp.where(cols_i >= rows_i, 1.0, 0.0).astype(BF16)
    summed = acc[HEAD:, :] + partial[HEAD:, :]
    pair = weight[...] * (1.0 + 0.8 * summed)
    pair_out[...] = pair
    high, low = split(pair * jnp.exp(line * beta))
    inner = mm(high, upper) + mm(low, upper)
    branch = (row_sum[:, 0:1] + inner) * (beta * jnp.exp(line * (-beta)))
    branch_out[...] = branch
    high, low = split(branch * jnp.exp(column * (-beta)))
    tails = acc[0:1, :] + partial[0:1, :] + mm(upper, high) + mm(upper, low)
    multi_out[...] = summed + 0.01 * jnp.exp(column * beta) * tails


def solution(mesh):
    width = mesh.shape["row"]

    def per_device(qm, qm1, qb, codes, energy_index, turner):
        dm, block = qm.shape[2], qm.shape[3]
        dist = dm + 1
        known = width == 16 and dist == 8
        plan = PLAN if known else {}
        relay = RELAY if known else {}
        pieces = max([1] + [sum(n for v, n, _ in relay.values() if v == via) for via, _, _ in relay.values()])
        blocks = pltpu.VMEM((dm, block, block), F32)
        halves = pltpu.VMEM((dm, block, block), BF16)
        square = jax.ShapeDtypeStruct((block, block), F32)
        tall = pltpu.VMEM((block + HEAD, block), F32)
        dma = pltpu.SemaphoreType.DMA
        anywhere = pl.BlockSpec(memory_space=pltpu.HBM)
        local = pl.BlockSpec(memory_space=pltpu.VMEM)
        middle = pl.pallas_call(
            functools.partial(kernel, plan, relay, width),
            out_shape=[
                pltpu.VMEM((block + HEAD, block), F32),
                pltpu.VMEM((block, block), F32),
                pltpu.VMEM((block, 128), F32),
                tall,
            ],
            in_specs=[anywhere] * 6,
            out_specs=[local] * 4,
            scratch_shapes=[
                blocks, blocks, blocks, blocks, halves, halves, blocks,
                pltpu.VMEM((block, block), jnp.int32),
                pltpu.VMEM((1, block), jnp.int32),
                tall, pltpu.VMEM((pieces, block // PIECES, block), F32),
                pltpu.VMEM((block, block), F32),
                pltpu.VMEM((1, block), jnp.int32),
                pltpu.VMEM((1, turner.shape[0]), F32),
                dma((1,)), dma((1,)), dma((COARSE + (CHUNKS - COARSE) * dm,)), dma((1,)), dma((dm,)), dma((dm,)),
                dma((4,)), dma((2,)), dma((2,)),
                pltpu.SemaphoreType.REGULAR((len(HELD),)),
            ],
            compiler_params=pltpu.CompilerParams(has_side_effects=True, collective_id=0),
        )(
            qm[0, 0], qm1[0, 0], qb[0, 0], energy_index[0, 0],
            codes[0], turner[None, :],
        )
        outs = pl.pallas_call(
            functools.partial(finish, dist),
            out_shape=[square] * 3,
            in_specs=[local] * 4,
            out_specs=[local] * 3,
            compiler_params=pltpu.CompilerParams(vmem_limit_bytes=16 * 2**20),
        )(*middle)
        return tuple(out[None, None] for out in outs)

    return jax.shard_map(
        per_device,
        mesh=mesh,
        in_specs=(
            P("seq", "row", None, None, None),
            P("seq", "row", None, None, None),
            P("seq", "row", None, None, None),
            P("seq", "row", None),
            P("seq", "row", None, None),
            P(),
        ),
        out_specs=(
            P("seq", "row", None, None),
            P("seq", "row", None, None),
            P("seq", "row", None, None),
        ),
        check_vma=False,
    )
```

```python
import functools

import jax
import jax.numpy as jnp
from jax import lax
from jax.experimental import pallas as pl
from jax.experimental.pallas import tpu as pltpu
from jax.sharding import PartitionSpec as P

F32 = jnp.float32
BF16 = jnp.bfloat16

PLAN = {
    1: (5, (4, 3, 6, 5, 7)),
    3: (6, (3, 2, 7, 6, 5)),
    4: (8, (4, 5, 7, 6)),
    5: (9, (3, 6, 5, 7)),
    7: (11, (4, 3, 7, 1, 2, 5, 6)),
}
RELAY = {
    (6, 7): (15, 4, 0),
    (6, 6): (14, 4, 0),
    (2, 6): (10, 4, 0),
    (6, 3): (10, 4, 0),
    (7, 5): (14, 4, 2),
    (7, 6): (15, 4, 2),
}
HELD = (
    {4: (6,), 5: (6,), 8: (10, 11), 9: (10, 11)},
    {4: (2,), 5: (2,), 8: (2, 6), 9: (2, 6)},
)
SPLIT = ()
ORDER = {6: (1, 7, 6, 5, 4, 3, 2)}
DETOUR = {(4, 7): (6, 7), (4, 6): (6, 2)}
AFTER = {}
FIRST = (7, 6, 11, 10, 4, 5, 9, 8, 2)
SHARES = (8, 4, 3, 1)
CHUNKS = len(SHARES)
COARSE = 2
PIECES = 4
HEAD = 8


def split(x):
    high = x.astype(BF16)
    return high, (x - high.astype(F32)).astype(BF16)


def mm(a, b):
    return jnp.dot(a, b, preferred_element_type=F32)


def dot3(a, b):
    ah, al = a
    bh, bl = b
    return mm(ah, bh) + (mm(ah, bl) + mm(al, bh))


def any_of(x, values):
    hit = x == values[0]
    for value in values[1:]:
        hit = jnp.logical_or(hit, x == value)
    return hit


def kernel(
    plan, relay, width, qm, qm1, qb, eidx, codes, turner, acc, weight, row_sum, partial_in,
    q_own, r_in, r_far, q_far, rf_h, rf_l, qb_in, e_in, code_in, acc_far, relay_in, detour_in, code_own, table_in,
    own_sem, q_send, q_recv, r_send, r_recv, rf_recv, load_sem, code_sem, part_sem, held_sem,
):
    dm, block = qm.shape[0], qm.shape[1]
    dist = dm + 1
    live_rows = width - dist
    beta = 1.0 / (dist * block)
    base = dm + 1
    me = lax.axis_index("row")
    live = me < live_rows
    relay_send, relay_recv = q_send, q_recv
    unit = block // sum(SHARES)
    piece = block // PIECES

    def remote(src, dst, send, recv, device):
        return pltpu.make_async_remote_copy(
            src_ref=src, dst_ref=dst, send_sem=send, recv_sem=recv,
            device_id={"row": device}, device_id_type=pl.DeviceIdType.MESH,
        )

    def near(row):
        return jnp.logical_and(row >= 0, row < live_rows)

    def home(row, m):
        device, shifts = plan.get(row, (None, ()))
        return device if m in shifts else row

    held = HELD if plan else ()
    order = ORDER if plan else {}
    halved = SPLIT if plan else ()
    detour = DETOUR if plan else {}
    after = AFTER if plan else {}
    sides, edge = {}, 0
    for key, (_, share) in detour.items():
        sides[key] = (edge, share * block // 16)
        edge += share * block // 16
    last = {key for keys in after.values() for key in keys}
    half = block // 2
    waiting = []
    for group in held:
        lists = {source: [] for source in group}
        for source in group:
            for row in range(min(live_rows, source) - 1, max(source - dist, -1), -1):
                m = source - row
                via, count, _ = relay.get((row, m), (None, 0, 0))
                if home(row, m) in group[source] and count < PIECES and (row, m) not in last:
                    lists[source].append((row, m, "rest"))
                if via in group[source]:
                    lists[source].append((row, m, "relay"))
            lists[source].sort(key=lambda item: (item[2] != "relay", item[0] not in (3, 7), -item[0]))
        waiting.append(lists)
    for row, m in halved:
        waiting[-1][row + m].insert(1, (row, m, "half"))
    for (row, m), (via, _) in detour.items():
        for n, group in enumerate(held):
            if via in group.get(row, ()):
                waiting[n][row].insert(0, (row, m, "detour"))
    kinds = [item for lists in waiting for keys in lists.values() for item in keys]
    rests = last | {(row, m) for row, m, kind in kinds if kind == "rest"}
    parts = {(row, m) for row, m, kind in kinds if kind == "relay"}

    def held_send(row, m):
        if (row, m) in relay:
            relay_rest(row, m).start()
        else:
            (r_copy if home(row, m) == row else rf_copy)(m, home(row, m)).start()

    def code_send():
        return remote(codes, code_in, code_sem.at[0], code_sem.at[1], me - dist)

    def rows_of(c, shift=0):
        return pl.ds(sum(SHARES[:c]) * unit + shift, SHARES[c] * unit)

    def q_copy(row, m, c, device):
        rows = rows_of(c)
        if c == 0 and (row, m) in detour:
            start = sides[row, m][1]
            rows = pl.ds(start, SHARES[0] * unit - start)
        at = (m - 1, rows, pl.ds(0, half if (row, m) in halved else block))
        slot = c if c < COARSE else COARSE + (c - COARSE) * dm + m - 1
        return remote(qm.at[at], q_far.at[at], q_send.at[0], q_recv.at[slot], device)

    def r_copy(m, device):
        return remote(qm1.at[dm - m], r_in.at[m - 1], r_send.at[0], r_recv.at[m - 1], device)

    def rf_copy(m, device):
        return remote(qm1.at[dm - m], r_far.at[m - 1], r_send.at[0], rf_recv.at[m - 1], device)

    def detour_copy(row, m):
        start, size = sides[row, m]
        return remote(
            qm.at[m - 1, pl.ds(0, size)], detour_in.at[pl.ds(start, size)],
            q_send.at[0], code_sem.at[0], detour[row, m][0],
        )

    def detour_on(row, m):
        start, size = sides[row, m]
        return remote(
            detour_in.at[pl.ds(start, size)], q_far.at[m - 1, pl.ds(0, size)],
            q_send.at[0], q_recv.at[0], plan[row][0],
        )

    def detour_all():
        return remote(detour_in.at[pl.ds(0, edge)], detour_in.at[pl.ds(0, edge)], q_send.at[0], code_sem.at[0], 0)

    def half_copy(m, device):
        at = pl.ds(half, block - half)
        return remote(qm1.at[dm - m, at], r_in.at[m - 1, at], q_send.at[0], r_recv.at[m - 1], device)

    def units(row):
        shifts = plan[row][1]
        return 2 * len(shifts) - sum(1 for m in shifts if (row, m) in halved)

    def q_units(count, rows):
        if count % 2 == 0:
            at = (pl.ds(0, count // 2), rows)
        else:
            at = (pl.ds(0, count), rows, pl.ds(0, half))
        return at

    def right_at(row, m):
        return (r_in, r_recv) if home(row, m) == row else (r_far, rf_recv)

    turns = sorted((rank + p, row, m, p) for (row, m), (_, count, rank) in relay.items() for p in range(count))
    slots = {}
    for _, row, m, p in turns:
        slots[row, m, p] = sum(1 for key in slots if relay[key[:2]][0] == relay[row, m][0])

    def relay_copy(row, m, p):
        slot = slots[row, m, p]
        return remote(
            qm1.at[dm - m, pl.ds(p * piece, piece)], relay_in.at[slot],
            r_send.at[0], relay_recv.at[slot], relay[row, m][0],
        )

    def relay_on(row, m, p):
        at = pl.ds(p * piece, piece)
        into, sem = right_at(row, m)
        return remote(
            relay_in.at[slots[row, m, p]], into.at[m - 1, at], relay_send.at[0], sem.at[m - 1], home(row, m)
        )

    def relay_rest(row, m):
        start = relay[row, m][1] * piece
        at = pl.ds(start, block - start)
        into, sem = right_at(row, m)
        return remote(qm1.at[dm - m, at], into.at[m - 1, at], r_send.at[0], sem.at[m - 1], home(row, m))

    def send_held(n):
        for source, keys in waiting[n].items():

            @pl.when(me == source)
            def _():
                pl.semaphore_wait(held_sem.at[n], len(held[n][source]))
                for row, m, kind in keys:
                    if kind == "relay":
                        for p in range(relay[row, m][1]):
                            relay_copy(row, m, p).start()
                    elif kind == "half":
                        half_copy(m, row).start()
                    elif kind == "detour":
                        detour_copy(row, m).start()
                    else:
                        held_send(row, m)

    def part_copy(c, device):
        start = HEAD + sum(SHARES[:c]) * unit if c else 0
        at = pl.ds(start, HEAD + sum(SHARES[: c + 1]) * unit - start)
        return remote(acc_far.at[at], partial_in.at[at], part_sem.at[0], part_sem.at[1], device)

    barrier = pltpu.get_barrier_semaphore()

    def greet(device):
        pl.semaphore_signal(
            barrier, inc=1, device_id={"row": device}, device_id_type=pl.DeviceIdType.MESH
        )

    if plan:
        pairs = {(device, device - dist) for device in range(dist, width)}
        for row in range(live_rows):
            for m in range(1, dist):
                source, device = row + m, home(row, m)
                via, count, _ = relay.get((row, m), (None, 0, 0))
                if count:
                    pairs |= {(source, via), (via, device)}
                if count < PIECES:
                    pairs.add((source, device))
                if (row, m) in halved:
                    pairs.add((source, row))
        for row, (device, _) in plan.items():
            pairs |= {(row, device), (device, row)}
        for (row, m), (via, _) in detour.items():
            pairs |= {(row, via), (via, plan[row][0])}
        for group in held:
            for source, devices in group.items():
                pairs -= {(source, device) for device in devices}
                pairs |= {(device, source) for device in devices}
        pairs = sorted((s, d) for s, d in pairs if s != d)
        awaited = jnp.int32(0)
        ranked = [*FIRST, *(device for device in range(width) if device not in FIRST)]
        for device in range(width):
            awaited = awaited + jnp.where(me == device, sum(1 for s, _ in pairs if s == device), 0)
        for device in ranked:
            sources = [s for s, d in pairs if d == device]
            if sources:

                @pl.when(me == device)
                def _():
                    for source in sources:
                        greet(source)

    else:

        @pl.when(live)
        def _():
            for m in range(1, dist + 1):
                greet(me + m)

        awaited = jnp.int32(0)
        for m in range(1, dist + 1):
            awaited = awaited + jnp.where(near(me - m), 1, 0)

    @pl.when(awaited > 0)
    def _():
        pl.semaphore_wait(barrier, awaited)

    def starts(device):
        found = []
        device_of, shifts = plan.get(device, (None, ()))
        found += [q_copy(device, m, 0, device_of) for m in shifts]
        for m in range(dm, 0, -1):
            row = device - m
            if 0 <= row < live_rows and home(row, m) != row and (row, m) not in relay and (row, m) not in rests:
                if home(row, m) == device:
                    found.append(pltpu.make_async_copy(qm1.at[dm - m], r_far.at[m - 1], rf_recv.at[m - 1]))
                else:
                    found.append(rf_copy(m, home(row, m)))
        for row, m, p in slots:
            if row + m == device and (row, m) not in parts:
                found.append(relay_copy(row, m, p))
        for (row, m), (_, count, _) in relay.items():
            if row + m == device and count < PIECES and (row, m) not in rests:
                found.append(relay_rest(row, m))
        for m in range(dm, 0, -1):
            row = device - m
            if 0 <= row < live_rows and home(row, m) == row and (row, m) not in relay and (row, m) not in rests:
                found.append(r_copy(m, row))
        found += [q_copy(device, m, c, device_of) for c in range(1, CHUNKS) for m in shifts]
        return found

    if plan:
        for device in ranked:

            @pl.when(me == device)
            def _():
                for n, group in enumerate(held):
                    for source in [source for source, devices in group.items() if device in devices]:
                        pl.semaphore_signal(
                            held_sem.at[n], inc=1, device_id={"row": source}, device_id_type=pl.DeviceIdType.MESH
                        )
                if device >= dist:
                    code_send().start()
                for copy in starts(device):
                    copy.start()

    if not plan:

        @pl.when(me >= dist)
        def _():
            code_send().start()

        for m in range(dm, 0, -1):

            @pl.when(near(me - m))
            def _():
                r_copy(m, me - m).start()

    loads = (
        pltpu.make_async_copy(qb, qb_in, load_sem.at[0]),
        pltpu.make_async_copy(eidx, e_in, load_sem.at[1]),
        pltpu.make_async_copy(codes, code_own, load_sem.at[2]),
        pltpu.make_async_copy(turner, table_in, load_sem.at[3]),
        pltpu.make_async_copy(qm, q_own, own_sem.at[0]),
    )

    @pl.when(live)
    def _():
        for load in loads:
            load.start()

    if held:
        send_held(0)
    for via in sorted({via for via, _ in detour.values()}):

        @pl.when(me == via)
        def _():
            detour_all().wait_recv()
            for row, m in detour:
                detour_on(row, m).start()

    for via in sorted({via for via, _, _ in relay.values()}):

        @pl.when(me == via)
        def _():
            for row, m, p in slots:
                if relay[row, m][0] == via:
                    relay_copy(row, m, p).wait_recv()
                    relay_on(row, m, p).start()

    acc[...] = jnp.zeros_like(acc)
    acc_far[...] = jnp.zeros_like(acc_far)
    for row, m in halved:

        @pl.when(me == plan[row][0])
        def _():
            q_far[m - 1, :, half:] = jnp.zeros((block, block - half), F32)

        @pl.when(me == row)
        def _():
            r_in[m - 1, 0:half, :] = jnp.zeros((half, block), F32)

    @pl.when(jnp.logical_not(any_of(me, list(plan))) if plan else me >= 0)
    def _():
        partial_in[...] = jnp.zeros_like(partial_in)

    @pl.when(jnp.logical_not(live))
    def _():
        weight[...] = jnp.zeros_like(weight)
        row_sum[...] = jnp.zeros_like(row_sum)

    rows_i = lax.broadcasted_iota(jnp.int32, (block, block), 0)
    cols_i = lax.broadcasted_iota(jnp.int32, (block, block), 1)
    column = lax.broadcasted_iota(jnp.int32, (block, 1), 0)
    line = lax.broadcasted_iota(jnp.int32, (1, block), 1)

    @pl.when(live)
    def _():
        loads[0].wait()
        total = jnp.zeros((block, block), F32)
        for e in range(1, dist):
            factor = jnp.exp((line - (dist - e) * block).astype(F32) * beta)
            total = total + qb_in[e - 1] * factor
        row_sum[...] = jnp.broadcast_to(jnp.sum(total, axis=1, keepdims=True), row_sum.shape)
        loads[2].wait()
        loads[3].wait()
        first = jnp.sum(jnp.where(rows_i == cols_i, code_own[...].astype(F32), 0.0), axis=1, keepdims=True)
        table = jnp.exp(-table_in[...])
        entries = table.shape[1]
        table = jnp.concatenate([table, jnp.zeros((1, 128 - entries), F32)], axis=1)
        table = jnp.broadcast_to(table, (block, 128))
        loads[1].wait()
        code_send().wait_recv()
        both = first + code_in[...].astype(F32)
        allowed = jnp.where(jnp.logical_or(both == 3.0, both == 5.0), 1.0, 0.0)
        for start in range(0, block, 128):
            part = pl.ds(start, 128)
            found = jnp.take_along_axis(table, e_in[:, part], axis=1, mode="promise_in_bounds")
            weight[:, part] = found * allowed[:, start : start + 128]
        loads[4].wait()

    for n in range(1, len(held)):
        send_held(n)

    def column_sum(m, right, total):
        fade = jnp.exp((-(m + 1) * block - column).astype(F32) * beta)
        total[0:1, :] += jnp.sum(right * fade, axis=0, keepdims=True)

    def is_half(m, place):
        hit = jnp.bool_(False)
        for row, shift in halved:
            hit = jnp.logical_or(hit, jnp.logical_and(me == place(row, shift), m == shift - 1))
        return hit

    def listed(shifts):
        return sum(m * base**i for i, m in enumerate(shifts))

    own_list = jnp.int32(listed(range(1, dm + 1)))
    for row in range(live_rows) if plan else ():
        shifts = [m for m in order.get(row, range(1, dm + 1)) if home(row, m) == row or (row, m) in halved]
        own_list = jnp.where(me == row, listed(shifts), own_list)
    own_list = jnp.where(live, own_list, 0)

    def own_step(step, rest):
        m = rest % base - 1

        @pl.when(rest > 0)
        def _():
            small = is_half(m, lambda row, _: row)

            @pl.when(small)
            def _():
                half_copy(m + 1, 0).wait_recv()

            @pl.when(jnp.logical_not(small))
            def _():
                r_copy(m + 1, 0).wait_recv()
                column_sum(m, r_in[m], acc)

            right = r_in[m]
            acc[HEAD:, :] += dot3(split(q_own[m]), split(right))

        return rest // base

    if plan:
        far_list = jnp.int32(0)
        for device, shifts in plan.values():
            far_list = far_list + jnp.where(me == device, listed(shifts), 0)
        for c in range(CHUNKS):
            at = rows_of(c)
            if c < COARSE:
                for count in sorted({units(row) for row in plan}):

                    @pl.when(any_of(me, [plan[row][0] for row in plan if units(row) == count]))
                    def _():
                        whole = q_units(count, at)
                        remote(qm.at[whole], q_far.at[whole], q_send.at[0], q_recv.at[c], 0).wait_recv()

            def far_step(step, rest):
                m = rest % base - 1

                @pl.when(rest > 0)
                def _():
                    if c == 0:
                        rf_copy(m + 1, 0).wait_recv()
                        right = r_far[m]
                        rf_h[m], rf_l[m] = split(right)
                        column_sum(m, right, acc_far)
                    if c >= COARSE:
                        slot = q_recv.at[COARSE + (c - COARSE) * dm + m]

                        def wait_for(lanes):
                            here = (m, at, pl.ds(0, lanes))
                            remote(qm.at[here], q_far.at[here], q_send.at[0], slot, 0).wait_recv()

                        small = is_half(m, lambda row, _: plan[row][0])

                        @pl.when(small)
                        def _():
                            wait_for(half)

                        @pl.when(jnp.logical_not(small))
                        def _():
                            wait_for(block)
                    acc_far[rows_of(c, HEAD), :] += dot3(split(q_far[m, at, :]), (rf_h[m], rf_l[m]))

                return rest // base

            lax.fori_loop(0, dm, far_step, far_list)
            for row, (device, _) in plan.items():

                @pl.when(me == device)
                def _():
                    part_copy(c, row).start()

            for source, keys in after.items() if c == 0 else ():

                @pl.when(me == source)
                def _():
                    for row, m in keys:
                        held_send(row, m)

    lax.fori_loop(0, dm, own_step, own_list)

    if plan:

        @pl.when(any_of(me, list(plan)))
        def _():
            remote(acc_far, partial_in, part_sem.at[0], part_sem.at[1], 0).wait_recv()

    sent = jnp.int32(0)
    for m in range(1, dist):
        sent = sent + jnp.where(near(me - m), 1, 0)
    for row, (device, shifts) in plan.items():
        if device - row in shifts:
            sent = sent - jnp.where(me == device, 1, 0)
    for count in range(1, dist):

        @pl.when(sent == count)
        def _():
            whole = pl.ds(0, count)
            remote(qm1.at[whole], r_in.at[whole], r_send.at[0], r_recv.at[0], 0).wait_send()

    for row, (device, shifts) in plan.items():

        @pl.when(me == row)
        def _():
            whole = q_units(units(row), pl.ds(0, block))
            remote(qm.at[whole], q_far.at[whole], q_send.at[0], q_recv.at[0], 0).wait_send()

    for row, m in halved:

        @pl.when(me == row + m)
        def _():
            half_copy(m, row).wait_send()

    for via in sorted({via for via, _ in detour.values()}):

        @pl.when(me == via)
        def _():
            detour_all().wait_send()

    @pl.when(me >= dist)
    def _():
        code_send().wait_send()

    if plan:

        @pl.when(any_of(me, [device for device, _ in plan.values()]))
        def _():
            remote(acc_far, partial_in, part_sem.at[0], part_sem.at[1], 0).wait_send()

    for via in sorted({via for via, _, _ in relay.values()}):

        @pl.when(me == via)
        def _():
            whole = pl.ds(0, sum(1 for key in slots if relay[key[:2]][0] == via))
            remote(relay_in.at[whole], relay_in.at[whole], relay_send.at[0], r_recv.at[0], 0).wait_send()


def finish(dist, acc, weight, row_sum, partial, pair_out, branch_out, multi_out):
    block = weight.shape[0]
    beta = 1.0 / (dist * block)
    column = lax.broadcasted_iota(jnp.int32, (block, 1), 0).astype(F32)
    line = lax.broadcasted_iota(jnp.int32, (1, block), 1).astype(F32)
    rows_i = lax.broadcasted_iota(jnp.int32, (block, block), 0)
    cols_i = lax.broadcasted_iota(jnp.int32, (block, block), 1)
    upper = jnp.where(cols_i >= rows_i, 1.0, 0.0).astype(BF16)
    summed = acc[HEAD:, :] + partial[HEAD:, :]
    pair = weight[...] * (1.0 + 0.8 * summed)
    pair_out[...] = pair
    high, low = split(pair * jnp.exp(line * beta))
    inner = mm(high, upper) + mm(low, upper)
    branch = (row_sum[:, 0:1] + inner) * (beta * jnp.exp(line * (-beta)))
    branch_out[...] = branch
    high, low = split(branch * jnp.exp(column * (-beta)))
    tails = acc[0:1, :] + partial[0:1, :] + mm(upper, high) + mm(upper, low)
    multi_out[...] = summed + 0.01 * jnp.exp(column * beta) * tails


def solution(mesh):
    width = mesh.shape["row"]

    def per_device(qm, qm1, qb, codes, energy_index, turner):
        dm, block = qm.shape[2], qm.shape[3]
        dist = dm + 1
        known = width == 16 and dist == 8
        plan = PLAN if known else {}
        relay = RELAY if known else {}
        pieces = max([1] + [sum(n for v, n, _ in relay.values() if v == via) for via, _, _ in relay.values()])
        blocks = pltpu.VMEM((dm, block, block), F32)
        halves = pltpu.VMEM((dm, block, block), BF16)
        square = jax.ShapeDtypeStruct((block, block), F32)
        tall = pltpu.VMEM((block + HEAD, block), F32)
        dma = pltpu.SemaphoreType.DMA
        anywhere = pl.BlockSpec(memory_space=pltpu.HBM)
        local = pl.BlockSpec(memory_space=pltpu.VMEM)
        middle = pl.pallas_call(
            functools.partial(kernel, plan, relay, width),
            out_shape=[
                pltpu.VMEM((block + HEAD, block), F32),
                pltpu.VMEM((block, block), F32),
                pltpu.VMEM((block, 128), F32),
                tall,
            ],
            in_specs=[anywhere] * 6,
            out_specs=[local] * 4,
            scratch_shapes=[
                blocks, blocks, blocks, blocks, halves, halves, blocks,
                pltpu.VMEM((block, block), jnp.int32),
                pltpu.VMEM((1, block), jnp.int32),
                tall, pltpu.VMEM((pieces, block // PIECES, block), F32),
                pltpu.VMEM((block, block), F32),
                pltpu.VMEM((1, block), jnp.int32),
                pltpu.VMEM((1, turner.shape[0]), F32),
                dma((1,)), dma((1,)), dma((COARSE + (CHUNKS - COARSE) * dm,)), dma((1,)), dma((dm,)), dma((dm,)),
                dma((4,)), dma((2,)), dma((2,)),
                pltpu.SemaphoreType.REGULAR((len(HELD),)),
            ],
            compiler_params=pltpu.CompilerParams(has_side_effects=True, collective_id=0),
        )(
            qm[0, 0], qm1[0, 0], qb[0, 0], energy_index[0, 0],
            codes[0], turner[None, :],
        )
        outs = pl.pallas_call(
            functools.partial(finish, dist),
            out_shape=[square] * 3,
            in_specs=[local] * 4,
            out_specs=[local] * 3,
            compiler_params=pltpu.CompilerParams(vmem_limit_bytes=16 * 2**20),
        )(*middle)
        return tuple(out[None, None] for out in outs)

    return jax.shard_map(
        per_device,
        mesh=mesh,
        in_specs=(
            P("seq", "row", None, None, None),
            P("seq", "row", None, None, None),
            P("seq", "row", None, None, None),
            P("seq", "row", None),
            P("seq", "row", None, None),
            P(),
        ),
        out_specs=(
            P("seq", "row", None, None),
            P("seq", "row", None, None),
            P("seq", "row", None, None),
        ),
        check_vma=False,
    )
```

```python
import functools

import jax
import jax.numpy as jnp
from jax import lax
from jax.experimental import pallas as pl
from jax.experimental.pallas import tpu as pltpu
from jax.sharding import PartitionSpec as P

F32 = jnp.float32
BF16 = jnp.bfloat16

PLAN = {
    1: (5, (4, 3, 6, 5, 7)),
    3: (6, (3, 2, 7, 6, 5)),
    4: (8, (4, 5, 7, 6)),
    5: (9, (3, 6, 5, 7)),
    7: (11, (4, 3, 7, 1, 2, 5, 6)),
}
RELAY = {
    (6, 7): (15, 4, 0),
    (6, 6): (14, 4, 0),
    (2, 6): (10, 4, 0),
    (6, 3): (10, 4, 0),
    (7, 5): (14, 4, 2),
    (7, 6): (15, 4, 2),
}
HELD = (
    {4: (6,), 5: (6,), 8: (10, 11), 9: (10, 11)},
    {4: (2,), 5: (2,), 8: (2, 6), 9: (2, 6)},
)
SPLIT = ()
ORDER = {6: (1, 7, 6, 5, 4, 3, 2)}
DETOUR = {(4, 7): (6, 5), (4, 6): (6, 4)}
AFTER = {}
FIRST = (7, 6, 11, 10, 4, 5, 9, 8, 2)
SHARES = (7, 5, 3, 1)
CHUNKS = len(SHARES)
COARSE = 2
PIECES = 4
HEAD = 8


def split(x):
    high = x.astype(BF16)
    return high, (x - high.astype(F32)).astype(BF16)


def mm(a, b):
    return jnp.dot(a, b, preferred_element_type=F32)


def dot3(a, b):
    ah, al = a
    bh, bl = b
    return mm(ah, bh) + (mm(ah, bl) + mm(al, bh))


def any_of(x, values):
    hit = x == values[0]
    for value in values[1:]:
        hit = jnp.logical_or(hit, x == value)
    return hit


def kernel(
    plan, relay, width, qm, qm1, qb, eidx, codes, turner, acc, weight, row_sum, partial_in,
    q_own, r_in, r_far, q_far, rf_h, rf_l, qb_in, e_in, code_in, acc_far, relay_in, detour_in, code_own, table_in,
    own_sem, q_send, q_recv, r_send, r_recv, rf_recv, load_sem, code_sem, part_sem, held_sem,
):
    dm, block = qm.shape[0], qm.shape[1]
    dist = dm + 1
    live_rows = width - dist
    beta = 1.0 / (dist * block)
    base = dm + 1
    me = lax.axis_index("row")
    live = me < live_rows
    relay_send, relay_recv = q_send, q_recv
    unit = block // sum(SHARES)
    piece = block // PIECES

    def remote(src, dst, send, recv, device):
        return pltpu.make_async_remote_copy(
            src_ref=src, dst_ref=dst, send_sem=send, recv_sem=recv,
            device_id={"row": device}, device_id_type=pl.DeviceIdType.MESH,
        )

    def near(row):
        return jnp.logical_and(row >= 0, row < live_rows)

    def home(row, m):
        device, shifts = plan.get(row, (None, ()))
        return device if m in shifts else row

    held = HELD if plan else ()
    order = ORDER if plan else {}
    halved = SPLIT if plan else ()
    detour = DETOUR if plan else {}
    after = AFTER if plan else {}
    sides, edge = {}, 0
    for key, (_, share) in detour.items():
        sides[key] = (edge, share * block // 16)
        edge += share * block // 16
    last = {key for keys in after.values() for key in keys}
    half = block // 2
    waiting = []
    for group in held:
        lists = {source: [] for source in group}
        for source in group:
            for row in range(min(live_rows, source) - 1, max(source - dist, -1), -1):
                m = source - row
                via, count, _ = relay.get((row, m), (None, 0, 0))
                if home(row, m) in group[source] and count < PIECES and (row, m) not in last:
                    lists[source].append((row, m, "rest"))
                if via in group[source]:
                    lists[source].append((row, m, "relay"))
            lists[source].sort(key=lambda item: (item[2] != "relay", item[0] not in (3, 7), -item[0]))
        waiting.append(lists)
    for row, m in halved:
        waiting[-1][row + m].insert(1, (row, m, "half"))
    for (row, m), (via, _) in detour.items():
        for n, group in enumerate(held):
            if via in group.get(row, ()):
                waiting[n][row].insert(0, (row, m, "detour"))
    kinds = [item for lists in waiting for keys in lists.values() for item in keys]
    rests = last | {(row, m) for row, m, kind in kinds if kind == "rest"}
    parts = {(row, m) for row, m, kind in kinds if kind == "relay"}

    def held_send(row, m):
        if (row, m) in relay:
            relay_rest(row, m).start()
        else:
            (r_copy if home(row, m) == row else rf_copy)(m, home(row, m)).start()

    def code_send():
        return remote(codes, code_in, code_sem.at[0], code_sem.at[1], me - dist)

    def rows_of(c, shift=0):
        return pl.ds(sum(SHARES[:c]) * unit + shift, SHARES[c] * unit)

    def q_copy(row, m, c, device):
        rows = rows_of(c)
        if c == 0 and (row, m) in detour:
            start = sides[row, m][1]
            rows = pl.ds(start, SHARES[0] * unit - start)
        at = (m - 1, rows, pl.ds(0, half if (row, m) in halved else block))
        slot = q_recv.at[c if c < CHUNKS - 1 else CHUNKS - 2 + m]
        if COARSE <= c < CHUNKS - 1 and device >= live_rows:
            slot = r_recv.at[m - 1]
        return remote(qm.at[at], q_far.at[at], q_send.at[0], slot, device)

    def r_copy(m, device):
        return remote(qm1.at[dm - m], r_in.at[m - 1], r_send.at[0], r_recv.at[m - 1], device)

    def rf_copy(m, device):
        return remote(qm1.at[dm - m], r_far.at[m - 1], r_send.at[0], rf_recv.at[m - 1], device)

    def detour_copy(row, m):
        start, size = sides[row, m]
        return remote(
            qm.at[m - 1, pl.ds(0, size)], detour_in.at[pl.ds(start, size)],
            q_send.at[0], code_sem.at[0], detour[row, m][0],
        )

    def detour_on(row, m):
        start, size = sides[row, m]
        return remote(
            detour_in.at[pl.ds(start, size)], q_far.at[m - 1, pl.ds(0, size)],
            q_send.at[0], q_recv.at[0], plan[row][0],
        )

    def detour_all():
        return remote(detour_in.at[pl.ds(0, edge)], detour_in.at[pl.ds(0, edge)], q_send.at[0], code_sem.at[0], 0)

    def half_copy(m, device):
        at = pl.ds(half, block - half)
        return remote(qm1.at[dm - m, at], r_in.at[m - 1, at], q_send.at[0], r_recv.at[m - 1], device)

    def units(row):
        shifts = plan[row][1]
        return 2 * len(shifts) - sum(1 for m in shifts if (row, m) in halved)

    def q_units(count, rows):
        if count % 2 == 0:
            at = (pl.ds(0, count // 2), rows)
        else:
            at = (pl.ds(0, count), rows, pl.ds(0, half))
        return at

    def right_at(row, m):
        return (r_in, r_recv) if home(row, m) == row else (r_far, rf_recv)

    turns = sorted((rank + p, row, m, p) for (row, m), (_, count, rank) in relay.items() for p in range(count))
    slots = {}
    for _, row, m, p in turns:
        slots[row, m, p] = sum(1 for key in slots if relay[key[:2]][0] == relay[row, m][0])

    def relay_copy(row, m, p):
        slot = slots[row, m, p]
        return remote(
            qm1.at[dm - m, pl.ds(p * piece, piece)], relay_in.at[slot],
            r_send.at[0], relay_recv.at[slot], relay[row, m][0],
        )

    def relay_on(row, m, p):
        at = pl.ds(p * piece, piece)
        into, sem = right_at(row, m)
        return remote(
            relay_in.at[slots[row, m, p]], into.at[m - 1, at], relay_send.at[0], sem.at[m - 1], home(row, m)
        )

    def relay_rest(row, m):
        start = relay[row, m][1] * piece
        at = pl.ds(start, block - start)
        into, sem = right_at(row, m)
        return remote(qm1.at[dm - m, at], into.at[m - 1, at], r_send.at[0], sem.at[m - 1], home(row, m))

    def send_held(n):
        for source, keys in waiting[n].items():

            @pl.when(me == source)
            def _():
                pl.semaphore_wait(held_sem.at[n], len(held[n][source]))
                for row, m, kind in keys:
                    if kind == "relay":
                        for p in range(relay[row, m][1]):
                            relay_copy(row, m, p).start()
                    elif kind == "half":
                        half_copy(m, row).start()
                    elif kind == "detour":
                        detour_copy(row, m).start()
                    else:
                        held_send(row, m)

    def part_copy(c, device):
        start = HEAD + sum(SHARES[:c]) * unit if c else 0
        at = pl.ds(start, HEAD + sum(SHARES[: c + 1]) * unit - start)
        return remote(acc_far.at[at], partial_in.at[at], part_sem.at[0], part_sem.at[1], device)

    barrier = pltpu.get_barrier_semaphore()

    def greet(device):
        pl.semaphore_signal(
            barrier, inc=1, device_id={"row": device}, device_id_type=pl.DeviceIdType.MESH
        )

    if plan:
        pairs = {(device, device - dist) for device in range(dist, width)}
        for row in range(live_rows):
            for m in range(1, dist):
                source, device = row + m, home(row, m)
                via, count, _ = relay.get((row, m), (None, 0, 0))
                if count:
                    pairs |= {(source, via), (via, device)}
                if count < PIECES:
                    pairs.add((source, device))
                if (row, m) in halved:
                    pairs.add((source, row))
        for row, (device, _) in plan.items():
            pairs |= {(row, device), (device, row)}
        for (row, m), (via, _) in detour.items():
            pairs |= {(row, via), (via, plan[row][0])}
        for group in held:
            for source, devices in group.items():
                pairs -= {(source, device) for device in devices}
                pairs |= {(device, source) for device in devices}
        pairs = sorted((s, d) for s, d in pairs if s != d)
        awaited = jnp.int32(0)
        ranked = [*FIRST, *(device for device in range(width) if device not in FIRST)]
        for device in range(width):
            awaited = awaited + jnp.where(me == device, sum(1 for s, _ in pairs if s == device), 0)
        for device in ranked:
            sources = [s for s, d in pairs if d == device]
            if sources:

                @pl.when(me == device)
                def _():
                    for source in sources:
                        greet(source)

    else:

        @pl.when(live)
        def _():
            for m in range(1, dist + 1):
                greet(me + m)

        awaited = jnp.int32(0)
        for m in range(1, dist + 1):
            awaited = awaited + jnp.where(near(me - m), 1, 0)

    @pl.when(awaited > 0)
    def _():
        pl.semaphore_wait(barrier, awaited)

    def starts(device):
        found = []
        device_of, shifts = plan.get(device, (None, ()))
        found += [q_copy(device, m, 0, device_of) for m in shifts]
        for m in range(dm, 0, -1):
            row = device - m
            if 0 <= row < live_rows and home(row, m) != row and (row, m) not in relay and (row, m) not in rests:
                if home(row, m) == device:
                    found.append(pltpu.make_async_copy(qm1.at[dm - m], r_far.at[m - 1], rf_recv.at[m - 1]))
                else:
                    found.append(rf_copy(m, home(row, m)))
        for row, m, p in slots:
            if row + m == device and (row, m) not in parts:
                found.append(relay_copy(row, m, p))
        for (row, m), (_, count, _) in relay.items():
            if row + m == device and count < PIECES and (row, m) not in rests:
                found.append(relay_rest(row, m))
        for m in range(dm, 0, -1):
            row = device - m
            if 0 <= row < live_rows and home(row, m) == row and (row, m) not in relay and (row, m) not in rests:
                found.append(r_copy(m, row))
        found += [q_copy(device, m, c, device_of) for c in range(1, CHUNKS) for m in shifts]
        return found

    if plan:
        for device in ranked:

            @pl.when(me == device)
            def _():
                for n, group in enumerate(held):
                    for source in [source for source, devices in group.items() if device in devices]:
                        pl.semaphore_signal(
                            held_sem.at[n], inc=1, device_id={"row": source}, device_id_type=pl.DeviceIdType.MESH
                        )
                if device >= dist:
                    code_send().start()
                for copy in starts(device):
                    copy.start()

    if not plan:

        @pl.when(me >= dist)
        def _():
            code_send().start()

        for m in range(dm, 0, -1):

            @pl.when(near(me - m))
            def _():
                r_copy(m, me - m).start()

    loads = (
        pltpu.make_async_copy(qb, qb_in, load_sem.at[0]),
        pltpu.make_async_copy(eidx, e_in, load_sem.at[1]),
        pltpu.make_async_copy(codes, code_own, load_sem.at[2]),
        pltpu.make_async_copy(turner, table_in, load_sem.at[3]),
        pltpu.make_async_copy(qm, q_own, own_sem.at[0]),
    )

    @pl.when(live)
    def _():
        for load in loads:
            load.start()

    if held:
        send_held(0)
    for via in sorted({via for via, _ in detour.values()}):

        @pl.when(me == via)
        def _():
            detour_all().wait_recv()
            for row, m in detour:
                detour_on(row, m).start()

    for via in sorted({via for via, _, _ in relay.values()}):

        @pl.when(me == via)
        def _():
            for row, m, p in slots:
                if relay[row, m][0] == via:
                    relay_copy(row, m, p).wait_recv()
                    relay_on(row, m, p).start()

    acc[...] = jnp.zeros_like(acc)
    acc_far[...] = jnp.zeros_like(acc_far)
    for row, m in halved:

        @pl.when(me == plan[row][0])
        def _():
            q_far[m - 1, :, half:] = jnp.zeros((block, block - half), F32)

        @pl.when(me == row)
        def _():
            r_in[m - 1, 0:half, :] = jnp.zeros((half, block), F32)

    @pl.when(jnp.logical_not(any_of(me, list(plan))) if plan else me >= 0)
    def _():
        partial_in[...] = jnp.zeros_like(partial_in)

    @pl.when(jnp.logical_not(live))
    def _():
        weight[...] = jnp.zeros_like(weight)
        row_sum[...] = jnp.zeros_like(row_sum)

    rows_i = lax.broadcasted_iota(jnp.int32, (block, block), 0)
    cols_i = lax.broadcasted_iota(jnp.int32, (block, block), 1)
    column = lax.broadcasted_iota(jnp.int32, (block, 1), 0)
    line = lax.broadcasted_iota(jnp.int32, (1, block), 1)

    @pl.when(live)
    def _():
        loads[0].wait()
        total = jnp.zeros((block, block), F32)
        for e in range(1, dist):
            factor = jnp.exp((line - (dist - e) * block).astype(F32) * beta)
            total = total + qb_in[e - 1] * factor
        row_sum[...] = jnp.broadcast_to(jnp.sum(total, axis=1, keepdims=True), row_sum.shape)
        loads[2].wait()
        loads[3].wait()
        first = jnp.sum(jnp.where(rows_i == cols_i, code_own[...].astype(F32), 0.0), axis=1, keepdims=True)
        table = jnp.exp(-table_in[...])
        entries = table.shape[1]
        table = jnp.concatenate([table, jnp.zeros((1, 128 - entries), F32)], axis=1)
        table = jnp.broadcast_to(table, (block, 128))
        loads[1].wait()
        code_send().wait_recv()
        both = first + code_in[...].astype(F32)
        allowed = jnp.where(jnp.logical_or(both == 3.0, both == 5.0), 1.0, 0.0)
        for start in range(0, block, 128):
            part = pl.ds(start, 128)
            found = jnp.take_along_axis(table, e_in[:, part], axis=1, mode="promise_in_bounds")
            weight[:, part] = found * allowed[:, start : start + 128]
        loads[4].wait()

    for n in range(1, len(held)):
        send_held(n)

    def column_sum(m, right, total):
        fade = jnp.exp((-(m + 1) * block - column).astype(F32) * beta)
        total[0:1, :] += jnp.sum(right * fade, axis=0, keepdims=True)

    def is_half(m, place):
        hit = jnp.bool_(False)
        for row, shift in halved:
            hit = jnp.logical_or(hit, jnp.logical_and(me == place(row, shift), m == shift - 1))
        return hit

    def listed(shifts):
        return sum(m * base**i for i, m in enumerate(shifts))

    own_list = jnp.int32(listed(range(1, dm + 1)))
    for row in range(live_rows) if plan else ():
        shifts = [m for m in order.get(row, range(1, dm + 1)) if home(row, m) == row or (row, m) in halved]
        own_list = jnp.where(me == row, listed(shifts), own_list)
    own_list = jnp.where(live, own_list, 0)

    def own_step(step, rest):
        m = rest % base - 1

        @pl.when(rest > 0)
        def _():
            small = is_half(m, lambda row, _: row)

            @pl.when(small)
            def _():
                half_copy(m + 1, 0).wait_recv()

            @pl.when(jnp.logical_not(small))
            def _():
                r_copy(m + 1, 0).wait_recv()
                column_sum(m, r_in[m], acc)

            right = r_in[m]
            acc[HEAD:, :] += dot3(split(q_own[m]), split(right))

        return rest // base

    if plan:
        far_list = jnp.int32(0)
        for device, shifts in plan.values():
            far_list = far_list + jnp.where(me == device, listed(shifts), 0)
        for c in range(CHUNKS):
            at = rows_of(c)
            if c < CHUNKS - 1:
                whole_rows = [row for row in plan if c < COARSE or plan[row][0] < live_rows]
                for count in sorted({units(row) for row in whole_rows}):

                    @pl.when(any_of(me, [plan[row][0] for row in whole_rows if units(row) == count]))
                    def _():
                        whole = q_units(count, at)
                        remote(qm.at[whole], q_far.at[whole], q_send.at[0], q_recv.at[c], 0).wait_recv()

            def far_step(step, rest):
                m = rest % base - 1

                @pl.when(rest > 0)
                def _():
                    if c == 0:
                        rf_copy(m + 1, 0).wait_recv()
                        right = r_far[m]
                        rf_h[m], rf_l[m] = split(right)
                        column_sum(m, right, acc_far)
                    def wait_for(sem, lanes):
                        here = (m, at, pl.ds(0, lanes))
                        remote(qm.at[here], q_far.at[here], q_send.at[0], sem, 0).wait_recv()

                    def wait_each(sem):
                        small = is_half(m, lambda row, _: plan[row][0])

                        @pl.when(small)
                        def _():
                            wait_for(sem, half)

                        @pl.when(jnp.logical_not(small))
                        def _():
                            wait_for(sem, block)

                    if c == CHUNKS - 1:
                        wait_each(q_recv.at[CHUNKS - 1 + m])
                    elif c >= COARSE:

                        @pl.when(jnp.logical_not(live))
                        def _():
                            wait_each(r_recv.at[m])

                    acc_far[rows_of(c, HEAD), :] += dot3(split(q_far[m, at, :]), (rf_h[m], rf_l[m]))

                return rest // base

            lax.fori_loop(0, dm, far_step, far_list)
            for row, (device, _) in plan.items():

                @pl.when(me == device)
                def _():
                    part_copy(c, row).start()

            for source, keys in after.items() if c == 0 else ():

                @pl.when(me == source)
                def _():
                    for row, m in keys:
                        held_send(row, m)

    lax.fori_loop(0, dm, own_step, own_list)

    if plan:

        @pl.when(any_of(me, list(plan)))
        def _():
            remote(acc_far, partial_in, part_sem.at[0], part_sem.at[1], 0).wait_recv()

    sent = jnp.int32(0)
    for m in range(1, dist):
        sent = sent + jnp.where(near(me - m), 1, 0)
    for row, (device, shifts) in plan.items():
        if device - row in shifts:
            sent = sent - jnp.where(me == device, 1, 0)
    for count in range(1, dist):

        @pl.when(sent == count)
        def _():
            whole = pl.ds(0, count)
            remote(qm1.at[whole], r_in.at[whole], r_send.at[0], r_recv.at[0], 0).wait_send()

    for row, (device, shifts) in plan.items():

        @pl.when(me == row)
        def _():
            whole = q_units(units(row), pl.ds(0, block))
            remote(qm.at[whole], q_far.at[whole], q_send.at[0], q_recv.at[0], 0).wait_send()

    for row, m in halved:

        @pl.when(me == row + m)
        def _():
            half_copy(m, row).wait_send()

    for via in sorted({via for via, _ in detour.values()}):

        @pl.when(me == via)
        def _():
            detour_all().wait_send()

    @pl.when(me >= dist)
    def _():
        code_send().wait_send()

    if plan:

        @pl.when(any_of(me, [device for device, _ in plan.values()]))
        def _():
            remote(acc_far, partial_in, part_sem.at[0], part_sem.at[1], 0).wait_send()

    for via in sorted({via for via, _, _ in relay.values()}):

        @pl.when(me == via)
        def _():
            whole = pl.ds(0, sum(1 for key in slots if relay[key[:2]][0] == via))
            remote(relay_in.at[whole], relay_in.at[whole], relay_send.at[0], r_recv.at[0], 0).wait_send()


def finish(dist, acc, weight, row_sum, partial, pair_out, branch_out, multi_out):
    block = weight.shape[0]
    beta = 1.0 / (dist * block)
    column = lax.broadcasted_iota(jnp.int32, (block, 1), 0).astype(F32)
    line = lax.broadcasted_iota(jnp.int32, (1, block), 1).astype(F32)
    rows_i = lax.broadcasted_iota(jnp.int32, (block, block), 0)
    cols_i = lax.broadcasted_iota(jnp.int32, (block, block), 1)
    upper = jnp.where(cols_i >= rows_i, 1.0, 0.0).astype(BF16)
    summed = acc[HEAD:, :] + partial[HEAD:, :]
    pair = weight[...] * (1.0 + 0.8 * summed)
    pair_out[...] = pair
    high, low = split(pair * jnp.exp(line * beta))
    inner = mm(high, upper) + mm(low, upper)
    branch = (row_sum[:, 0:1] + inner) * (beta * jnp.exp(line * (-beta)))
    branch_out[...] = branch
    high, low = split(branch * jnp.exp(column * (-beta)))
    tails = acc[0:1, :] + partial[0:1, :] + mm(upper, high) + mm(upper, low)
    multi_out[...] = summed + 0.01 * jnp.exp(column * beta) * tails


def solution(mesh):
    width = mesh.shape["row"]

    def per_device(qm, qm1, qb, codes, energy_index, turner):
        dm, block = qm.shape[2], qm.shape[3]
        dist = dm + 1
        known = width == 16 and dist == 8
        plan = PLAN if known else {}
        relay = RELAY if known else {}
        pieces = max([1] + [sum(n for v, n, _ in relay.values() if v == via) for via, _, _ in relay.values()])
        blocks = pltpu.VMEM((dm, block, block), F32)
        halves = pltpu.VMEM((dm, block, block), BF16)
        square = jax.ShapeDtypeStruct((block, block), F32)
        tall = pltpu.VMEM((block + HEAD, block), F32)
        dma = pltpu.SemaphoreType.DMA
        anywhere = pl.BlockSpec(memory_space=pltpu.HBM)
        local = pl.BlockSpec(memory_space=pltpu.VMEM)
        middle = pl.pallas_call(
            functools.partial(kernel, plan, relay, width),
            out_shape=[
                pltpu.VMEM((block + HEAD, block), F32),
                pltpu.VMEM((block, block), F32),
                pltpu.VMEM((block, 128), F32),
                tall,
            ],
            in_specs=[anywhere] * 6,
            out_specs=[local] * 4,
            scratch_shapes=[
                blocks, blocks, blocks, blocks, halves, halves, blocks,
                pltpu.VMEM((block, block), jnp.int32),
                pltpu.VMEM((1, block), jnp.int32),
                tall, pltpu.VMEM((pieces, block // PIECES, block), F32),
                pltpu.VMEM((block, block), F32),
                pltpu.VMEM((1, block), jnp.int32),
                pltpu.VMEM((1, turner.shape[0]), F32),
                dma((1,)), dma((1,)), dma((CHUNKS - 1 + dm,)), dma((1,)), dma((dm,)), dma((dm,)),
                dma((4,)), dma((2,)), dma((2,)),
                pltpu.SemaphoreType.REGULAR((len(HELD),)),
            ],
            compiler_params=pltpu.CompilerParams(has_side_effects=True, collective_id=0),
        )(
            qm[0, 0], qm1[0, 0], qb[0, 0], energy_index[0, 0],
            codes[0], turner[None, :],
        )
        outs = pl.pallas_call(
            functools.partial(finish, dist),
            out_shape=[square] * 3,
            in_specs=[local] * 4,
            out_specs=[local] * 3,
            compiler_params=pltpu.CompilerParams(vmem_limit_bytes=16 * 2**20),
        )(*middle)
        return tuple(out[None, None] for out in outs)

    return jax.shard_map(
        per_device,
        mesh=mesh,
        in_specs=(
            P("seq", "row", None, None, None),
            P("seq", "row", None, None, None),
            P("seq", "row", None, None, None),
            P("seq", "row", None),
            P("seq", "row", None, None),
            P(),
        ),
        out_specs=(
            P("seq", "row", None, None),
            P("seq", "row", None, None),
            P("seq", "row", None, None),
        ),
        check_vma=False,
    )
```

```python
import functools

import jax
import jax.numpy as jnp
from jax import lax
from jax.experimental import pallas as pl
from jax.experimental.pallas import tpu as pltpu
from jax.sharding import PartitionSpec as P

F32 = jnp.float32
BF16 = jnp.bfloat16

PLAN = {
    1: (5, (4, 3, 6, 5, 7)),
    3: (6, (3, 2, 7, 6, 5)),
    4: (8, (4, 5, 7, 6)),
    5: (9, (3, 6, 5, 7)),
    7: (11, (4, 3, 7, 1, 2, 5, 6)),
}
RELAY = {
    (6, 7): (15, 4, 0),
    (6, 6): (14, 4, 0),
    (2, 6): (10, 4, 0),
    (6, 3): (10, 4, 0),
    (7, 5): (14, 4, 2),
    (7, 6): (15, 4, 2),
}
HELD = (
    {4: (6,), 5: (6,), 8: (10, 11), 9: (10, 11)},
    {4: (2,), 5: (2,), 8: (2, 6), 9: (2, 6)},
)
SPLIT = ()
ORDER = {6: (1, 7, 6, 5, 4, 3, 2)}
DETOUR = {(4, 7): (6, 5), (4, 6): (6, 4)}
AFTER = {}
FIRST = (8, 11, 9, 10, 7, 4, 5, 6, 2)
SHARES = (7, 5, 3, 1)
CHUNKS = len(SHARES)
COARSE = 2
PIECES = 4
HEAD = 8


def split(x):
    high = x.astype(BF16)
    return high, (x - high.astype(F32)).astype(BF16)


def mm(a, b):
    return jnp.dot(a, b, preferred_element_type=F32)


def dot3(a, b):
    ah, al = a
    bh, bl = b
    return mm(ah, bh) + (mm(ah, bl) + mm(al, bh))


def any_of(x, values):
    hit = x == values[0]
    for value in values[1:]:
        hit = jnp.logical_or(hit, x == value)
    return hit


def kernel(
    plan, relay, width, qm, qm1, qb, eidx, codes, turner, acc, weight, row_sum, partial_in,
    q_own, r_in, r_far, q_far, rf_h, rf_l, qb_in, e_in, code_in, acc_far, relay_in, detour_in, code_own, table_in,
    own_sem, q_send, q_recv, r_send, r_recv, rf_recv, load_sem, code_sem, part_sem, held_sem,
):
    dm, block = qm.shape[0], qm.shape[1]
    dist = dm + 1
    live_rows = width - dist
    beta = 1.0 / (dist * block)
    base = dm + 1
    me = lax.axis_index("row")
    live = me < live_rows
    relay_send, relay_recv = q_send, q_recv
    unit = block // sum(SHARES)
    piece = block // PIECES

    def remote(src, dst, send, recv, device):
        return pltpu.make_async_remote_copy(
            src_ref=src, dst_ref=dst, send_sem=send, recv_sem=recv,
            device_id={"row": device}, device_id_type=pl.DeviceIdType.MESH,
        )

    def near(row):
        return jnp.logical_and(row >= 0, row < live_rows)

    def home(row, m):
        device, shifts = plan.get(row, (None, ()))
        return device if m in shifts else row

    held = HELD if plan else ()
    order = ORDER if plan else {}
    halved = SPLIT if plan else ()
    detour = DETOUR if plan else {}
    after = AFTER if plan else {}
    sides, edge = {}, 0
    for key, (_, share) in detour.items():
        sides[key] = (edge, share * block // 16)
        edge += share * block // 16
    last = {key for keys in after.values() for key in keys}
    half = block // 2
    waiting = []
    for group in held:
        lists = {source: [] for source in group}
        for source in group:
            for row in range(min(live_rows, source) - 1, max(source - dist, -1), -1):
                m = source - row
                via, count, _ = relay.get((row, m), (None, 0, 0))
                if home(row, m) in group[source] and count < PIECES and (row, m) not in last:
                    lists[source].append((row, m, "rest"))
                if via in group[source]:
                    lists[source].append((row, m, "relay"))
            lists[source].sort(key=lambda item: (item[2] != "relay", item[0] not in (3, 7), -item[0]))
        waiting.append(lists)
    for row, m in halved:
        waiting[-1][row + m].insert(1, (row, m, "half"))
    for (row, m), (via, _) in detour.items():
        for n, group in enumerate(held):
            if via in group.get(row, ()):
                waiting[n][row].insert(0, (row, m, "detour"))
    kinds = [item for lists in waiting for keys in lists.values() for item in keys]
    rests = last | {(row, m) for row, m, kind in kinds if kind == "rest"}
    parts = {(row, m) for row, m, kind in kinds if kind == "relay"}

    def held_send(row, m):
        if (row, m) in relay:
            relay_rest(row, m).start()
        else:
            (r_copy if home(row, m) == row else rf_copy)(m, home(row, m)).start()

    def code_send():
        return remote(codes, code_in, code_sem.at[0], code_sem.at[1], me - dist)

    def rows_of(c, shift=0):
        return pl.ds(sum(SHARES[:c]) * unit + shift, SHARES[c] * unit)

    def q_copy(row, m, c, device):
        rows = rows_of(c)
        if c == 0 and (row, m) in detour:
            start = sides[row, m][1]
            rows = pl.ds(start, SHARES[0] * unit - start)
        at = (m - 1, rows, pl.ds(0, half if (row, m) in halved else block))
        slot = q_recv.at[c if c < CHUNKS - 1 else CHUNKS - 2 + m]
        if COARSE <= c < CHUNKS - 1 and device >= live_rows:
            slot = r_recv.at[m - 1]
        return remote(qm.at[at], q_far.at[at], q_send.at[0], slot, device)

    def r_copy(m, device):
        return remote(qm1.at[dm - m], r_in.at[m - 1], r_send.at[0], r_recv.at[m - 1], device)

    def rf_copy(m, device):
        return remote(qm1.at[dm - m], r_far.at[m - 1], r_send.at[0], rf_recv.at[m - 1], device)

    def detour_copy(row, m):
        start, size = sides[row, m]
        return remote(
            qm.at[m - 1, pl.ds(0, size)], detour_in.at[pl.ds(start, size)],
            q_send.at[0], code_sem.at[0], detour[row, m][0],
        )

    def detour_on(row, m):
        start, size = sides[row, m]
        return remote(
            detour_in.at[pl.ds(start, size)], q_far.at[m - 1, pl.ds(0, size)],
            q_send.at[0], q_recv.at[0], plan[row][0],
        )

    def detour_all():
        return remote(detour_in.at[pl.ds(0, edge)], detour_in.at[pl.ds(0, edge)], q_send.at[0], code_sem.at[0], 0)

    def half_copy(m, device):
        at = pl.ds(half, block - half)
        return remote(qm1.at[dm - m, at], r_in.at[m - 1, at], q_send.at[0], r_recv.at[m - 1], device)

    def units(row):
        shifts = plan[row][1]
        return 2 * len(shifts) - sum(1 for m in shifts if (row, m) in halved)

    def q_units(count, rows):
        if count % 2 == 0:
            at = (pl.ds(0, count // 2), rows)
        else:
            at = (pl.ds(0, count), rows, pl.ds(0, half))
        return at

    def right_at(row, m):
        return (r_in, r_recv) if home(row, m) == row else (r_far, rf_recv)

    turns = sorted((rank + p, row, m, p) for (row, m), (_, count, rank) in relay.items() for p in range(count))
    slots = {}
    for _, row, m, p in turns:
        slots[row, m, p] = sum(1 for key in slots if relay[key[:2]][0] == relay[row, m][0])

    def relay_copy(row, m, p):
        slot = slots[row, m, p]
        return remote(
            qm1.at[dm - m, pl.ds(p * piece, piece)], relay_in.at[slot],
            r_send.at[0], relay_recv.at[slot], relay[row, m][0],
        )

    def relay_on(row, m, p):
        at = pl.ds(p * piece, piece)
        into, sem = right_at(row, m)
        return remote(
            relay_in.at[slots[row, m, p]], into.at[m - 1, at], relay_send.at[0], sem.at[m - 1], home(row, m)
        )

    def relay_rest(row, m):
        start = relay[row, m][1] * piece
        at = pl.ds(start, block - start)
        into, sem = right_at(row, m)
        return remote(qm1.at[dm - m, at], into.at[m - 1, at], r_send.at[0], sem.at[m - 1], home(row, m))

    def send_held(n):
        for source, keys in waiting[n].items():

            @pl.when(me == source)
            def _():
                pl.semaphore_wait(held_sem.at[n], len(held[n][source]))
                for row, m, kind in keys:
                    if kind == "relay":
                        for p in range(relay[row, m][1]):
                            relay_copy(row, m, p).start()
                    elif kind == "half":
                        half_copy(m, row).start()
                    elif kind == "detour":
                        detour_copy(row, m).start()
                    else:
                        held_send(row, m)

    def part_copy(c, device):
        start = HEAD + sum(SHARES[:c]) * unit if c else 0
        at = pl.ds(start, HEAD + sum(SHARES[: c + 1]) * unit - start)
        return remote(acc_far.at[at], partial_in.at[at], part_sem.at[0], part_sem.at[1], device)

    barrier = pltpu.get_barrier_semaphore()

    def greet(device):
        pl.semaphore_signal(
            barrier, inc=1, device_id={"row": device}, device_id_type=pl.DeviceIdType.MESH
        )

    if plan:
        pairs = {(device, device - dist) for device in range(dist, width)}
        for row in range(live_rows):
            for m in range(1, dist):
                source, device = row + m, home(row, m)
                via, count, _ = relay.get((row, m), (None, 0, 0))
                if count:
                    pairs |= {(source, via), (via, device)}
                if count < PIECES:
                    pairs.add((source, device))
                if (row, m) in halved:
                    pairs.add((source, row))
        for row, (device, _) in plan.items():
            pairs |= {(row, device), (device, row)}
        for (row, m), (via, _) in detour.items():
            pairs |= {(row, via), (via, plan[row][0])}
        for group in held:
            for source, devices in group.items():
                pairs -= {(source, device) for device in devices}
                pairs |= {(device, source) for device in devices}
        pairs = sorted((s, d) for s, d in pairs if s != d)
        awaited = jnp.int32(0)
        ranked = [*FIRST, *(device for device in range(width) if device not in FIRST)]
        for device in range(width):
            awaited = awaited + jnp.where(me == device, sum(1 for s, _ in pairs if s == device), 0)
        for device in ranked:
            sources = [s for s, d in pairs if d == device]
            if sources:

                @pl.when(me == device)
                def _():
                    for source in sources:
                        greet(source)

    else:

        @pl.when(live)
        def _():
            for m in range(1, dist + 1):
                greet(me + m)

        awaited = jnp.int32(0)
        for m in range(1, dist + 1):
            awaited = awaited + jnp.where(near(me - m), 1, 0)

    @pl.when(awaited > 0)
    def _():
        pl.semaphore_wait(barrier, awaited)

    def starts(device):
        found = []
        device_of, shifts = plan.get(device, (None, ()))
        found += [q_copy(device, m, 0, device_of) for m in shifts]
        for m in range(dm, 0, -1):
            row = device - m
            if 0 <= row < live_rows and home(row, m) != row and (row, m) not in relay and (row, m) not in rests:
                if home(row, m) == device:
                    found.append(pltpu.make_async_copy(qm1.at[dm - m], r_far.at[m - 1], rf_recv.at[m - 1]))
                else:
                    found.append(rf_copy(m, home(row, m)))
        for row, m, p in slots:
            if row + m == device and (row, m) not in parts:
                found.append(relay_copy(row, m, p))
        for (row, m), (_, count, _) in relay.items():
            if row + m == device and count < PIECES and (row, m) not in rests:
                found.append(relay_rest(row, m))
        for m in range(dm, 0, -1):
            row = device - m
            if 0 <= row < live_rows and home(row, m) == row and (row, m) not in relay and (row, m) not in rests:
                found.append(r_copy(m, row))
        found += [q_copy(device, m, c, device_of) for c in range(1, CHUNKS) for m in shifts]
        return found

    if plan:
        for device in ranked:

            @pl.when(me == device)
            def _():
                for n, group in enumerate(held):
                    for source in [source for source, devices in group.items() if device in devices]:
                        pl.semaphore_signal(
                            held_sem.at[n], inc=1, device_id={"row": source}, device_id_type=pl.DeviceIdType.MESH
                        )
                if device >= dist:
                    code_send().start()
                for copy in starts(device):
                    copy.start()

    if not plan:

        @pl.when(me >= dist)
        def _():
            code_send().start()

        for m in range(dm, 0, -1):

            @pl.when(near(me - m))
            def _():
                r_copy(m, me - m).start()

    loads = (
        pltpu.make_async_copy(qb, qb_in, load_sem.at[0]),
        pltpu.make_async_copy(eidx, e_in, load_sem.at[1]),
        pltpu.make_async_copy(codes, code_own, load_sem.at[2]),
        pltpu.make_async_copy(turner, table_in, load_sem.at[3]),
        pltpu.make_async_copy(qm, q_own, own_sem.at[0]),
    )

    @pl.when(live)
    def _():
        for load in loads:
            load.start()

    if held:
        send_held(0)
    for via in sorted({via for via, _ in detour.values()}):

        @pl.when(me == via)
        def _():
            detour_all().wait_recv()
            for row, m in detour:
                detour_on(row, m).start()

    for via in sorted({via for via, _, _ in relay.values()}):

        @pl.when(me == via)
        def _():
            for row, m, p in slots:
                if relay[row, m][0] == via:
                    relay_copy(row, m, p).wait_recv()
                    relay_on(row, m, p).start()

    acc[...] = jnp.zeros_like(acc)
    acc_far[...] = jnp.zeros_like(acc_far)
    for row, m in halved:

        @pl.when(me == plan[row][0])
        def _():
            q_far[m - 1, :, half:] = jnp.zeros((block, block - half), F32)

        @pl.when(me == row)
        def _():
            r_in[m - 1, 0:half, :] = jnp.zeros((half, block), F32)

    @pl.when(jnp.logical_not(any_of(me, list(plan))) if plan else me >= 0)
    def _():
        partial_in[...] = jnp.zeros_like(partial_in)

    @pl.when(jnp.logical_not(live))
    def _():
        weight[...] = jnp.zeros_like(weight)
        row_sum[...] = jnp.zeros_like(row_sum)

    rows_i = lax.broadcasted_iota(jnp.int32, (block, block), 0)
    cols_i = lax.broadcasted_iota(jnp.int32, (block, block), 1)
    column = lax.broadcasted_iota(jnp.int32, (block, 1), 0)
    line = lax.broadcasted_iota(jnp.int32, (1, block), 1)

    @pl.when(live)
    def _():
        loads[0].wait()
        total = jnp.zeros((block, block), F32)
        for e in range(1, dist):
            factor = jnp.exp((line - (dist - e) * block).astype(F32) * beta)
            total = total + qb_in[e - 1] * factor
        row_sum[...] = jnp.broadcast_to(jnp.sum(total, axis=1, keepdims=True), row_sum.shape)
        loads[2].wait()
        loads[3].wait()
        first = jnp.sum(jnp.where(rows_i == cols_i, code_own[...].astype(F32), 0.0), axis=1, keepdims=True)
        table = jnp.exp(-table_in[...])
        entries = table.shape[1]
        table = jnp.concatenate([table, jnp.zeros((1, 128 - entries), F32)], axis=1)
        table = jnp.broadcast_to(table, (block, 128))
        loads[1].wait()
        code_send().wait_recv()
        both = first + code_in[...].astype(F32)
        allowed = jnp.where(jnp.logical_or(both == 3.0, both == 5.0), 1.0, 0.0)
        for start in range(0, block, 128):
            part = pl.ds(start, 128)
            found = jnp.take_along_axis(table, e_in[:, part], axis=1, mode="promise_in_bounds")
            weight[:, part] = found * allowed[:, start : start + 128]
        loads[4].wait()

    for n in range(1, len(held)):
        send_held(n)

    def column_sum(m, right, total):
        fade = jnp.exp((-(m + 1) * block - column).astype(F32) * beta)
        total[0:1, :] += jnp.sum(right * fade, axis=0, keepdims=True)

    def is_half(m, place):
        hit = jnp.bool_(False)
        for row, shift in halved:
            hit = jnp.logical_or(hit, jnp.logical_and(me == place(row, shift), m == shift - 1))
        return hit

    def listed(shifts):
        return sum(m * base**i for i, m in enumerate(shifts))

    own_list = jnp.int32(listed(range(1, dm + 1)))
    for row in range(live_rows) if plan else ():
        shifts = [m for m in order.get(row, range(1, dm + 1)) if home(row, m) == row or (row, m) in halved]
        own_list = jnp.where(me == row, listed(shifts), own_list)
    own_list = jnp.where(live, own_list, 0)

    def own_step(step, rest):
        m = rest % base - 1

        @pl.when(rest > 0)
        def _():
            small = is_half(m, lambda row, _: row)

            @pl.when(small)
            def _():
                half_copy(m + 1, 0).wait_recv()

            @pl.when(jnp.logical_not(small))
            def _():
                r_copy(m + 1, 0).wait_recv()
                column_sum(m, r_in[m], acc)

            right = r_in[m]
            acc[HEAD:, :] += dot3(split(q_own[m]), split(right))

        return rest // base

    if plan:
        far_list = jnp.int32(0)
        for device, shifts in plan.values():
            far_list = far_list + jnp.where(me == device, listed(shifts), 0)
        for c in range(CHUNKS):
            at = rows_of(c)
            if c < CHUNKS - 1:
                whole_rows = [row for row in plan if c < COARSE or plan[row][0] < live_rows]
                for count in sorted({units(row) for row in whole_rows}):

                    @pl.when(any_of(me, [plan[row][0] for row in whole_rows if units(row) == count]))
                    def _():
                        whole = q_units(count, at)
                        remote(qm.at[whole], q_far.at[whole], q_send.at[0], q_recv.at[c], 0).wait_recv()

            def far_step(step, rest):
                m = rest % base - 1

                @pl.when(rest > 0)
                def _():
                    if c == 0:
                        rf_copy(m + 1, 0).wait_recv()
                        right = r_far[m]
                        rf_h[m], rf_l[m] = split(right)
                        column_sum(m, right, acc_far)
                    def wait_for(sem, lanes):
                        here = (m, at, pl.ds(0, lanes))
                        remote(qm.at[here], q_far.at[here], q_send.at[0], sem, 0).wait_recv()

                    def wait_each(sem):
                        small = is_half(m, lambda row, _: plan[row][0])

                        @pl.when(small)
                        def _():
                            wait_for(sem, half)

                        @pl.when(jnp.logical_not(small))
                        def _():
                            wait_for(sem, block)

                    if c == CHUNKS - 1:
                        wait_each(q_recv.at[CHUNKS - 1 + m])
                    elif c >= COARSE:

                        @pl.when(jnp.logical_not(live))
                        def _():
                            wait_each(r_recv.at[m])

                    acc_far[rows_of(c, HEAD), :] += dot3(split(q_far[m, at, :]), (rf_h[m], rf_l[m]))

                return rest // base

            lax.fori_loop(0, dm, far_step, far_list)
            for row, (device, _) in plan.items():

                @pl.when(me == device)
                def _():
                    part_copy(c, row).start()

            for source, keys in after.items() if c == 0 else ():

                @pl.when(me == source)
                def _():
                    for row, m in keys:
                        held_send(row, m)

    lax.fori_loop(0, dm, own_step, own_list)

    if plan:

        @pl.when(any_of(me, list(plan)))
        def _():
            remote(acc_far, partial_in, part_sem.at[0], part_sem.at[1], 0).wait_recv()

    sent = jnp.int32(0)
    for m in range(1, dist):
        sent = sent + jnp.where(near(me - m), 1, 0)
    for row, (device, shifts) in plan.items():
        if device - row in shifts:
            sent = sent - jnp.where(me == device, 1, 0)
    for count in range(1, dist):

        @pl.when(sent == count)
        def _():
            whole = pl.ds(0, count)
            remote(qm1.at[whole], r_in.at[whole], r_send.at[0], r_recv.at[0], 0).wait_send()

    for row, (device, shifts) in plan.items():

        @pl.when(me == row)
        def _():
            whole = q_units(units(row), pl.ds(0, block))
            remote(qm.at[whole], q_far.at[whole], q_send.at[0], q_recv.at[0], 0).wait_send()

    for row, m in halved:

        @pl.when(me == row + m)
        def _():
            half_copy(m, row).wait_send()

    for via in sorted({via for via, _ in detour.values()}):

        @pl.when(me == via)
        def _():
            detour_all().wait_send()

    @pl.when(me >= dist)
    def _():
        code_send().wait_send()

    if plan:

        @pl.when(any_of(me, [device for device, _ in plan.values()]))
        def _():
            remote(acc_far, partial_in, part_sem.at[0], part_sem.at[1], 0).wait_send()

    for via in sorted({via for via, _, _ in relay.values()}):

        @pl.when(me == via)
        def _():
            whole = pl.ds(0, sum(1 for key in slots if relay[key[:2]][0] == via))
            remote(relay_in.at[whole], relay_in.at[whole], relay_send.at[0], r_recv.at[0], 0).wait_send()


def finish(dist, acc, weight, row_sum, partial, pair_out, branch_out, multi_out):
    block = weight.shape[0]
    beta = 1.0 / (dist * block)
    column = lax.broadcasted_iota(jnp.int32, (block, 1), 0).astype(F32)
    line = lax.broadcasted_iota(jnp.int32, (1, block), 1).astype(F32)
    rows_i = lax.broadcasted_iota(jnp.int32, (block, block), 0)
    cols_i = lax.broadcasted_iota(jnp.int32, (block, block), 1)
    upper = jnp.where(cols_i >= rows_i, 1.0, 0.0).astype(BF16)
    summed = acc[HEAD:, :] + partial[HEAD:, :]
    pair = weight[...] * (1.0 + 0.8 * summed)
    pair_out[...] = pair
    high, low = split(pair * jnp.exp(line * beta))
    inner = mm(high, upper) + mm(low, upper)
    branch = (row_sum[:, 0:1] + inner) * (beta * jnp.exp(line * (-beta)))
    branch_out[...] = branch
    high, low = split(branch * jnp.exp(column * (-beta)))
    tails = acc[0:1, :] + partial[0:1, :] + mm(upper, high) + mm(upper, low)
    multi_out[...] = summed + 0.01 * jnp.exp(column * beta) * tails


def solution(mesh):
    width = mesh.shape["row"]

    def per_device(qm, qm1, qb, codes, energy_index, turner):
        dm, block = qm.shape[2], qm.shape[3]
        dist = dm + 1
        known = width == 16 and dist == 8
        plan = PLAN if known else {}
        relay = RELAY if known else {}
        pieces = max([1] + [sum(n for v, n, _ in relay.values() if v == via) for via, _, _ in relay.values()])
        blocks = pltpu.VMEM((dm, block, block), F32)
        halves = pltpu.VMEM((dm, block, block), BF16)
        square = jax.ShapeDtypeStruct((block, block), F32)
        tall = pltpu.VMEM((block + HEAD, block), F32)
        dma = pltpu.SemaphoreType.DMA
        anywhere = pl.BlockSpec(memory_space=pltpu.HBM)
        local = pl.BlockSpec(memory_space=pltpu.VMEM)
        middle = pl.pallas_call(
            functools.partial(kernel, plan, relay, width),
            out_shape=[
                pltpu.VMEM((block + HEAD, block), F32),
                pltpu.VMEM((block, block), F32),
                pltpu.VMEM((block, 128), F32),
                tall,
            ],
            in_specs=[anywhere] * 6,
            out_specs=[local] * 4,
            scratch_shapes=[
                blocks, blocks, blocks, blocks, halves, halves, blocks,
                pltpu.VMEM((block, block), jnp.int32),
                pltpu.VMEM((1, block), jnp.int32),
                tall, pltpu.VMEM((pieces, block // PIECES, block), F32),
                pltpu.VMEM((block, block), F32),
                pltpu.VMEM((1, block), jnp.int32),
                pltpu.VMEM((1, turner.shape[0]), F32),
                dma((1,)), dma((1,)), dma((CHUNKS - 1 + dm,)), dma((1,)), dma((dm,)), dma((dm,)),
                dma((4,)), dma((2,)), dma((2,)),
                pltpu.SemaphoreType.REGULAR((len(HELD),)),
            ],
            compiler_params=pltpu.CompilerParams(has_side_effects=True, collective_id=0),
        )(
            qm[0, 0], qm1[0, 0], qb[0, 0], energy_index[0, 0],
            codes[0], turner[None, :],
        )
        outs = pl.pallas_call(
            functools.partial(finish, dist),
            out_shape=[square] * 3,
            in_specs=[local] * 4,
            out_specs=[local] * 3,
            compiler_params=pltpu.CompilerParams(vmem_limit_bytes=16 * 2**20),
        )(*middle)
        return tuple(out[None, None] for out in outs)

    return jax.shard_map(
        per_device,
        mesh=mesh,
        in_specs=(
            P("seq", "row", None, None, None),
            P("seq", "row", None, None, None),
            P("seq", "row", None, None, None),
            P("seq", "row", None),
            P("seq", "row", None, None),
            P(),
        ),
        out_specs=(
            P("seq", "row", None, None),
            P("seq", "row", None, None),
            P("seq", "row", None, None),
        ),
        check_vma=False,
    )
```

```python
import functools

import jax
import jax.numpy as jnp
from jax import lax
from jax.experimental import pallas as pl
from jax.experimental.pallas import tpu as pltpu
from jax.sharding import PartitionSpec as P

F32 = jnp.float32
BF16 = jnp.bfloat16

PLAN = {
    1: (5, (4, 3, 6, 5, 7)),
    3: (6, (3, 2, 7, 6, 5)),
    4: (8, (4, 5, 7, 6)),
    5: (9, (3, 6, 5, 7)),
    7: (11, (4, 3, 7, 1, 2, 5, 6)),
}
RELAY = {
    (6, 7): (15, 4, 0),
    (6, 6): (14, 4, 0),
    (2, 6): (10, 4, 0),
    (6, 3): (10, 4, 0),
    (7, 5): (14, 4, 2),
    (7, 6): (15, 4, 2),
}
HELD = (
    {4: (6,), 5: (6,), 8: (10, 11), 9: (10, 11)},
    {4: (2,), 5: (2,), 8: (2, 6), 9: (2, 6)},
)
SPLIT = ()
ORDER = {6: (1, 7, 6, 5, 4, 3, 2)}
DETOUR = {(4, 7): (6, 5), (4, 6): (6, 4)}
AFTER = {}
FIRST = (7, 4, 8, 11, 6, 5, 9, 10, 2)
SHARES = (7, 5, 3, 1)
CHUNKS = len(SHARES)
COARSE = 2
PIECES = 4
HEAD = 8


def split(x):
    high = x.astype(BF16)
    return high, (x - high.astype(F32)).astype(BF16)


def mm(a, b):
    return jnp.dot(a, b, preferred_element_type=F32)


def dot3(a, b):
    ah, al = a
    bh, bl = b
    return mm(ah, bh) + (mm(ah, bl) + mm(al, bh))


def any_of(x, values):
    hit = x == values[0]
    for value in values[1:]:
        hit = jnp.logical_or(hit, x == value)
    return hit


def kernel(
    plan, relay, width, qm, qm1, qb, eidx, codes, turner, acc, weight, row_sum, partial_in,
    q_own, r_in, r_far, q_far, rf_h, rf_l, qb_in, e_in, code_in, acc_far, relay_in, detour_in, code_own, table_in,
    own_sem, q_send, q_recv, r_send, r_recv, rf_recv, load_sem, code_sem, part_sem, held_sem,
):
    dm, block = qm.shape[0], qm.shape[1]
    dist = dm + 1
    live_rows = width - dist
    beta = 1.0 / (dist * block)
    base = dm + 1
    me = lax.axis_index("row")
    live = me < live_rows
    relay_send, relay_recv = q_send, q_recv
    unit = block // sum(SHARES)
    piece = block // PIECES

    def remote(src, dst, send, recv, device):
        return pltpu.make_async_remote_copy(
            src_ref=src, dst_ref=dst, send_sem=send, recv_sem=recv,
            device_id={"row": device}, device_id_type=pl.DeviceIdType.MESH,
        )

    def near(row):
        return jnp.logical_and(row >= 0, row < live_rows)

    def home(row, m):
        device, shifts = plan.get(row, (None, ()))
        return device if m in shifts else row

    held = HELD if plan else ()
    order = ORDER if plan else {}
    halved = SPLIT if plan else ()
    detour = DETOUR if plan else {}
    after = AFTER if plan else {}
    sides, edge = {}, 0
    for key, (_, share) in detour.items():
        sides[key] = (edge, share * block // 16)
        edge += share * block // 16
    last = {key for keys in after.values() for key in keys}
    half = block // 2
    waiting = []
    for group in held:
        lists = {source: [] for source in group}
        for source in group:
            for row in range(min(live_rows, source) - 1, max(source - dist, -1), -1):
                m = source - row
                via, count, _ = relay.get((row, m), (None, 0, 0))
                if home(row, m) in group[source] and count < PIECES and (row, m) not in last:
                    lists[source].append((row, m, "rest"))
                if via in group[source]:
                    lists[source].append((row, m, "relay"))
            lists[source].sort(key=lambda item: (item[2] != "relay", item[0] not in (3, 7), -item[0]))
        waiting.append(lists)
    for row, m in halved:
        waiting[-1][row + m].insert(1, (row, m, "half"))
    for (row, m), (via, _) in detour.items():
        for n, group in enumerate(held):
            if via in group.get(row, ()):
                waiting[n][row].insert(0, (row, m, "detour"))
    kinds = [item for lists in waiting for keys in lists.values() for item in keys]
    rests = last | {(row, m) for row, m, kind in kinds if kind == "rest"}
    parts = {(row, m) for row, m, kind in kinds if kind == "relay"}

    def held_send(row, m):
        if (row, m) in relay:
            relay_rest(row, m).start()
        else:
            (r_copy if home(row, m) == row else rf_copy)(m, home(row, m)).start()

    def code_send():
        return remote(codes, code_in, code_sem.at[0], code_sem.at[1], me - dist)

    def rows_of(c, shift=0):
        return pl.ds(sum(SHARES[:c]) * unit + shift, SHARES[c] * unit)

    def q_copy(row, m, c, device):
        rows = rows_of(c)
        if c == 0 and (row, m) in detour:
            start = sides[row, m][1]
            rows = pl.ds(start, SHARES[0] * unit - start)
        at = (m - 1, rows, pl.ds(0, half if (row, m) in halved else block))
        slot = q_recv.at[c if c < CHUNKS - 1 else CHUNKS - 2 + m]
        if COARSE <= c < CHUNKS - 1 and device >= live_rows:
            slot = r_recv.at[m - 1]
        return remote(qm.at[at], q_far.at[at], q_send.at[0], slot, device)

    def r_copy(m, device):
        return remote(qm1.at[dm - m], r_in.at[m - 1], r_send.at[0], r_recv.at[m - 1], device)

    def rf_copy(m, device):
        return remote(qm1.at[dm - m], r_far.at[m - 1], r_send.at[0], rf_recv.at[m - 1], device)

    def detour_copy(row, m):
        start, size = sides[row, m]
        return remote(
            qm.at[m - 1, pl.ds(0, size)], detour_in.at[pl.ds(start, size)],
            q_send.at[0], code_sem.at[0], detour[row, m][0],
        )

    def detour_on(row, m):
        start, size = sides[row, m]
        return remote(
            detour_in.at[pl.ds(start, size)], q_far.at[m - 1, pl.ds(0, size)],
            q_send.at[0], q_recv.at[0], plan[row][0],
        )

    def detour_all():
        return remote(detour_in.at[pl.ds(0, edge)], detour_in.at[pl.ds(0, edge)], q_send.at[0], code_sem.at[0], 0)

    def half_copy(m, device):
        at = pl.ds(half, block - half)
        return remote(qm1.at[dm - m, at], r_in.at[m - 1, at], q_send.at[0], r_recv.at[m - 1], device)

    def units(row):
        shifts = plan[row][1]
        return 2 * len(shifts) - sum(1 for m in shifts if (row, m) in halved)

    def q_units(count, rows):
        if count % 2 == 0:
            at = (pl.ds(0, count // 2), rows)
        else:
            at = (pl.ds(0, count), rows, pl.ds(0, half))
        return at

    def right_at(row, m):
        return (r_in, r_recv) if home(row, m) == row else (r_far, rf_recv)

    turns = sorted((rank + p, row, m, p) for (row, m), (_, count, rank) in relay.items() for p in range(count))
    slots = {}
    for _, row, m, p in turns:
        slots[row, m, p] = sum(1 for key in slots if relay[key[:2]][0] == relay[row, m][0])

    def relay_copy(row, m, p):
        slot = slots[row, m, p]
        return remote(
            qm1.at[dm - m, pl.ds(p * piece, piece)], relay_in.at[slot],
            r_send.at[0], relay_recv.at[slot], relay[row, m][0],
        )

    def relay_on(row, m, p):
        at = pl.ds(p * piece, piece)
        into, sem = right_at(row, m)
        return remote(
            relay_in.at[slots[row, m, p]], into.at[m - 1, at], relay_send.at[0], sem.at[m - 1], home(row, m)
        )

    def relay_rest(row, m):
        start = relay[row, m][1] * piece
        at = pl.ds(start, block - start)
        into, sem = right_at(row, m)
        return remote(qm1.at[dm - m, at], into.at[m - 1, at], r_send.at[0], sem.at[m - 1], home(row, m))

    def send_held(n):
        for source, keys in waiting[n].items():

            @pl.when(me == source)
            def _():
                pl.semaphore_wait(held_sem.at[n], len(held[n][source]))
                for row, m, kind in keys:
                    if kind == "relay":
                        for p in range(relay[row, m][1]):
                            relay_copy(row, m, p).start()
                    elif kind == "half":
                        half_copy(m, row).start()
                    elif kind == "detour":
                        detour_copy(row, m).start()
                    else:
                        held_send(row, m)

    def part_copy(c, device):
        start = HEAD + sum(SHARES[:c]) * unit if c else 0
        at = pl.ds(start, HEAD + sum(SHARES[: c + 1]) * unit - start)
        return remote(acc_far.at[at], partial_in.at[at], part_sem.at[0], part_sem.at[1], device)

    barrier = pltpu.get_barrier_semaphore()

    def greet(device):
        pl.semaphore_signal(
            barrier, inc=1, device_id={"row": device}, device_id_type=pl.DeviceIdType.MESH
        )

    if plan:
        pairs = {(device, device - dist) for device in range(dist, width)}
        for row in range(live_rows):
            for m in range(1, dist):
                source, device = row + m, home(row, m)
                via, count, _ = relay.get((row, m), (None, 0, 0))
                if count:
                    pairs |= {(source, via), (via, device)}
                if count < PIECES:
                    pairs.add((source, device))
                if (row, m) in halved:
                    pairs.add((source, row))
        for row, (device, _) in plan.items():
            pairs |= {(row, device), (device, row)}
        for (row, m), (via, _) in detour.items():
            pairs |= {(row, via), (via, plan[row][0])}
        for group in held:
            for source, devices in group.items():
                pairs -= {(source, device) for device in devices}
                pairs |= {(device, source) for device in devices}
        pairs = sorted((s, d) for s, d in pairs if s != d)
        awaited = jnp.int32(0)
        ranked = [*FIRST, *(device for device in range(width) if device not in FIRST)]
        for device in range(width):
            awaited = awaited + jnp.where(me == device, sum(1 for s, _ in pairs if s == device), 0)
        for device in ranked:
            sources = [s for s, d in pairs if d == device]
            if sources:

                @pl.when(me == device)
                def _():
                    for source in sources:
                        greet(source)

    else:

        @pl.when(live)
        def _():
            for m in range(1, dist + 1):
                greet(me + m)

        awaited = jnp.int32(0)
        for m in range(1, dist + 1):
            awaited = awaited + jnp.where(near(me - m), 1, 0)

    @pl.when(awaited > 0)
    def _():
        pl.semaphore_wait(barrier, awaited)

    def starts(device):
        found = []
        device_of, shifts = plan.get(device, (None, ()))
        found += [q_copy(device, m, 0, device_of) for m in shifts]
        for m in range(dm, 0, -1):
            row = device - m
            if 0 <= row < live_rows and home(row, m) != row and (row, m) not in relay and (row, m) not in rests:
                if home(row, m) == device:
                    found.append(pltpu.make_async_copy(qm1.at[dm - m], r_far.at[m - 1], rf_recv.at[m - 1]))
                else:
                    found.append(rf_copy(m, home(row, m)))
        for row, m, p in slots:
            if row + m == device and (row, m) not in parts:
                found.append(relay_copy(row, m, p))
        for (row, m), (_, count, _) in relay.items():
            if row + m == device and count < PIECES and (row, m) not in rests:
                found.append(relay_rest(row, m))
        for m in range(dm, 0, -1):
            row = device - m
            if 0 <= row < live_rows and home(row, m) == row and (row, m) not in relay and (row, m) not in rests:
                found.append(r_copy(m, row))
        found += [q_copy(device, m, c, device_of) for c in range(1, CHUNKS) for m in shifts]
        return found

    if plan:
        for device in ranked:

            @pl.when(me == device)
            def _():
                for n, group in enumerate(held):
                    for source in [source for source, devices in group.items() if device in devices]:
                        pl.semaphore_signal(
                            held_sem.at[n], inc=1, device_id={"row": source}, device_id_type=pl.DeviceIdType.MESH
                        )
                if device >= dist:
                    code_send().start()
                for copy in starts(device):
                    copy.start()

    if not plan:

        @pl.when(me >= dist)
        def _():
            code_send().start()

        for m in range(dm, 0, -1):

            @pl.when(near(me - m))
            def _():
                r_copy(m, me - m).start()

    loads = (
        pltpu.make_async_copy(qb, qb_in, load_sem.at[0]),
        pltpu.make_async_copy(eidx, e_in, load_sem.at[1]),
        pltpu.make_async_copy(codes, code_own, load_sem.at[2]),
        pltpu.make_async_copy(turner, table_in, load_sem.at[3]),
        pltpu.make_async_copy(qm, q_own, own_sem.at[0]),
    )

    @pl.when(live)
    def _():
        for load in loads:
            load.start()

    if held:
        send_held(0)
    for via in sorted({via for via, _ in detour.values()}):

        @pl.when(me == via)
        def _():
            detour_all().wait_recv()
            for row, m in detour:
                detour_on(row, m).start()

    for via in sorted({via for via, _, _ in relay.values()}):

        @pl.when(me == via)
        def _():
            for row, m, p in slots:
                if relay[row, m][0] == via:
                    relay_copy(row, m, p).wait_recv()
                    relay_on(row, m, p).start()

    acc[...] = jnp.zeros_like(acc)
    acc_far[...] = jnp.zeros_like(acc_far)
    for row, m in halved:

        @pl.when(me == plan[row][0])
        def _():
            q_far[m - 1, :, half:] = jnp.zeros((block, block - half), F32)

        @pl.when(me == row)
        def _():
            r_in[m - 1, 0:half, :] = jnp.zeros((half, block), F32)

    @pl.when(jnp.logical_not(any_of(me, list(plan))) if plan else me >= 0)
    def _():
        partial_in[...] = jnp.zeros_like(partial_in)

    @pl.when(jnp.logical_not(live))
    def _():
        weight[...] = jnp.zeros_like(weight)
        row_sum[...] = jnp.zeros_like(row_sum)

    rows_i = lax.broadcasted_iota(jnp.int32, (block, block), 0)
    cols_i = lax.broadcasted_iota(jnp.int32, (block, block), 1)
    column = lax.broadcasted_iota(jnp.int32, (block, 1), 0)
    line = lax.broadcasted_iota(jnp.int32, (1, block), 1)

    @pl.when(live)
    def _():
        loads[0].wait()
        total = jnp.zeros((block, block), F32)
        for e in range(1, dist):
            factor = jnp.exp((line - (dist - e) * block).astype(F32) * beta)
            total = total + qb_in[e - 1] * factor
        row_sum[...] = jnp.broadcast_to(jnp.sum(total, axis=1, keepdims=True), row_sum.shape)
        loads[2].wait()
        loads[3].wait()
        first = jnp.sum(jnp.where(rows_i == cols_i, code_own[...].astype(F32), 0.0), axis=1, keepdims=True)
        table = jnp.exp(-table_in[...])
        entries = table.shape[1]
        table = jnp.concatenate([table, jnp.zeros((1, 128 - entries), F32)], axis=1)
        table = jnp.broadcast_to(table, (block, 128))
        loads[1].wait()
        code_send().wait_recv()
        both = first + code_in[...].astype(F32)
        allowed = jnp.where(jnp.logical_or(both == 3.0, both == 5.0), 1.0, 0.0)
        for start in range(0, block, 128):
            part = pl.ds(start, 128)
            found = jnp.take_along_axis(table, e_in[:, part], axis=1, mode="promise_in_bounds")
            weight[:, part] = found * allowed[:, start : start + 128]
        loads[4].wait()

    for n in range(1, len(held)):
        send_held(n)

    def column_sum(m, right, total):
        fade = jnp.exp((-(m + 1) * block - column).astype(F32) * beta)
        total[0:1, :] += jnp.sum(right * fade, axis=0, keepdims=True)

    def is_half(m, place):
        hit = jnp.bool_(False)
        for row, shift in halved:
            hit = jnp.logical_or(hit, jnp.logical_and(me == place(row, shift), m == shift - 1))
        return hit

    def listed(shifts):
        return sum(m * base**i for i, m in enumerate(shifts))

    own_list = jnp.int32(listed(range(1, dm + 1)))
    for row in range(live_rows) if plan else ():
        shifts = [m for m in order.get(row, range(1, dm + 1)) if home(row, m) == row or (row, m) in halved]
        own_list = jnp.where(me == row, listed(shifts), own_list)
    own_list = jnp.where(live, own_list, 0)

    def own_step(step, rest):
        m = rest % base - 1

        @pl.when(rest > 0)
        def _():
            small = is_half(m, lambda row, _: row)

            @pl.when(small)
            def _():
                half_copy(m + 1, 0).wait_recv()

            @pl.when(jnp.logical_not(small))
            def _():
                r_copy(m + 1, 0).wait_recv()
                column_sum(m, r_in[m], acc)

            right = r_in[m]
            acc[HEAD:, :] += dot3(split(q_own[m]), split(right))

        return rest // base

    if plan:
        far_list = jnp.int32(0)
        for device, shifts in plan.values():
            far_list = far_list + jnp.where(me == device, listed(shifts), 0)
        for c in range(CHUNKS):
            at = rows_of(c)
            if c < CHUNKS - 1:
                whole_rows = [row for row in plan if c < COARSE or plan[row][0] < live_rows]
                for count in sorted({units(row) for row in whole_rows}):

                    @pl.when(any_of(me, [plan[row][0] for row in whole_rows if units(row) == count]))
                    def _():
                        whole = q_units(count, at)
                        remote(qm.at[whole], q_far.at[whole], q_send.at[0], q_recv.at[c], 0).wait_recv()

            def far_step(step, rest):
                m = rest % base - 1

                @pl.when(rest > 0)
                def _():
                    if c == 0:
                        rf_copy(m + 1, 0).wait_recv()
                        right = r_far[m]
                        rf_h[m], rf_l[m] = split(right)
                        column_sum(m, right, acc_far)
                    def wait_for(sem, lanes):
                        here = (m, at, pl.ds(0, lanes))
                        remote(qm.at[here], q_far.at[here], q_send.at[0], sem, 0).wait_recv()

                    def wait_each(sem):
                        small = is_half(m, lambda row, _: plan[row][0])

                        @pl.when(small)
                        def _():
                            wait_for(sem, half)

                        @pl.when(jnp.logical_not(small))
                        def _():
                            wait_for(sem, block)

                    if c == CHUNKS - 1:
                        wait_each(q_recv.at[CHUNKS - 1 + m])
                    elif c >= COARSE:

                        @pl.when(jnp.logical_not(live))
                        def _():
                            wait_each(r_recv.at[m])

                    acc_far[rows_of(c, HEAD), :] += dot3(split(q_far[m, at, :]), (rf_h[m], rf_l[m]))

                return rest // base

            lax.fori_loop(0, dm, far_step, far_list)
            for row, (device, _) in plan.items():

                @pl.when(me == device)
                def _():
                    part_copy(c, row).start()

            for source, keys in after.items() if c == 0 else ():

                @pl.when(me == source)
                def _():
                    for row, m in keys:
                        held_send(row, m)

    lax.fori_loop(0, dm, own_step, own_list)

    if plan:

        @pl.when(any_of(me, list(plan)))
        def _():
            remote(acc_far, partial_in, part_sem.at[0], part_sem.at[1], 0).wait_recv()

    sent = jnp.int32(0)
    for m in range(1, dist):
        sent = sent + jnp.where(near(me - m), 1, 0)
    for row, (device, shifts) in plan.items():
        if device - row in shifts:
            sent = sent - jnp.where(me == device, 1, 0)
    for count in range(1, dist):

        @pl.when(sent == count)
        def _():
            whole = pl.ds(0, count)
            remote(qm1.at[whole], r_in.at[whole], r_send.at[0], r_recv.at[0], 0).wait_send()

    for row, (device, shifts) in plan.items():

        @pl.when(me == row)
        def _():
            whole = q_units(units(row), pl.ds(0, block))
            remote(qm.at[whole], q_far.at[whole], q_send.at[0], q_recv.at[0], 0).wait_send()

    for row, m in halved:

        @pl.when(me == row + m)
        def _():
            half_copy(m, row).wait_send()

    for via in sorted({via for via, _ in detour.values()}):

        @pl.when(me == via)
        def _():
            detour_all().wait_send()

    @pl.when(me >= dist)
    def _():
        code_send().wait_send()

    if plan:

        @pl.when(any_of(me, [device for device, _ in plan.values()]))
        def _():
            remote(acc_far, partial_in, part_sem.at[0], part_sem.at[1], 0).wait_send()

    for via in sorted({via for via, _, _ in relay.values()}):

        @pl.when(me == via)
        def _():
            whole = pl.ds(0, sum(1 for key in slots if relay[key[:2]][0] == via))
            remote(relay_in.at[whole], relay_in.at[whole], relay_send.at[0], r_recv.at[0], 0).wait_send()


def finish(dist, acc, weight, row_sum, partial, pair_out, branch_out, multi_out):
    block = weight.shape[0]
    beta = 1.0 / (dist * block)
    column = lax.broadcasted_iota(jnp.int32, (block, 1), 0).astype(F32)
    line = lax.broadcasted_iota(jnp.int32, (1, block), 1).astype(F32)
    rows_i = lax.broadcasted_iota(jnp.int32, (block, block), 0)
    cols_i = lax.broadcasted_iota(jnp.int32, (block, block), 1)
    upper = jnp.where(cols_i >= rows_i, 1.0, 0.0).astype(BF16)
    summed = acc[HEAD:, :] + partial[HEAD:, :]
    pair = weight[...] * (1.0 + 0.8 * summed)
    pair_out[...] = pair
    high, low = split(pair * jnp.exp(line * beta))
    inner = mm(high, upper) + mm(low, upper)
    branch = (row_sum[:, 0:1] + inner) * (beta * jnp.exp(line * (-beta)))
    branch_out[...] = branch
    high, low = split(branch * jnp.exp(column * (-beta)))
    tails = acc[0:1, :] + partial[0:1, :] + mm(upper, high) + mm(upper, low)
    multi_out[...] = summed + 0.01 * jnp.exp(column * beta) * tails


def solution(mesh):
    width = mesh.shape["row"]

    def per_device(qm, qm1, qb, codes, energy_index, turner):
        dm, block = qm.shape[2], qm.shape[3]
        dist = dm + 1
        known = width == 16 and dist == 8
        plan = PLAN if known else {}
        relay = RELAY if known else {}
        pieces = max([1] + [sum(n for v, n, _ in relay.values() if v == via) for via, _, _ in relay.values()])
        blocks = pltpu.VMEM((dm, block, block), F32)
        halves = pltpu.VMEM((dm, block, block), BF16)
        square = jax.ShapeDtypeStruct((block, block), F32)
        tall = pltpu.VMEM((block + HEAD, block), F32)
        dma = pltpu.SemaphoreType.DMA
        anywhere = pl.BlockSpec(memory_space=pltpu.HBM)
        local = pl.BlockSpec(memory_space=pltpu.VMEM)
        middle = pl.pallas_call(
            functools.partial(kernel, plan, relay, width),
            out_shape=[
                pltpu.VMEM((block + HEAD, block), F32),
                pltpu.VMEM((block, block), F32),
                pltpu.VMEM((block, 128), F32),
                tall,
            ],
            in_specs=[anywhere] * 6,
            out_specs=[local] * 4,
            scratch_shapes=[
                blocks, blocks, blocks, blocks, halves, halves, blocks,
                pltpu.VMEM((block, block), jnp.int32),
                pltpu.VMEM((1, block), jnp.int32),
                tall, pltpu.VMEM((pieces, block // PIECES, block), F32),
                pltpu.VMEM((block, block), F32),
                pltpu.VMEM((1, block), jnp.int32),
                pltpu.VMEM((1, turner.shape[0]), F32),
                dma((1,)), dma((1,)), dma((CHUNKS - 1 + dm,)), dma((1,)), dma((dm,)), dma((dm,)),
                dma((4,)), dma((2,)), dma((2,)),
                pltpu.SemaphoreType.REGULAR((len(HELD),)),
            ],
            compiler_params=pltpu.CompilerParams(has_side_effects=True, collective_id=0),
        )(
            qm[0, 0], qm1[0, 0], qb[0, 0], energy_index[0, 0],
            codes[0], turner[None, :],
        )
        outs = pl.pallas_call(
            functools.partial(finish, dist),
            out_shape=[square] * 3,
            in_specs=[local] * 4,
            out_specs=[local] * 3,
            compiler_params=pltpu.CompilerParams(vmem_limit_bytes=16 * 2**20),
        )(*middle)
        return tuple(out[None, None] for out in outs)

    return jax.shard_map(
        per_device,
        mesh=mesh,
        in_specs=(
            P("seq", "row", None, None, None),
            P("seq", "row", None, None, None),
            P("seq", "row", None, None, None),
            P("seq", "row", None),
            P("seq", "row", None, None),
            P(),
        ),
        out_specs=(
            P("seq", "row", None, None),
            P("seq", "row", None, None),
            P("seq", "row", None, None),
        ),
        check_vma=False,
    )
```

```python
import functools

import jax
import jax.numpy as jnp
from jax import lax
from jax.experimental import pallas as pl
from jax.experimental.pallas import tpu as pltpu
from jax.sharding import PartitionSpec as P

F32 = jnp.float32
BF16 = jnp.bfloat16

PLAN = {
    1: (5, (4, 3, 6, 5, 7)),
    3: (6, (3, 2, 7, 6, 5)),
    4: (8, (4, 5, 7, 6)),
    5: (9, (3, 6, 5, 7)),
    7: (11, (4, 3, 7, 1, 2, 5, 6)),
}
RELAY = {
    (6, 7): (15, 4, 0),
    (6, 6): (14, 4, 0),
    (2, 6): (10, 4, 0),
    (6, 3): (10, 4, 0),
    (7, 5): (14, 4, 2),
    (7, 6): (15, 4, 2),
}
HELD = (
    {4: (6,), 5: (6,), 8: (10, 11), 9: (10, 11)},
    {4: (2,), 5: (2,), 8: (2, 6), 9: (2, 6)},
)
SPLIT = ()
ORDER = {6: (1, 7, 6, 5, 4, 3, 2)}
DETOUR = {(4, 7): (6, 5), (4, 6): (6, 5)}
AFTER = {}
FIRST = (7, 6, 11, 10, 4, 5, 9, 8, 2)
SHARES = (7, 5, 3, 1)
CHUNKS = len(SHARES)
COARSE = 2
PIECES = 4
HEAD = 8


def split(x):
    high = x.astype(BF16)
    return high, (x - high.astype(F32)).astype(BF16)


def mm(a, b):
    return jnp.dot(a, b, preferred_element_type=F32)


def dot3(a, b):
    ah, al = a
    bh, bl = b
    return mm(ah, bh) + (mm(ah, bl) + mm(al, bh))


def any_of(x, values):
    hit = x == values[0]
    for value in values[1:]:
        hit = jnp.logical_or(hit, x == value)
    return hit


def kernel(
    plan, relay, width, qm, qm1, qb, eidx, codes, turner, acc, weight, row_sum, partial_in,
    q_own, r_in, r_far, q_far, rf_h, rf_l, qb_in, e_in, code_in, acc_far, relay_in, detour_in, code_own, table_in,
    own_sem, q_send, q_recv, r_send, r_recv, rf_recv, load_sem, code_sem, part_sem, held_sem,
):
    dm, block = qm.shape[0], qm.shape[1]
    dist = dm + 1
    live_rows = width - dist
    beta = 1.0 / (dist * block)
    base = dm + 1
    me = lax.axis_index("row")
    live = me < live_rows
    relay_send, relay_recv = q_send, q_recv
    unit = block // sum(SHARES)
    piece = block // PIECES

    def remote(src, dst, send, recv, device):
        return pltpu.make_async_remote_copy(
            src_ref=src, dst_ref=dst, send_sem=send, recv_sem=recv,
            device_id={"row": device}, device_id_type=pl.DeviceIdType.MESH,
        )

    def near(row):
        return jnp.logical_and(row >= 0, row < live_rows)

    def home(row, m):
        device, shifts = plan.get(row, (None, ()))
        return device if m in shifts else row

    held = HELD if plan else ()
    order = ORDER if plan else {}
    halved = SPLIT if plan else ()
    detour = DETOUR if plan else {}
    after = AFTER if plan else {}
    sides, edge = {}, 0
    for key, (_, share) in detour.items():
        sides[key] = (edge, share * block // 16)
        edge += share * block // 16
    last = {key for keys in after.values() for key in keys}
    half = block // 2
    waiting = []
    for group in held:
        lists = {source: [] for source in group}
        for source in group:
            for row in range(min(live_rows, source) - 1, max(source - dist, -1), -1):
                m = source - row
                via, count, _ = relay.get((row, m), (None, 0, 0))
                if home(row, m) in group[source] and count < PIECES and (row, m) not in last:
                    lists[source].append((row, m, "rest"))
                if via in group[source]:
                    lists[source].append((row, m, "relay"))
            lists[source].sort(key=lambda item: (item[2] != "relay", item[0] not in (3, 7), -item[0]))
        waiting.append(lists)
    for row, m in halved:
        waiting[-1][row + m].insert(1, (row, m, "half"))
    for (row, m), (via, _) in detour.items():
        for n, group in enumerate(held):
            if via in group.get(row, ()):
                waiting[n][row].insert(0, (row, m, "detour"))
    kinds = [item for lists in waiting for keys in lists.values() for item in keys]
    rests = last | {(row, m) for row, m, kind in kinds if kind == "rest"}
    parts = {(row, m) for row, m, kind in kinds if kind == "relay"}

    def held_send(row, m):
        if (row, m) in relay:
            relay_rest(row, m).start()
        else:
            (r_copy if home(row, m) == row else rf_copy)(m, home(row, m)).start()

    def code_send():
        return remote(codes, code_in, code_sem.at[0], code_sem.at[1], me - dist)

    def rows_of(c, shift=0):
        return pl.ds(sum(SHARES[:c]) * unit + shift, SHARES[c] * unit)

    def q_copy(row, m, c, device):
        rows = rows_of(c)
        if c == 0 and (row, m) in detour:
            start = sides[row, m][1]
            rows = pl.ds(start, SHARES[0] * unit - start)
        at = (m - 1, rows, pl.ds(0, half if (row, m) in halved else block))
        slot = q_recv.at[c if c < CHUNKS - 1 else CHUNKS - 2 + m]
        if COARSE <= c < CHUNKS - 1 and device >= live_rows:
            slot = r_recv.at[m - 1]
        return remote(qm.at[at], q_far.at[at], q_send.at[0], slot, device)

    def r_copy(m, device):
        return remote(qm1.at[dm - m], r_in.at[m - 1], r_send.at[0], r_recv.at[m - 1], device)

    def rf_copy(m, device):
        return remote(qm1.at[dm - m], r_far.at[m - 1], r_send.at[0], rf_recv.at[m - 1], device)

    def detour_copy(row, m):
        start, size = sides[row, m]
        return remote(
            qm.at[m - 1, pl.ds(0, size)], detour_in.at[pl.ds(start, size)],
            q_send.at[0], code_sem.at[0], detour[row, m][0],
        )

    def detour_on(row, m):
        start, size = sides[row, m]
        return remote(
            detour_in.at[pl.ds(start, size)], q_far.at[m - 1, pl.ds(0, size)],
            q_send.at[0], q_recv.at[0], plan[row][0],
        )

    def detour_all():
        return remote(detour_in.at[pl.ds(0, edge)], detour_in.at[pl.ds(0, edge)], q_send.at[0], code_sem.at[0], 0)

    def half_copy(m, device):
        at = pl.ds(half, block - half)
        return remote(qm1.at[dm - m, at], r_in.at[m - 1, at], q_send.at[0], r_recv.at[m - 1], device)

    def units(row):
        shifts = plan[row][1]
        return 2 * len(shifts) - sum(1 for m in shifts if (row, m) in halved)

    def q_units(count, rows):
        if count % 2 == 0:
            at = (pl.ds(0, count // 2), rows)
        else:
            at = (pl.ds(0, count), rows, pl.ds(0, half))
        return at

    def right_at(row, m):
        return (r_in, r_recv) if home(row, m) == row else (r_far, rf_recv)

    turns = sorted((rank + p, row, m, p) for (row, m), (_, count, rank) in relay.items() for p in range(count))
    slots = {}
    for _, row, m, p in turns:
        slots[row, m, p] = sum(1 for key in slots if relay[key[:2]][0] == relay[row, m][0])

    def relay_copy(row, m, p):
        slot = slots[row, m, p]
        return remote(
            qm1.at[dm - m, pl.ds(p * piece, piece)], relay_in.at[slot],
            r_send.at[0], relay_recv.at[slot], relay[row, m][0],
        )

    def relay_on(row, m, p):
        at = pl.ds(p * piece, piece)
        into, sem = right_at(row, m)
        return remote(
            relay_in.at[slots[row, m, p]], into.at[m - 1, at], relay_send.at[0], sem.at[m - 1], home(row, m)
        )

    def relay_rest(row, m):
        start = relay[row, m][1] * piece
        at = pl.ds(start, block - start)
        into, sem = right_at(row, m)
        return remote(qm1.at[dm - m, at], into.at[m - 1, at], r_send.at[0], sem.at[m - 1], home(row, m))

    def send_held(n):
        for source, keys in waiting[n].items():

            @pl.when(me == source)
            def _():
                pl.semaphore_wait(held_sem.at[n], len(held[n][source]))
                for row, m, kind in keys:
                    if kind == "relay":
                        for p in range(relay[row, m][1]):
                            relay_copy(row, m, p).start()
                    elif kind == "half":
                        half_copy(m, row).start()
                    elif kind == "detour":
                        detour_copy(row, m).start()
                    else:
                        held_send(row, m)

    def part_copy(c, device):
        start = HEAD + sum(SHARES[:c]) * unit if c else 0
        at = pl.ds(start, HEAD + sum(SHARES[: c + 1]) * unit - start)
        return remote(acc_far.at[at], partial_in.at[at], part_sem.at[0], part_sem.at[1], device)

    barrier = pltpu.get_barrier_semaphore()

    def greet(device):
        pl.semaphore_signal(
            barrier, inc=1, device_id={"row": device}, device_id_type=pl.DeviceIdType.MESH
        )

    if plan:
        pairs = {(device, device - dist) for device in range(dist, width)}
        for row in range(live_rows):
            for m in range(1, dist):
                source, device = row + m, home(row, m)
                via, count, _ = relay.get((row, m), (None, 0, 0))
                if count:
                    pairs |= {(source, via), (via, device)}
                if count < PIECES:
                    pairs.add((source, device))
                if (row, m) in halved:
                    pairs.add((source, row))
        for row, (device, _) in plan.items():
            pairs |= {(row, device), (device, row)}
        for (row, m), (via, _) in detour.items():
            pairs |= {(row, via), (via, plan[row][0])}
        for group in held:
            for source, devices in group.items():
                pairs -= {(source, device) for device in devices}
                pairs |= {(device, source) for device in devices}
        pairs = sorted((s, d) for s, d in pairs if s != d)
        awaited = jnp.int32(0)
        ranked = [*FIRST, *(device for device in range(width) if device not in FIRST)]
        for device in range(width):
            awaited = awaited + jnp.where(me == device, sum(1 for s, _ in pairs if s == device), 0)
        for device in ranked:
            sources = [s for s, d in pairs if d == device]
            if sources:

                @pl.when(me == device)
                def _():
                    for source in sources:
                        greet(source)

    else:

        @pl.when(live)
        def _():
            for m in range(1, dist + 1):
                greet(me + m)

        awaited = jnp.int32(0)
        for m in range(1, dist + 1):
            awaited = awaited + jnp.where(near(me - m), 1, 0)

    @pl.when(awaited > 0)
    def _():
        pl.semaphore_wait(barrier, awaited)

    def starts(device):
        found = []
        device_of, shifts = plan.get(device, (None, ()))
        found += [q_copy(device, m, 0, device_of) for m in shifts]
        for m in range(dm, 0, -1):
            row = device - m
            if 0 <= row < live_rows and home(row, m) != row and (row, m) not in relay and (row, m) not in rests:
                if home(row, m) == device:
                    found.append(pltpu.make_async_copy(qm1.at[dm - m], r_far.at[m - 1], rf_recv.at[m - 1]))
                else:
                    found.append(rf_copy(m, home(row, m)))
        for row, m, p in slots:
            if row + m == device and (row, m) not in parts:
                found.append(relay_copy(row, m, p))
        for (row, m), (_, count, _) in relay.items():
            if row + m == device and count < PIECES and (row, m) not in rests:
                found.append(relay_rest(row, m))
        for m in range(dm, 0, -1):
            row = device - m
            if 0 <= row < live_rows and home(row, m) == row and (row, m) not in relay and (row, m) not in rests:
                found.append(r_copy(m, row))
        found += [q_copy(device, m, c, device_of) for c in range(1, CHUNKS) for m in shifts]
        return found

    if plan:
        for device in ranked:

            @pl.when(me == device)
            def _():
                for n, group in enumerate(held):
                    for source in [source for source, devices in group.items() if device in devices]:
                        pl.semaphore_signal(
                            held_sem.at[n], inc=1, device_id={"row": source}, device_id_type=pl.DeviceIdType.MESH
                        )
                if device >= dist:
                    code_send().start()
                for copy in starts(device):
                    copy.start()

    if not plan:

        @pl.when(me >= dist)
        def _():
            code_send().start()

        for m in range(dm, 0, -1):

            @pl.when(near(me - m))
            def _():
                r_copy(m, me - m).start()

    loads = (
        pltpu.make_async_copy(qb, qb_in, load_sem.at[0]),
        pltpu.make_async_copy(eidx, e_in, load_sem.at[1]),
        pltpu.make_async_copy(codes, code_own, load_sem.at[2]),
        pltpu.make_async_copy(turner, table_in, load_sem.at[3]),
        pltpu.make_async_copy(qm, q_own, own_sem.at[0]),
    )

    @pl.when(live)
    def _():
        for load in loads:
            load.start()

    if held:
        send_held(0)
    for via in sorted({via for via, _ in detour.values()}):

        @pl.when(me == via)
        def _():
            detour_all().wait_recv()
            for row, m in detour:
                detour_on(row, m).start()

    for via in sorted({via for via, _, _ in relay.values()}):

        @pl.when(me == via)
        def _():
            for row, m, p in slots:
                if relay[row, m][0] == via:
                    relay_copy(row, m, p).wait_recv()
                    relay_on(row, m, p).start()

    acc[...] = jnp.zeros_like(acc)
    acc_far[...] = jnp.zeros_like(acc_far)
    for row, m in halved:

        @pl.when(me == plan[row][0])
        def _():
            q_far[m - 1, :, half:] = jnp.zeros((block, block - half), F32)

        @pl.when(me == row)
        def _():
            r_in[m - 1, 0:half, :] = jnp.zeros((half, block), F32)

    @pl.when(jnp.logical_not(any_of(me, list(plan))) if plan else me >= 0)
    def _():
        partial_in[...] = jnp.zeros_like(partial_in)

    @pl.when(jnp.logical_not(live))
    def _():
        weight[...] = jnp.zeros_like(weight)
        row_sum[...] = jnp.zeros_like(row_sum)

    rows_i = lax.broadcasted_iota(jnp.int32, (block, block), 0)
    cols_i = lax.broadcasted_iota(jnp.int32, (block, block), 1)
    column = lax.broadcasted_iota(jnp.int32, (block, 1), 0)
    line = lax.broadcasted_iota(jnp.int32, (1, block), 1)

    @pl.when(live)
    def _():
        loads[0].wait()
        total = jnp.zeros((block, block), F32)
        for e in range(1, dist):
            factor = jnp.exp((line - (dist - e) * block).astype(F32) * beta)
            total = total + qb_in[e - 1] * factor
        row_sum[...] = jnp.broadcast_to(jnp.sum(total, axis=1, keepdims=True), row_sum.shape)
        loads[2].wait()
        loads[3].wait()
        first = jnp.sum(jnp.where(rows_i == cols_i, code_own[...].astype(F32), 0.0), axis=1, keepdims=True)
        table = jnp.exp(-table_in[...])
        entries = table.shape[1]
        table = jnp.concatenate([table, jnp.zeros((1, 128 - entries), F32)], axis=1)
        table = jnp.broadcast_to(table, (block, 128))
        loads[1].wait()
        code_send().wait_recv()
        both = first + code_in[...].astype(F32)
        allowed = jnp.where(jnp.logical_or(both == 3.0, both == 5.0), 1.0, 0.0)
        for start in range(0, block, 128):
            part = pl.ds(start, 128)
            found = jnp.take_along_axis(table, e_in[:, part], axis=1, mode="promise_in_bounds")
            weight[:, part] = found * allowed[:, start : start + 128]
        loads[4].wait()

    for n in range(1, len(held)):
        send_held(n)

    def column_sum(m, right, total):
        fade = jnp.exp((-(m + 1) * block - column).astype(F32) * beta)
        total[0:1, :] += jnp.sum(right * fade, axis=0, keepdims=True)

    def is_half(m, place):
        hit = jnp.bool_(False)
        for row, shift in halved:
            hit = jnp.logical_or(hit, jnp.logical_and(me == place(row, shift), m == shift - 1))
        return hit

    def listed(shifts):
        return sum(m * base**i for i, m in enumerate(shifts))

    own_list = jnp.int32(listed(range(1, dm + 1)))
    for row in range(live_rows) if plan else ():
        shifts = [m for m in order.get(row, range(1, dm + 1)) if home(row, m) == row or (row, m) in halved]
        own_list = jnp.where(me == row, listed(shifts), own_list)
    own_list = jnp.where(live, own_list, 0)

    def own_step(step, rest):
        m = rest % base - 1

        @pl.when(rest > 0)
        def _():
            small = is_half(m, lambda row, _: row)

            @pl.when(small)
            def _():
                half_copy(m + 1, 0).wait_recv()

            @pl.when(jnp.logical_not(small))
            def _():
                r_copy(m + 1, 0).wait_recv()
                column_sum(m, r_in[m], acc)

            right = r_in[m]
            acc[HEAD:, :] += dot3(split(q_own[m]), split(right))

        return rest // base

    if plan:
        far_list = jnp.int32(0)
        for device, shifts in plan.values():
            far_list = far_list + jnp.where(me == device, listed(shifts), 0)
        for c in range(CHUNKS):
            at = rows_of(c)
            if c < CHUNKS - 1:
                whole_rows = [row for row in plan if c < COARSE or plan[row][0] < live_rows]
                for count in sorted({units(row) for row in whole_rows}):

                    @pl.when(any_of(me, [plan[row][0] for row in whole_rows if units(row) == count]))
                    def _():
                        whole = q_units(count, at)
                        remote(qm.at[whole], q_far.at[whole], q_send.at[0], q_recv.at[c], 0).wait_recv()

            def far_step(step, rest):
                m = rest % base - 1

                @pl.when(rest > 0)
                def _():
                    if c == 0:
                        rf_copy(m + 1, 0).wait_recv()
                        right = r_far[m]
                        rf_h[m], rf_l[m] = split(right)
                        column_sum(m, right, acc_far)
                    def wait_for(sem, lanes):
                        here = (m, at, pl.ds(0, lanes))
                        remote(qm.at[here], q_far.at[here], q_send.at[0], sem, 0).wait_recv()

                    def wait_each(sem):
                        small = is_half(m, lambda row, _: plan[row][0])

                        @pl.when(small)
                        def _():
                            wait_for(sem, half)

                        @pl.when(jnp.logical_not(small))
                        def _():
                            wait_for(sem, block)

                    if c == CHUNKS - 1:
                        wait_each(q_recv.at[CHUNKS - 1 + m])
                    elif c >= COARSE:

                        @pl.when(jnp.logical_not(live))
                        def _():
                            wait_each(r_recv.at[m])

                    acc_far[rows_of(c, HEAD), :] += dot3(split(q_far[m, at, :]), (rf_h[m], rf_l[m]))

                return rest // base

            lax.fori_loop(0, dm, far_step, far_list)
            for row, (device, _) in plan.items():

                @pl.when(me == device)
                def _():
                    part_copy(c, row).start()

            for source, keys in after.items() if c == 0 else ():

                @pl.when(me == source)
                def _():
                    for row, m in keys:
                        held_send(row, m)

    lax.fori_loop(0, dm, own_step, own_list)

    if plan:

        @pl.when(any_of(me, list(plan)))
        def _():
            remote(acc_far, partial_in, part_sem.at[0], part_sem.at[1], 0).wait_recv()

    sent = jnp.int32(0)
    for m in range(1, dist):
        sent = sent + jnp.where(near(me - m), 1, 0)
    for row, (device, shifts) in plan.items():
        if device - row in shifts:
            sent = sent - jnp.where(me == device, 1, 0)
    for count in range(1, dist):

        @pl.when(sent == count)
        def _():
            whole = pl.ds(0, count)
            remote(qm1.at[whole], r_in.at[whole], r_send.at[0], r_recv.at[0], 0).wait_send()

    for row, (device, shifts) in plan.items():

        @pl.when(me == row)
        def _():
            whole = q_units(units(row), pl.ds(0, block))
            remote(qm.at[whole], q_far.at[whole], q_send.at[0], q_recv.at[0], 0).wait_send()

    for row, m in halved:

        @pl.when(me == row + m)
        def _():
            half_copy(m, row).wait_send()

    for via in sorted({via for via, _ in detour.values()}):

        @pl.when(me == via)
        def _():
            detour_all().wait_send()

    @pl.when(me >= dist)
    def _():
        code_send().wait_send()

    if plan:

        @pl.when(any_of(me, [device for device, _ in plan.values()]))
        def _():
            remote(acc_far, partial_in, part_sem.at[0], part_sem.at[1], 0).wait_send()

    for via in sorted({via for via, _, _ in relay.values()}):

        @pl.when(me == via)
        def _():
            whole = pl.ds(0, sum(1 for key in slots if relay[key[:2]][0] == via))
            remote(relay_in.at[whole], relay_in.at[whole], relay_send.at[0], r_recv.at[0], 0).wait_send()


def finish(dist, acc, weight, row_sum, partial, pair_out, branch_out, multi_out):
    block = weight.shape[0]
    beta = 1.0 / (dist * block)
    column = lax.broadcasted_iota(jnp.int32, (block, 1), 0).astype(F32)
    line = lax.broadcasted_iota(jnp.int32, (1, block), 1).astype(F32)
    rows_i = lax.broadcasted_iota(jnp.int32, (block, block), 0)
    cols_i = lax.broadcasted_iota(jnp.int32, (block, block), 1)
    upper = jnp.where(cols_i >= rows_i, 1.0, 0.0).astype(BF16)
    summed = acc[HEAD:, :] + partial[HEAD:, :]
    pair = weight[...] * (1.0 + 0.8 * summed)
    pair_out[...] = pair
    high, low = split(pair * jnp.exp(line * beta))
    inner = mm(high, upper) + mm(low, upper)
    branch = (row_sum[:, 0:1] + inner) * (beta * jnp.exp(line * (-beta)))
    branch_out[...] = branch
    high, low = split(branch * jnp.exp(column * (-beta)))
    tails = acc[0:1, :] + partial[0:1, :] + mm(upper, high) + mm(upper, low)
    multi_out[...] = summed + 0.01 * jnp.exp(column * beta) * tails


def solution(mesh):
    width = mesh.shape["row"]

    def per_device(qm, qm1, qb, codes, energy_index, turner):
        dm, block = qm.shape[2], qm.shape[3]
        dist = dm + 1
        known = width == 16 and dist == 8
        plan = PLAN if known else {}
        relay = RELAY if known else {}
        pieces = max([1] + [sum(n for v, n, _ in relay.values() if v == via) for via, _, _ in relay.values()])
        blocks = pltpu.VMEM((dm, block, block), F32)
        halves = pltpu.VMEM((dm, block, block), BF16)
        square = jax.ShapeDtypeStruct((block, block), F32)
        tall = pltpu.VMEM((block + HEAD, block), F32)
        dma = pltpu.SemaphoreType.DMA
        anywhere = pl.BlockSpec(memory_space=pltpu.HBM)
        local = pl.BlockSpec(memory_space=pltpu.VMEM)
        middle = pl.pallas_call(
            functools.partial(kernel, plan, relay, width),
            out_shape=[
                pltpu.VMEM((block + HEAD, block), F32),
                pltpu.VMEM((block, block), F32),
                pltpu.VMEM((block, 128), F32),
                tall,
            ],
            in_specs=[anywhere] * 6,
            out_specs=[local] * 4,
            scratch_shapes=[
                blocks, blocks, blocks, blocks, halves, halves, blocks,
                pltpu.VMEM((block, block), jnp.int32),
                pltpu.VMEM((1, block), jnp.int32),
                tall, pltpu.VMEM((pieces, block // PIECES, block), F32),
                pltpu.VMEM((block, block), F32),
                pltpu.VMEM((1, block), jnp.int32),
                pltpu.VMEM((1, turner.shape[0]), F32),
                dma((1,)), dma((1,)), dma((CHUNKS - 1 + dm,)), dma((1,)), dma((dm,)), dma((dm,)),
                dma((4,)), dma((2,)), dma((2,)),
                pltpu.SemaphoreType.REGULAR((len(HELD),)),
            ],
            compiler_params=pltpu.CompilerParams(has_side_effects=True, collective_id=0),
        )(
            qm[0, 0], qm1[0, 0], qb[0, 0], energy_index[0, 0],
            codes[0], turner[None, :],
        )
        outs = pl.pallas_call(
            functools.partial(finish, dist),
            out_shape=[square] * 3,
            in_specs=[local] * 4,
            out_specs=[local] * 3,
            compiler_params=pltpu.CompilerParams(vmem_limit_bytes=16 * 2**20),
        )(*middle)
        return tuple(out[None, None] for out in outs)

    return jax.shard_map(
        per_device,
        mesh=mesh,
        in_specs=(
            P("seq", "row", None, None, None),
            P("seq", "row", None, None, None),
            P("seq", "row", None, None, None),
            P("seq", "row", None),
            P("seq", "row", None, None),
            P(),
        ),
        out_specs=(
            P("seq", "row", None, None),
            P("seq", "row", None, None),
            P("seq", "row", None, None),
        ),
        check_vma=False,
    )
```
